32 devices in a mesh: grp: 4 (over z), shard: 8 (over y, x, core).
Axes of the slice: x: 2, y: 2, z: 4, core: 2. Of those that a mesh axis runs over, the one named last changes fastest.
Arguments:
- frames_in: float32 [128, 256, 768], P(('grp', 'shard')), may hold values from -6 to 6
- cotangent: float32 [128, 256, 768], P(('grp', 'shard')), may hold values from -6 to 6
- time_table: bfloat16 [1000, 768], P(None, 'shard'), may hold values from -6 to 6
- ada_weight: bfloat16 [768, 6912], P('shard'), may hold values from -0.21875 to 0.21875
- ada_bias: bfloat16 [6912], P('shard'), may hold values from -4 to 4
- space_qkv: bfloat16 [768, 2304], P('shard'), may hold values from -0.21875 to 0.21875
- space_out: bfloat16 [768, 768], P('shard'), may hold values from -2.5 to 2.5
- time_qkv: bfloat16 [768, 2304], P('shard'), may hold values from -0.21875 to 0.21875
- time_out: bfloat16 [768, 768], P('shard'), may hold values from -0.875 to 0.875
- up_weight: bfloat16 [768, 3072], P('shard'), may hold values from -0.21875 to 0.21875
- up_bias: bfloat16 [3072], P('shard'), may hold values from -6 to 6
- down_weight: bfloat16 [3072, 768], P('shard'), may hold values from -0.109375 to 0.109375
- down_bias: bfloat16 [768], P('shard'), may hold values from -4 to 4
- timesteps: int32 [8], P('grp'), may hold values from 0 to 999
- task_mask: int32 [8, 16], P('grp'), may hold values 0 or 1
- clip_weight: float32 [8], P('grp'), may hold values from 0.5 to 2
- frame_table: int32 [4, 32], P('grp'), may hold values from 0 to 31, each once within a row
Outputs:
- frames_out: float32 [128, 256, 768], P(('grp', 'shard'))
- grad_frames_in: float32 [128, 256, 768], P(('grp', 'shard'))
- grad_time_table: float32 [1000, 768], P(None, 'shard')
- grad_ada_weight: float32 [768, 6912], P('shard')
- grad_ada_bias: float32 [6912], P('shard')
- grad_space_qkv: float32 [768, 2304], P('shard')
- grad_space_out: float32 [768, 768], P('shard')
- grad_time_qkv: float32 [768, 2304], P('shard')
- grad_time_out: float32 [768, 768], P('shard')
- grad_up_weight: float32 [768, 3072], P('shard')
- grad_up_bias: float32 [3072], P('shard')
- grad_down_weight: float32 [3072, 768], P('shard')
- grad_down_bias: float32 [768], P('shard')
The draws below stay inside these ranges and needn't reach their ends.
Inputs may be any that keep to these rules, and one draw needn't show every extreme that they name: `frame_table`: each row lists every frame of its group once.
All inputs are finite; a program needn't handle non-finite values. No bound on the sum of `task_mask` on one device may be relied on, other than what follows from the above.
Results may differ from the reference program's by a relative error of at most 0.014.
Values may be sent and summed in bfloat16 or wider, within the bound.
No kernel may reach another device: no remote copies, remote signals or barrier semaphores. Data moves between devices by JAX's collectives and lax.ppermute only.
A program may use at most 256 MiB of HBM per device.

```python
import math
import jax
import jax.numpy as jnp
from jax import lax

D = 768
HEADS = 12
HEAD_DIM = 64
FF = 3072
TIME_IDS = 1000
FRAMES = 16
PATCHES = 256
CLIPS = 2
FR_GRP = 32
CLIPS_ALL = 8
FRAMES_ALL = 128
N_GRP = 4


def place_ends(entries, stream_key, least, high):
    extent = entries.shape
    place = [jax.random.randint(jax.random.fold_in(stream_key, axis), (), 0, extent[axis]) for axis in range(len(extent))]
    entries = entries.at[tuple(place)].set(least)
    longest = extent.index(max(extent))
    place[longest] = (place[longest] + 1) % extent[longest]
    return entries.at[tuple(place)].set(high)


def steps_of(own_key, dims, split, least, top_value):
    loudness, own = 1.0, jax.random.fold_in(own_key, 6)
    for dim, shards_of in split:
        draws = jnp.exp(jax.random.uniform(jax.random.fold_in(own, dim), (shards_of,), jnp.float32, least / len(split), top_value / len(split)))
        loudness = loudness * jnp.repeat(draws, dims[dim] // shards_of).reshape([-1 if axis == dim else 1 for axis in range(len(dims))])
    return loudness


def normal_values(key, extent, scale, reach, shards=(), kind=jnp.bfloat16):
    entries = jax.random.normal(key, extent, jnp.float32) * scale
    if len(shards) > 0:
        entries = steps_of(key, extent, shards, -0.22, 0.18) * entries
    return jnp.clip(entries, min=-reach, max=reach).astype(kind)


def setup_inputs(seed: int = 0) -> dict:
    seeds = jax.random.split(jax.random.key(seed), 18)
    return {
        "frames_in": normal_values(seeds[0], (FRAMES_ALL, PATCHES, D), 1.0, 6.0, ((0, 32),), jnp.float32),
        "cotangent": normal_values(seeds[1], (FRAMES_ALL, PATCHES, D), 1.0, 6.0, ((0, 32),), jnp.float32),
        "time_table": normal_values(seeds[2], (TIME_IDS, D), 1.0, 6.0, ((1, 8),)),
        "ada_weight": normal_values(seeds[3], (D, 9 * D), D ** -0.5, 0.21875, ((0, 8),)),
        "ada_bias": normal_values(seeds[4], (9 * D,), 0.3, 4.0, ((0, 8),)),
        "space_qkv": normal_values(seeds[5], (D, 3 * D), D ** -0.5, 0.21875, ((0, 8),)),
        "space_out": normal_values(seeds[6], (D, D), (D // 128) ** -0.5, 2.5, ((0, 8),)),
        "time_qkv": normal_values(seeds[7], (D, 3 * D), D ** -0.5, 0.21875, ((0, 8),)),
        "time_out": normal_values(seeds[8], (D, D), (D // 16) ** -0.5, 0.875, ((0, 8),)),
        "up_weight": normal_values(seeds[9], (D, FF), D ** -0.5, 0.21875, ((0, 8),)),
        "up_bias": normal_values(seeds[10], (FF,), 0.5, 6.0, ((0, 8),)),
        "down_weight": normal_values(seeds[11], (FF, D), FF ** -0.5, 0.109375, ((0, 8),)),
        "down_bias": normal_values(seeds[12], (D,), 0.3, 4.0, ((0, 8),)),
        "timesteps": place_ends(jax.random.randint(seeds[13], (CLIPS_ALL,), 0, TIME_IDS), jax.random.fold_in(seeds[13], 1), 0, TIME_IDS - 1).astype(jnp.int32),
        "task_mask": place_ends((jax.random.randint(seeds[14], (CLIPS_ALL, FRAMES), 0, 4) < 3).astype(jnp.int32), jax.random.fold_in(seeds[14], 1), 0, 1),
        "clip_weight": jnp.clip(jnp.exp(math.log(2.0) - 1.3862944 * jax.random.uniform(seeds[15], (CLIPS_ALL,), jnp.float32) ** steps_of(seeds[15], (CLIPS_ALL,), ((0, 4),), -0.2, 0.2)), 0.5, 2.0),
        "frame_table": jax.vmap(lambda own: jax.random.permutation(own, FR_GRP))(jax.random.split(seeds[16], N_GRP)).reshape((N_GRP, FR_GRP)).astype(jnp.int32),
    }


HIGH = lax.Precision.HIGHEST
EPSILON = 1e-06

@jax.custom_vjp
def low(v):
    return lax.optimization_barrier(v.astype(jnp.bfloat16)).astype(jnp.float32)

@jax.custom_vjp
def low_back(v):
    return v

def low_keep(v):
    return (low(v), None)

def low_pass(kept, grad):
    return (grad,)

def back_keep(v):
    return (v, None)

def back_low(kept, grad):
    return (low(grad),)
low.defvjp(low_keep, low_pass)
low_back.defvjp(back_keep, back_low)

def both_ways(value):
    return low(low_back(value))

def layer_norm(values):
    center = values - lax.optimization_barrier(jnp.mean(values, axis=-1, keepdims=True))
    spread = lax.optimization_barrier(jnp.mean(center * center, axis=-1, keepdims=True))
    return center * lax.rsqrt(spread + EPSILON)

def attention(entry, qkv_weight, out_weight):
    batch, length, across, width = entry.shape
    packed = both_ways(jnp.einsum('blmd,de->blme', entry, qkv_weight, precision=HIGH))
    shape = (batch, length, across, HEADS, HEAD_DIM)
    query = packed[..., :width].reshape(shape)
    keys = packed[..., width:2 * width].reshape(shape)
    values = packed[..., 2 * width:].reshape(shape)
    scores = low_back(jnp.einsum('blmhe,bkmhe->bmhlk', query, keys, precision=HIGH) * HEAD_DIM ** (-0.5))
    probs = low(jax.nn.softmax(scores, axis=-1))
    mixed = jnp.einsum('bmhlk,bkmhe->blmhe', probs, values, precision=HIGH).reshape(batch, length, across, width)
    mixed = both_ways(mixed)
    return low_back(jnp.einsum('blmd,de->blme', mixed, out_weight, precision=HIGH))

def layer(params, frames, timesteps):
    time_table, ada_weight, ada_bias, space_qkv, space_out, time_qkv, time_out, up_weight, up_bias, down_weight, down_bias = params
    clips = frames.shape[0]
    width = frames.shape[-1]
    onehot = (timesteps[:, None] == jnp.arange(time_table.shape[0], dtype=jnp.int32)[None, :]).astype(jnp.float32)
    embed = jnp.dot(onehot, time_table, precision=HIGH)
    cond = low(jax.nn.silu(embed))
    modul = low_back(jnp.dot(cond, ada_weight, precision=HIGH) + ada_bias)
    parts = [modul[:, part_at * width:(part_at + 1) * width][:, None, None, :] for part_at in range(9)]
    space_in = low(layer_norm(frames) * (1.0 + parts[1]) + parts[0])
    space_mix = attention(space_in.reshape(clips * FRAMES, PATCHES, 1, width), space_qkv, space_out)
    after_space = frames + parts[2] * space_mix.reshape(frames.shape)
    time_in = low(layer_norm(after_space) * (1.0 + parts[4]) + parts[3])
    after_time = after_space + parts[5] * attention(time_in, time_qkv, time_out)
    mlp_in = low(layer_norm(after_time) * (1.0 + parts[7]) + parts[6])
    upward = low_back(jnp.einsum('cfpd,dh->cfph', mlp_in, up_weight, precision=HIGH) + up_bias)
    active = low(jax.nn.gelu(upward, approximate=False))
    downward = low_back(jnp.einsum('cfph,hd->cfpd', active, down_weight, precision=HIGH) + down_bias)
    return after_time + parts[8] * downward

def reference(frames_in, cotangent, time_table, ada_weight, ada_bias, space_qkv, space_out, time_qkv, time_out, up_weight, up_bias, down_weight, down_bias, timesteps, task_mask, clip_weight, frame_table):
    params = tuple((weight_arg.astype(jnp.float32) for weight_arg in (time_table, ada_weight, ada_bias, space_qkv, space_out, time_qkv, time_out, up_weight, up_bias, down_weight, down_bias)))

    def group_step(totals, inputs):
        frames_grp, cot_grp, table, steps_grp, mask_grp, weight_grp = inputs
        slots = jnp.arange(FR_GRP, dtype=jnp.int32)
        inverse = jnp.zeros((FR_GRP,), jnp.int32).at[table].set(slots)
        clip_of = table // FRAMES
        frame_of = table % FRAMES
        scale_rows = mask_grp[clip_of, frame_of].astype(jnp.float32) * weight_grp[clip_of]
        ordered = jnp.take(frames_grp, inverse, axis=0).reshape(CLIPS, FRAMES, PATCHES, D)
        weighted = jnp.take(cot_grp * scale_rows[:, None, None], inverse, axis=0).reshape(CLIPS, FRAMES, PATCHES, D)
        result, pullback = jax.vjp(lambda pars, vals: layer(pars, vals, steps_grp), params, ordered)
        grad_pars, grad_vals = pullback(weighted)
        out_rows = jnp.take(result.reshape(FR_GRP, PATCHES, D), table, axis=0)
        grad_rows = jnp.take(grad_vals.reshape(FR_GRP, PATCHES, D), table, axis=0)
        totals = jax.tree.map(lambda left, right: left + right, totals, grad_pars)
        return (totals, (out_rows, grad_rows))
    start = tuple((jnp.zeros_like(weight_arg) for weight_arg in params))
    inputs = (frames_in.reshape(N_GRP, FR_GRP, PATCHES, D), cotangent.reshape(N_GRP, FR_GRP, PATCHES, D), frame_table, timesteps.reshape(N_GRP, CLIPS), task_mask.reshape(N_GRP, CLIPS, FRAMES), clip_weight.reshape(N_GRP, CLIPS))
    totals, stacked = lax.scan(group_step, start, inputs)
    frames_out = stacked[0].reshape(N_GRP * FR_GRP, PATCHES, D)
    grad_in = stacked[1].reshape(N_GRP * FR_GRP, PATCHES, D)
    return (frames_out, grad_in, totals[0], totals[1], totals[2], totals[3], totals[4], totals[5], totals[6], totals[7], totals[8], totals[9], totals[10])
```

```python
from functools import partial

import jax
import jax.numpy as jnp
from jax import lax
from jax.sharding import PartitionSpec as P

HEADS = 12
HEAD_DIM = 64


HIGH = lax.Precision.HIGHEST
EPSILON = 1e-06


def layer_norm(values):
    center = values - jnp.mean(values, axis=-1, keepdims=True)
    spread = jnp.mean(center * center, axis=-1, keepdims=True)
    inverse = lax.rsqrt(spread + EPSILON)
    return (center * inverse, inverse)


def norm_back(grad_normed, normed, inverse):
    first = jnp.mean(grad_normed, axis=-1, keepdims=True)
    second = jnp.mean(grad_normed * normed, axis=-1, keepdims=True)
    return inverse * (grad_normed - first - normed * second)


def split_heads(packed, width):
    shape = packed.shape[:-1] + (HEADS, HEAD_DIM)
    return (
        packed[..., :width].reshape(shape),
        packed[..., width : 2 * width].reshape(shape),
        packed[..., 2 * width :].reshape(shape),
    )


def attend_forward(packed):
    width = packed.shape[-1] // 3
    query, keys, values = split_heads(packed, width)
    scores = jnp.einsum(
        "blmhe,bkmhe->bmhlk", query, keys, preferred_element_type=jnp.float32
    ) * HEAD_DIM ** (-0.5)
    highest = jnp.max(scores, axis=-1, keepdims=True)
    logsum = highest + jnp.log(jnp.sum(jnp.exp(scores - highest), axis=-1, keepdims=True))
    probs = jnp.exp(scores - logsum).astype(jnp.bfloat16)
    mixed = jnp.einsum("bmhlk,bkmhe->blmhe", probs, values, preferred_element_type=jnp.float32)
    return (mixed.reshape(packed.shape[:-1] + (width,)).astype(jnp.bfloat16), logsum)


def attend_backward(packed, logsum, grad_mixed):
    width = packed.shape[-1] // 3
    query, keys, values = split_heads(packed, width)
    factor = HEAD_DIM ** (-0.5)
    scores = (
        jnp.einsum("blmhe,bkmhe->bmhlk", query, keys, preferred_element_type=jnp.float32) * factor
    )
    probs = jnp.exp(scores - logsum)
    grad_heads = grad_mixed.reshape(query.shape)
    grad_probs = jnp.einsum(
        "blmhe,bkmhe->bmhlk", grad_heads, values, preferred_element_type=jnp.float32
    )
    grad_values = jnp.einsum(
        "bmhlk,blmhe->bkmhe",
        probs.astype(jnp.bfloat16),
        grad_heads,
        preferred_element_type=jnp.float32,
    )
    grad_scores = (
        probs * (grad_probs - jnp.sum(probs * grad_probs, axis=-1, keepdims=True))
    ).astype(jnp.bfloat16)
    grad_query = (
        jnp.einsum("bmhlk,bkmhe->blmhe", grad_scores, keys, preferred_element_type=jnp.float32)
        * factor
    )
    grad_keys = (
        jnp.einsum("bmhlk,blmhe->bkmhe", grad_scores, query, preferred_element_type=jnp.float32)
        * factor
    )
    shape = packed.shape[:-1] + (width,)
    joined = jnp.concatenate(
        [grad_query.reshape(shape), grad_keys.reshape(shape), grad_values.reshape(shape)], axis=-1
    )
    return joined.astype(jnp.bfloat16)


def mixer_forward(resid, shift, scale, gate, qkv_weight, out_weight):
    normed, inverse = layer_norm(resid)
    entry = (normed * (1.0 + scale) + shift).astype(jnp.bfloat16)
    packed = jnp.einsum(
        "blmd,de->blme", entry, qkv_weight, preferred_element_type=jnp.float32
    ).astype(jnp.bfloat16)
    mixed, logsum = attend_forward(packed)
    branch = jnp.einsum("blmd,de->blme", mixed, out_weight, preferred_element_type=jnp.float32)
    return (resid + gate * branch, (normed, inverse, entry, packed, logsum, mixed, branch))


def mixer_backward(grad_out, scale, gate, qkv_weight, out_weight, kept, per_clip):
    normed, inverse, entry, packed, logsum, mixed, branch = kept
    grad_gate = per_clip(grad_out * branch)
    grad_branch = (gate * grad_out).astype(jnp.bfloat16)
    grad_outw = jnp.einsum("blmd,blme->de", mixed, grad_branch, preferred_element_type=jnp.float32)
    grad_mixed = jnp.einsum(
        "blme,de->blmd", grad_branch, out_weight, preferred_element_type=jnp.float32
    ).astype(jnp.bfloat16)
    grad_packed = attend_backward(packed, logsum, grad_mixed)
    grad_qkvw = jnp.einsum("blmd,blme->de", entry, grad_packed, preferred_element_type=jnp.float32)
    grad_entry = jnp.einsum(
        "blme,de->blmd", grad_packed, qkv_weight, preferred_element_type=jnp.float32
    )
    grad_shift = per_clip(grad_entry)
    grad_scale = per_clip(grad_entry * normed)
    grad_in = grad_out + norm_back(grad_entry * (1.0 + scale), normed, inverse)
    return (grad_in, (grad_shift, grad_scale, grad_gate), grad_qkvw, grad_outw)


def feed_forward(resid, shift, scale, gate, up_full, up_bias_full, down_full, down_bias_full):
    normed, inverse = layer_norm(resid)
    entry = (normed * (1.0 + scale) + shift).astype(jnp.bfloat16)
    upward = jnp.einsum(
        "blmd,df->blmf", entry, up_full, preferred_element_type=jnp.float32
    ) + up_bias_full.astype(jnp.float32)
    active = jax.nn.gelu(upward, approximate=False).astype(jnp.bfloat16)
    downward = jnp.einsum(
        "blmf,fd->blmd", active, down_full, preferred_element_type=jnp.float32
    ) + down_bias_full.astype(jnp.float32)
    return (resid + gate * downward, (normed, inverse, entry, upward, active, downward))


def feed_backward(grad_out, scale, gate, up_full, down_full, kept, per_clip):
    normed, inverse, entry, upward, active, downward = kept
    grad_gate = per_clip(grad_out * downward)
    grad_down_in = (gate * grad_out).astype(jnp.bfloat16)
    grad_down = jnp.einsum(
        "blmf,blmd->fd", active, grad_down_in, preferred_element_type=jnp.float32
    )
    grad_down_bias = jnp.sum(grad_down_in.astype(jnp.float32), axis=(0, 1, 2))
    grad_active = jnp.einsum(
        "blmd,fd->blmf", grad_down_in, down_full, preferred_element_type=jnp.float32
    )
    _, gelu_back = jax.vjp(partial(jax.nn.gelu, approximate=False), upward)
    grad_up_in = gelu_back(grad_active)[0].astype(jnp.bfloat16)
    grad_up = jnp.einsum("blmd,blmf->df", entry, grad_up_in, preferred_element_type=jnp.float32)
    grad_up_bias = jnp.sum(grad_up_in.astype(jnp.float32), axis=(0, 1, 2))
    grad_entry = jnp.einsum(
        "blmf,df->blmd", grad_up_in, up_full, preferred_element_type=jnp.float32
    )
    grad_shift = per_clip(grad_entry)
    grad_scale = per_clip(grad_entry * normed)
    grad_in = grad_out + norm_back(grad_entry * (1.0 + scale), normed, inverse)
    return (
        grad_in,
        (grad_shift, grad_scale, grad_gate),
        grad_up,
        grad_up_bias,
        grad_down,
        grad_down_bias,
    )


def body(
    frames_in,
    cotangent,
    time_table,
    ada_weight,
    ada_bias,
    space_qkv,
    space_out,
    time_qkv,
    time_out,
    up_weight,
    up_bias,
    down_weight,
    down_bias,
    timesteps,
    task_mask,
    clip_weight,
    frame_table,
):
    shards = lax.axis_size("shard")
    shard_at = lax.axis_index("shard")
    frame_count, patches, width = frames_in.shape
    clips = timesteps.shape[0]
    frames = task_mask.shape[1]
    table = frame_table[0]
    group_frames = table.shape[0]
    columns = patches // shards
    space_qkv_full = lax.all_gather(space_qkv, "shard", axis=0, tiled=True)
    space_out_full = lax.all_gather(space_out, "shard", axis=0, tiled=True)
    time_qkv_full = lax.all_gather(time_qkv, "shard", axis=0, tiled=True)
    time_out_full = lax.all_gather(time_out, "shard", axis=0, tiled=True)
    up_full = lax.all_gather(up_weight, "shard", axis=0, tiled=True)
    down_full = lax.all_gather(down_weight, "shard", axis=0, tiled=True)
    embed = jnp.take(time_table, timesteps, axis=0).astype(jnp.float32)
    cond = jax.nn.silu(embed).astype(jnp.bfloat16)
    mod_local = jnp.dot(cond, ada_weight, preferred_element_type=jnp.float32)

    def spread(local):
        full = jnp.zeros((shards, local.shape[0]), jnp.float32)
        return lax.dynamic_update_slice_in_dim(
            full, local.astype(jnp.float32)[None], shard_at, 0
        ).reshape(-1)

    small = jnp.concatenate(
        [
            (mod_local + spread(ada_bias)[None]).reshape(-1),
            spread(up_bias),
            spread(down_bias),
        ]
    )
    small = lax.psum(small, "shard")
    modul = small[: clips * 9 * width].reshape(clips, 9 * width)
    up_bias_full = small[clips * 9 * width : -width]
    down_bias_full = small[-width:]
    slot_ids = shard_at * frame_count + jnp.arange(frame_count, dtype=jnp.int32)
    frame_ids = jnp.take(table, slot_ids)
    clip_of = frame_ids // frames
    frame_of = frame_ids % frames
    clip_hot = (clip_of[:, None] == jnp.arange(clips, dtype=jnp.int32)[None, :]).astype(jnp.float32)
    frame_mod = jnp.take(modul, clip_of, axis=0)
    own_parts = [
        frame_mod[:, part_at * width : (part_at + 1) * width][:, None, None, :]
        for part_at in range(9)
    ]
    all_parts = [
        modul[:, part_at * width : (part_at + 1) * width][:, None, None, :] for part_at in range(9)
    ]
    inverse = (
        jnp.zeros((group_frames,), jnp.int32)
        .at[table]
        .set(jnp.arange(group_frames, dtype=jnp.int32))
    )

    def frame_sums(values):
        return jnp.dot(clip_hot.T, jnp.sum(values, axis=(1, 2)), precision=HIGH)

    def column_sums(values):
        return jnp.sum(values, axis=(1, 2))

    def to_columns(rows):
        parts = rows.astype(jnp.bfloat16).reshape(frame_count, shards, columns, width)
        parts = jnp.swapaxes(parts, 0, 1)
        moved = lax.all_to_all(parts, "shard", split_axis=0, concat_axis=0, tiled=True)
        return moved.reshape(group_frames, columns, width)

    def to_frames(cols):
        parts = cols.astype(jnp.bfloat16).reshape(shards, frame_count, columns, width)
        moved = lax.all_to_all(parts, "shard", split_axis=0, concat_axis=0, tiled=True)
        moved = jnp.swapaxes(moved, 0, 1)
        return moved.reshape(frame_count, patches, width).astype(jnp.float32)

    space_rows = frames_in.reshape(frame_count, patches, 1, width)
    after_space, space_kept = mixer_forward(
        space_rows, own_parts[0], own_parts[1], own_parts[2], space_qkv_full, space_out_full
    )
    received = to_columns(after_space.reshape(frame_count, patches, width))
    columned = jnp.take(received, inverse, axis=0).reshape(clips, frames, columns, width)
    columned = columned.astype(jnp.float32)
    after_time, time_kept = mixer_forward(
        columned, all_parts[3], all_parts[4], all_parts[5], time_qkv_full, time_out_full
    )
    result, mlp_kept = feed_forward(
        after_time,
        all_parts[6],
        all_parts[7],
        all_parts[8],
        up_full,
        up_bias_full,
        down_full,
        down_bias_full,
    )
    leaving = jnp.take(result.reshape(group_frames, columns, width), table, axis=0)
    frames_out = to_frames(leaving)
    row_weights = task_mask[clip_of, frame_of].astype(jnp.float32) * clip_weight[clip_of]
    weighted = cotangent * row_weights[:, None, None]
    arriving = to_columns(weighted)
    grad_result = jnp.take(arriving, inverse, axis=0).reshape(clips, frames, columns, width)
    grad_result = grad_result.astype(jnp.float32)
    grad_after_time, mlp_mods, grad_up, grad_up_bias, grad_down, grad_down_bias = feed_backward(
        grad_result, all_parts[7], all_parts[8], up_full, down_full, mlp_kept, column_sums
    )
    grad_columned, time_mods, grad_time_qkv, grad_time_out = mixer_backward(
        grad_after_time,
        all_parts[4],
        all_parts[5],
        time_qkv_full,
        time_out_full,
        time_kept,
        column_sums,
    )
    going = jnp.take(grad_columned.reshape(group_frames, columns, width), table, axis=0)
    grad_space = to_frames(going)
    grad_rows, space_mods, grad_space_qkv, grad_space_out = mixer_backward(
        grad_space.reshape(frame_count, patches, 1, width),
        own_parts[1],
        own_parts[2],
        space_qkv_full,
        space_out_full,
        space_kept,
        frame_sums,
    )
    mod_part = jnp.concatenate(space_mods + time_mods + mlp_mods, axis=1)
    small_grads = jnp.concatenate([mod_part.reshape(-1), grad_up_bias, grad_down_bias])
    small_grads = lax.psum(small_grads, "shard")
    mod_size = clips * 9 * width
    grad_modul = small_grads[:mod_size].reshape(clips, 9 * width).astype(jnp.bfloat16)
    up_dev = up_bias.shape[0]
    down_dev = down_bias.shape[0]
    bias_dev = ada_bias.shape[0]
    every_modul = lax.all_gather(grad_modul, "grp", axis=0, tiled=True)
    bias_sums = lax.psum(
        jnp.concatenate(
            [
                lax.dynamic_slice_in_dim(small_grads, mod_size + shard_at * up_dev, up_dev, 0),
                lax.dynamic_slice_in_dim(
                    small_grads, mod_size + shards * up_dev + shard_at * down_dev, down_dev, 0
                ),
            ]
        ),
        "grp",
    )
    every_embed = lax.all_gather(embed.astype(jnp.bfloat16), "grp", axis=0, tiled=True)
    every_embed = every_embed.astype(jnp.float32)
    groups = lax.axis_size("grp")
    step_slots = jnp.zeros((groups, clips), jnp.float32)
    step_slots = lax.dynamic_update_slice_in_dim(
        step_slots, timesteps.astype(jnp.float32)[None], lax.axis_index("grp"), 0
    )
    every_steps = lax.psum(step_slots.reshape(-1), "grp").astype(jnp.int32)
    every_cond = jax.nn.silu(every_embed).astype(jnp.bfloat16)
    grad_ada = jnp.einsum("cd,cj->dj", every_cond, every_modul, preferred_element_type=jnp.float32)
    grad_ada_bias = lax.dynamic_slice_in_dim(
        jnp.sum(every_modul.astype(jnp.float32), axis=0), shard_at * bias_dev, bias_dev, 0
    )
    grad_cond = jnp.einsum(
        "cj,dj->cd", every_modul, ada_weight, preferred_element_type=jnp.float32
    )
    _, silu_back = jax.vjp(jax.nn.silu, every_embed)
    grad_embed = silu_back(grad_cond)[0]
    vocab = time_table.shape[0]
    onehot = (jnp.arange(vocab, dtype=jnp.int32)[:, None] == every_steps[None, :]).astype(
        jnp.float32
    )
    grad_table = jnp.dot(onehot, grad_embed, precision=HIGH)

    def total(parts):
        flat = [part.astype(jnp.bfloat16).reshape(shards, -1, width) for part in parts]
        rows = [part.shape[1] for part in flat]
        packed = jnp.concatenate(flat, axis=1)
        share = lax.psum_scatter(packed, "shard", scatter_dimension=0, tiled=True)[0]
        share = lax.psum(share, "grp").astype(jnp.float32)
        out, at = [], 0
        for part, count in zip(parts, rows):
            piece = share[at : at + count].reshape(part.shape[0] // shards, part.shape[1])
            out.append(piece)
            at += count
        return out

    grad_up, grad_down = total([grad_up, grad_down])
    grad_time_qkv, grad_time_out = total([grad_time_qkv, grad_time_out])
    grad_space_qkv, grad_space_out = total([grad_space_qkv, grad_space_out])
    return (
        frames_out,
        grad_rows.reshape(frame_count, patches, width),
        grad_table,
        grad_ada,
        grad_ada_bias,
        grad_space_qkv,
        grad_space_out,
        grad_time_qkv,
        grad_time_out,
        grad_up,
        bias_sums[:up_dev],
        grad_down,
        bias_sums[up_dev:],
    )


def solution(mesh):
    placed = (
        P(("grp", "shard"), None, None),
        P(("grp", "shard"), None, None),
        P(None, "shard"),
        P("shard", None),
        P("shard"),
        P("shard", None),
        P("shard", None),
        P("shard", None),
        P("shard", None),
        P("shard", None),
        P("shard"),
        P("shard", None),
        P("shard"),
        P("grp"),
        P("grp", None),
        P("grp"),
        P("grp", None),
    )
    return jax.shard_map(
        body,
        mesh=mesh,
        in_specs=placed,
        out_specs=(
            P(("grp", "shard"), None, None),
            P(("grp", "shard"), None, None),
            P(None, "shard"),
            P("shard", None),
            P("shard"),
            P("shard", None),
            P("shard", None),
            P("shard", None),
            P("shard", None),
            P("shard", None),
            P("shard"),
            P("shard", None),
            P("shard"),
        ),
        check_vma=False,
    )
```

```python
from functools import partial

import jax
import jax.numpy as jnp
from jax import lax
from jax.experimental import pallas as pl
from jax.experimental.pallas import tpu as pltpu
from jax.sharding import PartitionSpec as P

HEADS = 12
HEAD_DIM = 64
PAIR = 2 * HEAD_DIM
ROWS = 256
NEAR = 16
HIGH = lax.Precision.HIGHEST
EPSILON = 1e-06
BF = jnp.bfloat16
F32 = jnp.float32
VMEM_LIMIT = 60 * 1024 * 1024


def layer_norm(values):
    center = values - jnp.mean(values, axis=-1, keepdims=True)
    spread = jnp.mean(center * center, axis=-1, keepdims=True)
    inverse = lax.rsqrt(spread + EPSILON)
    return (center * inverse, inverse)


def norm_back(grad_normed, normed, inverse):
    first = jnp.mean(grad_normed, axis=-1, keepdims=True)
    second = jnp.mean(grad_normed * normed, axis=-1, keepdims=True)
    return inverse * (grad_normed - first - normed * second)


def mul(left, right):
    return jnp.dot(left, right, preferred_element_type=F32)


def mul_rt(left, right):
    return lax.dot_general(left, right, (((1,), (1,)), ((), ())), preferred_element_type=F32)


def mul_lt(left, right):
    return lax.dot_general(left, right, (((0,), (0,)), ((), ())), preferred_element_type=F32)


def half_masks(value):
    lane = lax.broadcasted_iota(jnp.int32, (1, PAIR), 1)
    low = jnp.where(lane < HEAD_DIM, value, 0.0)
    return (low.astype(BF), (value - low).astype(BF))


def same_patch():
    rows = lax.broadcasted_iota(jnp.int32, (ROWS, ROWS), 0)
    cols = lax.broadcasted_iota(jnp.int32, (ROWS, ROWS), 1)
    return jnp.bitwise_and(rows, NEAR - 1) == jnp.bitwise_and(cols, NEAR - 1)


def mixer_forward(resid, mods, at, width, weight, out_weight, keep, near):
    packed_ref, mixed_ref, lse_ref, branch_ref = keep
    shift, scale, gate = mods[at : at + 1], mods[at + 1 : at + 2], mods[at + 2 : at + 3]
    normed, _ = layer_norm(resid)
    entry = (normed * (1.0 + scale) + shift).astype(BF)
    for part in range(3):
        packed_ref[0, :, part * width : (part + 1) * width] = mul(
            entry, weight[:, part * width : (part + 1) * width]
        ).astype(BF)
    same = same_patch() if near else None
    lane = lax.broadcasted_iota(jnp.int32, (ROWS, PAIR), 1)
    scaled = half_masks(HEAD_DIM ** (-0.5))
    for pair in range(HEADS // 2):
        at_q = pair * PAIR
        query = packed_ref[0, :, at_q : at_q + PAIR]
        keys = packed_ref[0, :, width + at_q : width + at_q + PAIR]
        values = packed_ref[0, :, 2 * width + at_q : 2 * width + at_q + PAIR]
        halves = []
        for half in range(2):
            scores = mul_rt(keys, query * scaled[half])
            if near:
                scores = jnp.where(same, scores, -jnp.inf)
            highest = jnp.max(scores, axis=0, keepdims=True)
            weights = jnp.exp(scores - highest)
            total = jnp.sum(weights, axis=0, keepdims=True)
            head = 2 * pair + half
            lse_ref[0, head : head + 1, :] = highest + jnp.log(total)
            probs = (weights * (1.0 / total)).astype(BF)
            halves.append(mul_lt(probs, values))
        mixed_ref[0, :, at_q : at_q + PAIR] = jnp.where(
            lane < HEAD_DIM, halves[0], halves[1]
        ).astype(BF)
    branch = mul(mixed_ref[0], out_weight[...])
    branch_ref[0] = branch.astype(BF)
    return resid + gate * branch


def mixer_backward(grad_out, resid, mods, at, width, weight, out_weight, kept, work, near):
    packed_ref, mixed_ref, lse_ref, branch_ref = kept
    entry_ref, packed_grad_ref, branch_grad_ref = work
    shift, scale, gate = mods[at : at + 1], mods[at + 1 : at + 2], mods[at + 2 : at + 3]
    grad_gate = jnp.sum(grad_out * branch_ref[0].astype(F32), axis=0, keepdims=True)
    grad_branch = (gate * grad_out).astype(BF)
    branch_grad_ref[...] = grad_branch
    grad_mixed = mul_rt(grad_branch, out_weight[...]).astype(BF)
    same = same_patch() if near else None
    lane = lax.broadcasted_iota(jnp.int32, (ROWS, PAIR), 1)
    scaled = half_masks(HEAD_DIM ** (-0.5))
    ones = half_masks(1.0)
    for pair in range(HEADS // 2):
        at_q = pair * PAIR
        query = packed_ref[0, :, at_q : at_q + PAIR]
        keys = packed_ref[0, :, width + at_q : width + at_q + PAIR]
        values = packed_ref[0, :, 2 * width + at_q : 2 * width + at_q + PAIR]
        grads = grad_mixed[:, at_q : at_q + PAIR]
        grad_query = []
        grad_keys = None
        grad_values = None
        for half in range(2):
            head = 2 * pair + half
            own_query = query * scaled[half]
            own_grads = grads * ones[half]
            scores = mul_rt(keys, own_query)
            if near:
                scores = jnp.where(same, scores, -jnp.inf)
            probs = jnp.exp(scores - lse_ref[0, head : head + 1, :])
            grad_probs = mul_rt(values, own_grads)
            inner = jnp.sum(probs * grad_probs, axis=0, keepdims=True)
            grad_scores = (probs * (grad_probs - inner)).astype(BF)
            part_values = mul(probs.astype(BF), own_grads)
            part_keys = mul(grad_scores, own_query)
            grad_query.append(mul_lt(grad_scores, keys))
            grad_keys = part_keys if half == 0 else grad_keys + part_keys
            grad_values = part_values if half == 0 else grad_values + part_values
        joined = jnp.where(lane < HEAD_DIM, grad_query[0], grad_query[1])
        packed_grad_ref[:, at_q : at_q + PAIR] = (joined * HEAD_DIM ** (-0.5)).astype(BF)
        packed_grad_ref[:, width + at_q : width + at_q + PAIR] = grad_keys.astype(BF)
        packed_grad_ref[:, 2 * width + at_q : 2 * width + at_q + PAIR] = (
            grad_values.astype(BF)
        )
    grad_entry = mul_rt(packed_grad_ref[...], weight[...])
    normed, inverse = layer_norm(resid)
    entry_ref[...] = (normed * (1.0 + scale) + shift).astype(BF)
    grad_shift = jnp.sum(grad_entry, axis=0, keepdims=True)
    grad_scale = jnp.sum(grad_entry * normed, axis=0, keepdims=True)
    grad_in = grad_out + norm_back(grad_entry * (1.0 + scale), normed, inverse)
    return grad_in, (grad_shift, grad_scale, grad_gate)


def fetch_weights(packed, places, sem):
    copies = []
    for shard in range(packed.shape[0]):
        for block in range(packed.shape[1]):
            copies.append(
                pltpu.make_async_copy(packed.at[shard, block], places(shard, block), sem)
            )
    for copy in copies:
        copy.start()
    for copy in copies:
        copy.wait()


def fetch_pieces(me, pieces, weight, out_weight, sem):
    _, rows, width = pieces[0].shape
    copies = []
    for distance, piece in enumerate(pieces):
        first = pl.multiple_of(jnp.bitwise_xor(me, distance) * rows, rows)
        for block in range(3):
            target = weight.at[pl.ds(first, rows), block * width : (block + 1) * width]
            copies.append(pltpu.make_async_copy(piece.at[block], target, sem))
        copies.append(
            pltpu.make_async_copy(piece.at[3], out_weight.at[pl.ds(first, rows), :], sem)
        )
    for copy in copies:
        copy.start()
    for copy in copies:
        copy.wait()


def mixer_places(weight, out_weight, rows, width):
    def places(shard, block):
        if block < 3:
            return weight.at[
                shard * rows : (shard + 1) * rows, block * width : (block + 1) * width
            ]
        return out_weight.at[shard * rows : (shard + 1) * rows, :]

    return places


def mixer_weight_grads(entry, packed_grad, mixed, branch_grad, out, shards, width):
    rows = width // shards
    entry_t = entry[...].T
    for block in range(3):
        grad = mul(entry_t, packed_grad[:, block * width : (block + 1) * width]).astype(BF)
        out[:, block] = grad.reshape(shards, rows, width)
    grad = mul(mixed.T, branch_grad[...]).astype(BF)
    out[:, 3] = grad.reshape(shards, rows, width)


def add_mods(mods_out, clip, grads):
    for at, grad in enumerate(grads):
        mods_out[clip, at : at + 1, :] += grad


def space_forward_kernel(shards, where, frames_ref, mods_ref, *refs):
    pieces = refs[:shards]
    after_ref, packed_ref, mixed_ref, lse_ref, branch_ref = refs[shards : shards + 5]
    weight, out_weight, sem = refs[shards + 5 :]
    step = pl.program_id(0)
    width = frames_ref.shape[-1]

    @pl.when(step == 0)
    def _():
        fetch_pieces(where[pl.num_programs(0)], pieces, weight, out_weight, sem)

    mods = mods_ref[where[step]]
    after = mixer_forward(
        frames_ref[0], mods, 0, width, weight, out_weight,
        (packed_ref, mixed_ref, lse_ref, branch_ref), False,
    )
    after_ref[...] = after.astype(BF).reshape(after_ref.shape)


def space_backward_kernel(
    shards, where, grad_ref, frames_ref, mods_ref, packed_ref, mixed_ref, lse_ref, branch_ref, *refs
):
    pieces = refs[:shards]
    rows_out, mods_out, grads_out = refs[shards : shards + 3]
    weight, out_weight, entry, packed_grad, mixed, branch_grad, sem = refs[shards + 3 :]
    step = pl.program_id(0)
    width = frames_ref.shape[-1]

    @pl.when(step == 0)
    def _():
        fetch_pieces(where[pl.num_programs(0)], pieces, weight, out_weight, sem)
        mods_out[...] = jnp.zeros_like(mods_out)

    clip = where[step]
    own = pl.ds(pl.multiple_of(step * ROWS, ROWS), ROWS)
    grad_out = grad_ref[...].reshape(ROWS, width).astype(F32)
    grad_in, grads = mixer_backward(
        grad_out, frames_ref[0], mods_ref[clip], 0, width, weight, out_weight,
        (packed_ref, mixed_ref, lse_ref, branch_ref),
        (entry.at[own], packed_grad.at[own], branch_grad.at[own]), False,
    )
    rows_out[0] = grad_in
    mixed[own] = mixed_ref[0]
    add_mods(mods_out, clip, grads)

    @pl.when(step == pl.num_programs(0) - 1)
    def _():
        mixer_weight_grads(entry, packed_grad, mixed[...], branch_grad, grads_out, shards, width)


def load_near(source, inverse, resid, clip, first, frames):
    for frame in range(frames):
        values = source[inverse[clip * frames + frame], pl.ds(first, NEAR), :]
        resid[frame * NEAR : (frame + 1) * NEAR, :] = values.astype(F32)


def store_near(target, inverse, values, clip, first, frames):
    for frame in range(frames):
        own = values[frame * NEAR : (frame + 1) * NEAR]
        target[inverse[clip * frames + frame], pl.ds(first, NEAR), :] = own.astype(BF)


def block_place(columns):
    step = pl.program_id(0)
    per_clip = columns // NEAR
    clip = step // per_clip
    first = pl.multiple_of((step - clip * per_clip) * NEAR, NEAR)
    return step, clip, first


def time_forward_kernel(
    frames, inverse, source, mods_ref, packed_w, resid_ref, after_ref, packed_ref, mixed_ref,
    lse_ref, branch_ref, weight, out_weight, resid, sem,
):
    step, clip, first = block_place(source.shape[1])
    shards, _, rows, width = packed_w.shape

    @pl.when(step == 0)
    def _():
        fetch_weights(packed_w, mixer_places(weight, out_weight, rows, width), sem)

    load_near(source, inverse, resid, clip, first, frames)
    resid_ref[0] = resid[...].astype(BF)
    after_ref[0] = mixer_forward(
        resid[...], mods_ref[clip], 3, width, weight, out_weight,
        (packed_ref, mixed_ref, lse_ref, branch_ref), True,
    )


def time_backward_kernel(
    frames, inverse, grad_ref, resid_ref, mods_ref, packed_ref, mixed_ref, lse_ref, branch_ref,
    packed_w, going, mods_out, grads_out, weight, out_weight, entry, packed_grad, mixed,
    branch_grad, sem,
):
    step, clip, first = block_place(going.shape[1])
    shards, _, rows, width = packed_w.shape

    @pl.when(step == 0)
    def _():
        fetch_weights(packed_w, mixer_places(weight, out_weight, rows, width), sem)
        mods_out[...] = jnp.zeros_like(mods_out)

    own = pl.ds(pl.multiple_of(step * ROWS, ROWS), ROWS)
    grad_in, grads = mixer_backward(
        grad_ref[0], resid_ref[0].astype(F32), mods_ref[clip], 3, width, weight, out_weight,
        (packed_ref, mixed_ref, lse_ref, branch_ref),
        (entry.at[own], packed_grad.at[own], branch_grad.at[own]), True,
    )
    store_near(going, inverse, grad_in, clip, first, frames)
    mixed[own] = mixed_ref[0]
    add_mods(mods_out, clip, grads)

    @pl.when(step == pl.num_programs(0) - 1)
    def _():
        mixer_weight_grads(entry, packed_grad, mixed[...], branch_grad, grads_out, shards, width)


def feed_kernel(
    frames, inverse, after_ref, source, mods_ref, up_bias, down_bias, packed_w, result, grad_ref,
    mods_out, up_bias_out, down_bias_out, grads_out, up, down, entry, active, grad_up_in,
    grad_down_in, grad_result, staged, sem, out_sem,
):
    step, clip, first = block_place(source.shape[1])
    shards, _, rows, width = packed_w.shape
    hidden = up.shape[1]
    chunks = hidden // width

    @pl.when(step == 0)
    def _():
        def places(shard, block):
            if block < chunks:
                return up.at[
                    shard * rows : (shard + 1) * rows, block * width : (block + 1) * width
                ]
            start = (shard * chunks + block - chunks) * rows
            return down.at[start : start + rows, :]

        fetch_weights(packed_w, places, sem)
        mods_out[...] = jnp.zeros_like(mods_out)
        up_bias_out[...] = jnp.zeros_like(up_bias_out)
        down_bias_out[...] = jnp.zeros_like(down_bias_out)

    own = pl.ds(pl.multiple_of(step * ROWS, ROWS), ROWS)
    mods = mods_ref[clip]
    shift, scale, gate = mods[6:7], mods[7:8], mods[8:9]
    load_near(source, inverse, grad_result, clip, first, frames)
    grad_out = grad_result[...]
    down_in = (gate * grad_out).astype(BF)
    grad_down_in[own] = down_in
    down_bias_out[...] += jnp.sum(down_in.astype(F32), axis=0, keepdims=True)
    resid = after_ref[0]
    normed, inverse_std = layer_norm(resid)
    entered = (normed * (1.0 + scale) + shift).astype(BF)
    entry[own] = entered
    downward = jnp.broadcast_to(down_bias[...], (ROWS, width))
    grad_entry = jnp.zeros((ROWS, width), F32)
    for chunk in range(chunks):
        cols = slice(chunk * width, (chunk + 1) * width)
        upward = mul(entered, up[:, cols]) + up_bias[:, cols]
        below = 0.5 + 0.5 * lax.erf(upward * 2.0 ** (-0.5))
        density = jnp.exp(-0.5 * upward * upward) * 0.3989422804014327
        acted = (upward * below).astype(BF)
        active[own, cols] = acted
        downward = downward + mul(acted, down[cols, :])
        grad_active = mul_rt(down_in, down[cols, :])
        up_in = (grad_active * (below + upward * density)).astype(BF)
        grad_up_in[own, cols] = up_in
        up_bias_out[:, cols] += jnp.sum(up_in.astype(F32), axis=0, keepdims=True)
        grad_entry = grad_entry + mul_rt(up_in, up[:, cols])
    store_near(result, inverse, resid + gate * downward, clip, first, frames)
    grad_gate = jnp.sum(grad_out * downward, axis=0, keepdims=True)
    grad_shift = jnp.sum(grad_entry, axis=0, keepdims=True)
    grad_scale = jnp.sum(grad_entry * normed, axis=0, keepdims=True)
    add_mods(mods_out, clip, (grad_shift, grad_scale, grad_gate))
    grad_ref[0] = grad_out + norm_back(grad_entry * (1.0 + scale), normed, inverse_std)

    @pl.when(step == pl.num_programs(0) - 1)
    def _():
        entry_t = entry[...].T
        copies = []
        for chunk in range(chunks):
            grad = mul(entry_t, grad_up_in[:, chunk * width : (chunk + 1) * width]).astype(BF)
            staged[chunk] = grad.reshape(shards, rows, width)
            copies.append(
                pltpu.make_async_copy(staged.at[chunk], grads_out.at[:, chunk], out_sem.at[chunk])
            )
            copies[-1].start()
        group = shards // chunks
        for chunk in range(chunks):
            grad = mul_lt(active[:, chunk * width : (chunk + 1) * width], grad_down_in[...])
            slot = chunks + chunk
            staged[slot] = grad.astype(BF).reshape(shards, rows, width)
            copies.append(
                pltpu.make_async_copy(
                    staged.at[slot].reshape(group, chunks, rows, width),
                    grads_out.at[chunk * group : (chunk + 1) * group, chunks:],
                    out_sem.at[slot],
                )
            )
            copies[-1].start()
        for copy in copies:
            copy.wait()


def whole(shape):
    return pl.BlockSpec(shape, lambda *_: (0,) * len(shape))


def per_step(shape):
    return pl.BlockSpec((1,) + tuple(shape[1:]), lambda step, *_: (step,) + (0,) * (len(shape) - 1))


ANY = pl.BlockSpec(memory_space=pl.ANY)


def run(kernel, steps, table, ins, in_specs, outs, out_specs, scratch, flops, name):
    size = lambda shaped: shaped.size * shaped.dtype.itemsize
    moved = sum(size(a) for a in ins) + sum(size(a) for a in outs)
    return pl.pallas_call(
        kernel,
        grid_spec=pltpu.PrefetchScalarGridSpec(
            num_scalar_prefetch=1, grid=(steps,), in_specs=in_specs, out_specs=out_specs,
            scratch_shapes=scratch,
        ),
        out_shape=outs,
        compiler_params=pltpu.CompilerParams(
            dimension_semantics=("arbitrary",), vmem_limit_bytes=VMEM_LIMIT
        ),
        cost_estimate=pl.CostEstimate(flops=flops, bytes_accessed=moved, transcendentals=0),
        name=name,
    )(table, *ins)


def body(
    frames_in,
    cotangent,
    time_table,
    ada_weight,
    ada_bias,
    space_qkv,
    space_out,
    time_qkv,
    time_out,
    up_weight,
    up_bias,
    down_weight,
    down_bias,
    timesteps,
    task_mask,
    clip_weight,
    frame_table,
):
    shards = lax.axis_size("shard")
    shard_at = lax.axis_index("shard")
    frame_count, patches, width = frames_in.shape
    clips = timesteps.shape[0]
    frames = task_mask.shape[1]
    table = frame_table[0]
    group_frames = table.shape[0]
    columns = patches // shards
    rows = width // shards
    hidden = up_weight.shape[1]
    chunks = hidden // width
    tokens = group_frames * columns
    steps = tokens // ROWS
    shaped = jax.ShapeDtypeStruct

    def column_blocks(weight):
        return jnp.swapaxes(weight.reshape(rows, -1, width), 0, 1)

    def swap(values, distance):
        pairs = [(at, at ^ distance) for at in range(shards)]
        return lax.ppermute(values, "shard", pairs)

    def gather(packed):
        return lax.all_gather(packed[None], "shard", axis=0, tiled=True)

    def shard_sum(values):
        distance = 1
        while distance < shards:
            values = values + swap(values, distance)
            distance *= 2
        return values

    own_space = jnp.concatenate([column_blocks(space_qkv), space_out[None]], axis=0)
    even = [own_space] + [swap(own_space, distance) for distance in range(2, shards, 2)]

    embed = jnp.take(time_table, timesteps, axis=0).astype(F32)
    cond = jax.nn.silu(embed).astype(BF)
    mod_local = jnp.dot(cond, ada_weight, preferred_element_type=F32)

    def spread(local):
        full = jnp.zeros((shards, local.shape[0]), F32)
        return lax.dynamic_update_slice_in_dim(
            full, local.astype(F32)[None], shard_at, 0
        ).reshape(-1)

    small = jnp.concatenate(
        [
            (mod_local + spread(ada_bias)[None]).reshape(-1),
            spread(up_bias),
            spread(down_bias),
        ]
    )
    small = lax.all_gather(small.reshape(1, -1, 128), "shard", axis=0, tiled=True)
    small, even[1] = lax.optimization_barrier((small, even[1]))
    small = jnp.sum(small, axis=0).reshape(-1)
    space_w = []
    for piece in even:
        space_w += [piece, swap(piece, 1)]
    own_time = jnp.concatenate([column_blocks(time_qkv), time_out[None]], axis=0)
    own_feed = jnp.concatenate(
        [column_blocks(up_weight), down_weight.reshape(chunks, rows, width)], axis=0
    )
    own_time, own_feed, *_ = lax.optimization_barrier((own_time, own_feed, *even[1:]))
    time_w = gather(own_time)
    feed_w = gather(own_feed)
    mod_size = clips * 9 * width
    modul = small[:mod_size].reshape(clips, 9, width)
    up_bias_full = small[mod_size:-width].reshape(1, hidden)
    down_bias_full = small[-width:].reshape(1, width)

    slot_ids = shard_at * frame_count + jnp.arange(frame_count, dtype=jnp.int32)
    frame_ids = jnp.take(table, slot_ids)
    clip_of = frame_ids // frames
    frame_of = frame_ids % frames
    where = jnp.concatenate([clip_of, shard_at[None].astype(jnp.int32)])
    slots = jnp.arange(group_frames, dtype=jnp.int32)
    inverse = jnp.sum(jnp.where(table[None, :] == slots[:, None], slots[None, :], 0), axis=1)

    def exchange(parts):
        return lax.all_to_all(parts, "shard", split_axis=0, concat_axis=0, tiled=True)

    row_weights = task_mask[clip_of, frame_of].astype(F32) * clip_weight[clip_of]
    weighted = (cotangent * row_weights[:, None, None]).astype(BF)
    weighted = jnp.swapaxes(weighted.reshape(frame_count, shards, columns, width), 0, 1)
    arriving = exchange(weighted).reshape(group_frames, columns, width)

    own_shape = (shards, frame_count, columns, width)
    own_spec = pl.BlockSpec((shards, 1, columns, width), lambda step, *_: (0, step, 0, 0))
    mods_spec = whole((clips, 9, width))
    mods_out = shaped((clips, 3, width), F32)
    mods_out_spec = whole((clips, 3, width))
    grads_shape = (shards, 4, rows, width)
    weight_scratch = [
        pltpu.VMEM((width, 3 * width), BF),
        pltpu.VMEM((width, width), BF),
    ]
    dma = pltpu.SemaphoreType.DMA

    def kept(count):
        shapes = [
            shaped((count, ROWS, 3 * width), BF),
            shaped((count, ROWS, width), BF),
            shaped((count, 16, ROWS), F32),
            shaped((count, ROWS, width), BF),
        ]
        return shapes, [per_step(one.shape) for one in shapes]

    def back_scratch(count):
        return [
            pltpu.VMEM((count * ROWS, width), BF),
            pltpu.VMEM((count * ROWS, 3 * width), BF),
            pltpu.VMEM((count * ROWS, width), BF),
            pltpu.VMEM((count * ROWS, width), BF),
        ]

    mixer_flops = 2 * tokens * width * 4 * width + 4 * tokens * ROWS * width * 2
    space_keep, space_keep_specs = kept(frame_count)
    after_space, *space_kept = run(
        partial(space_forward_kernel, shards), frame_count, where,
        [frames_in, modul] + space_w,
        [per_step(frames_in.shape), mods_spec] + [ANY] * shards,
        [shaped(own_shape, BF)] + space_keep,
        [own_spec] + space_keep_specs,
        weight_scratch + [dma(())],
        mixer_flops, "space_forward",
    )
    received = exchange(after_space).reshape(group_frames, columns, width)
    own_ids = jnp.concatenate([embed, timesteps.astype(F32)[:, None]], axis=1)
    own_ids, _ = lax.optimization_barrier((own_ids, after_space))
    every_ids = lax.all_gather(own_ids, "grp", axis=0, tiled=True)
    received, every_ids = lax.optimization_barrier((received, every_ids))

    cols_spec = whole((group_frames, columns, width))
    cols_shape = shaped((group_frames, columns, width), BF)
    block_shape = (steps, ROWS, width)
    time_keep, time_keep_specs = kept(steps)
    time_resid, after_time, *time_kept = run(
        partial(time_forward_kernel, frames), steps, inverse,
        [received, modul, time_w],
        [cols_spec, mods_spec, ANY],
        [shaped(block_shape, BF), shaped(block_shape, F32)] + time_keep,
        [per_step(block_shape)] * 2 + time_keep_specs,
        weight_scratch + [pltpu.VMEM((ROWS, width), F32), dma(())],
        mixer_flops, "time_forward",
    )

    result, grad_after_time, mlp_mods, grad_up_bias, grad_down_bias, feed_grads = run(
        partial(feed_kernel, frames), steps, inverse,
        [after_time, arriving, modul, up_bias_full, down_bias_full, feed_w],
        [per_step(block_shape), cols_spec, mods_spec, whole((1, hidden)), whole((1, width)), ANY],
        [
            cols_shape,
            shaped(block_shape, F32),
            mods_out,
            shaped((1, hidden), F32),
            shaped((1, width), F32),
            shaped((shards, 2 * chunks, rows, width), BF),
        ],
        [
            cols_spec, per_step(block_shape), mods_out_spec, whole((1, hidden)),
            whole((1, width)), ANY,
        ],
        [
            pltpu.VMEM((width, hidden), BF),
            pltpu.VMEM((hidden, width), BF),
            pltpu.VMEM((tokens, width), BF),
            pltpu.VMEM((tokens, hidden), BF),
            pltpu.VMEM((tokens, hidden), BF),
            pltpu.VMEM((tokens, width), BF),
            pltpu.VMEM((ROWS, width), F32),
            pltpu.VMEM((2 * chunks, shards, rows, width), BF),
            dma(()),
            dma((2 * chunks,)),
        ],
        6 * 2 * tokens * width * hidden, "feed",
    )

    def to_rows(moved):
        moved = jnp.swapaxes(moved.reshape(own_shape), 0, 1)
        return moved.reshape(frame_count, patches, width).astype(F32)

    def shard_total(packed):
        return lax.psum_scatter(packed, "shard", scatter_dimension=0, tiled=True)[0]

    groups = lax.axis_size("grp")
    group_at = lax.axis_index("grp")

    def swap_group(values, distance):
        pairs = [(at, at ^ distance) for at in range(groups)]
        return lax.ppermute(values, "grp", pairs)

    def total(share):
        parts = share.reshape(groups, -1, width)

        def part(values, at):
            return lax.dynamic_index_in_dim(values, at, 0, keepdims=False)

        own = part(parts, group_at).astype(F32)
        for distance in range(1, groups):
            own = own + swap_group(part(parts, group_at ^ distance), distance).astype(F32)
        own = own.astype(BF)
        near = jnp.stack([own] + [swap_group(own, distance) for distance in range(1, groups)])
        step = 1
        while step < groups:
            flipped = near.reshape(-1, 2, step, *own.shape)[:, ::-1].reshape(near.shape)
            near = jnp.where(jnp.bitwise_and(group_at, step) > 0, flipped, near)
            step *= 2
        return near.reshape(share.shape).astype(F32)

    feed_share = shard_total(feed_grads)

    going, time_mods, time_grads = run(
        partial(time_backward_kernel, frames), steps, inverse,
        [grad_after_time, time_resid, modul] + time_kept + [time_w],
        [per_step(block_shape)] * 2 + [mods_spec] + time_keep_specs + [ANY],
        [cols_shape, mods_out, shaped(grads_shape, BF)],
        [cols_spec, mods_out_spec, whole(grads_shape)],
        weight_scratch + back_scratch(steps) + [dma(())],
        3 * mixer_flops, "time_backward",
    )
    grad_space = exchange(going.reshape(own_shape))
    time_grads, feed_share, grad_space, result = lax.optimization_barrier(
        (time_grads, feed_share, grad_space, result)
    )
    time_share = shard_total(time_grads)
    arrived = exchange(result.reshape(own_shape))
    grad_rows, space_mods, space_grads = run(
        partial(space_backward_kernel, shards), frame_count, where,
        [grad_space, frames_in, modul] + space_kept + space_w,
        [own_spec, per_step(frames_in.shape), mods_spec] + space_keep_specs + [ANY] * shards,
        [shaped(frames_in.shape, F32), mods_out, shaped(grads_shape, BF)],
        [per_step(frames_in.shape), mods_out_spec, whole(grads_shape)],
        weight_scratch + back_scratch(frame_count) + [dma(())],
        3 * mixer_flops, "space_backward",
    )
    space_grads, arrived = lax.optimization_barrier((space_grads, arrived))
    space_share = shard_total(space_grads)
    frames_out = to_rows(arrived)
    feed_share, space_mods = lax.optimization_barrier((feed_share, space_mods))
    feed_share = total(feed_share)
    time_share = total(time_share)
    space_share = total(space_share)

    mod_part = jnp.concatenate([space_mods, time_mods, mlp_mods], axis=1)
    small_grads = jnp.concatenate(
        [mod_part.reshape(-1), grad_up_bias.reshape(-1), grad_down_bias.reshape(-1)]
    )
    small_grads = shard_sum(small_grads.reshape(-1, 128)).reshape(-1)
    up_dev = up_bias.shape[0]
    down_dev = down_bias.shape[0]
    bias_dev = ada_bias.shape[0]
    small_grads = jnp.concatenate(
        [
            small_grads[:mod_size],
            lax.dynamic_slice_in_dim(small_grads, mod_size + shard_at * up_dev, up_dev, 0),
            lax.dynamic_slice_in_dim(
                small_grads, mod_size + shards * up_dev + shard_at * down_dev, down_dev, 0
            ),
        ]
    )
    small_size = small_grads.shape[0]
    small_grads = jnp.pad(small_grads, (0, -small_size % 1024)).reshape(1, -1, 128)
    every_small = lax.all_gather(small_grads, "grp", axis=0, tiled=True).reshape(groups, -1)
    every_modul = every_small[:, :mod_size].reshape(groups * clips, 9 * width).astype(BF)
    bias_sums = jnp.sum(every_small[:, mod_size:small_size], axis=0)
    every_embed = every_ids[:, :-1]
    every_steps = every_ids[:, -1].astype(jnp.int32)
    every_cond = jax.nn.silu(every_embed).astype(BF)
    grad_ada = jnp.einsum("cd,cj->dj", every_cond, every_modul, preferred_element_type=F32)
    grad_ada_bias = lax.dynamic_slice_in_dim(
        jnp.sum(every_modul.astype(F32), axis=0), shard_at * bias_dev, bias_dev, 0
    )
    grad_cond = jnp.einsum("cj,dj->cd", every_modul, ada_weight, preferred_element_type=F32)
    _, silu_back = jax.vjp(jax.nn.silu, every_embed)
    grad_embed = silu_back(grad_cond)[0]
    vocab = time_table.shape[0]
    onehot = (jnp.arange(vocab, dtype=jnp.int32)[:, None] == every_steps[None, :]).astype(F32)
    grad_table = jnp.dot(onehot, grad_embed, precision=HIGH)

    def rows_of(blocks):
        return jnp.swapaxes(blocks, 0, 1).reshape(rows, -1)

    return (
        frames_out,
        grad_rows,
        grad_table,
        grad_ada,
        grad_ada_bias,
        rows_of(space_share[:3]),
        space_share[3],
        rows_of(time_share[:3]),
        time_share[3],
        rows_of(feed_share[:chunks]),
        bias_sums[:up_dev],
        feed_share[chunks:].reshape(chunks * rows, width),
        bias_sums[up_dev:],
    )


def solution(mesh):
    placed = (
        P(("grp", "shard"), None, None),
        P(("grp", "shard"), None, None),
        P(None, "shard"),
        P("shard", None),
        P("shard"),
        P("shard", None),
        P("shard", None),
        P("shard", None),
        P("shard", None),
        P("shard", None),
        P("shard"),
        P("shard", None),
        P("shard"),
        P("grp"),
        P("grp", None),
        P("grp"),
        P("grp", None),
    )
    return jax.shard_map(
        body,
        mesh=mesh,
        in_specs=placed,
        out_specs=(
            P(("grp", "shard"), None, None),
            P(("grp", "shard"), None, None),
            P(None, "shard"),
            P("shard", None),
            P("shard"),
            P("shard", None),
            P("shard", None),
            P("shard", None),
            P("shard", None),
            P("shard", None),
            P("shard"),
            P("shard", None),
            P("shard"),
        ),
        check_vma=False,
    )
```

```python
from functools import partial

import jax
import jax.numpy as jnp
from jax import lax
from jax.experimental import pallas as pl
from jax.experimental.pallas import tpu as pltpu
from jax.sharding import PartitionSpec as P

HEADS = 12
HEAD_DIM = 64
PAIR = 2 * HEAD_DIM
ROWS = 256
NEAR = 16
HIGH = lax.Precision.HIGHEST
EPSILON = 1e-06
BF = jnp.bfloat16
F32 = jnp.float32
VMEM_LIMIT = 60 * 1024 * 1024


def layer_norm(values):
    center = values - jnp.mean(values, axis=-1, keepdims=True)
    spread = jnp.mean(center * center, axis=-1, keepdims=True)
    inverse = lax.rsqrt(spread + EPSILON)
    return (center * inverse, inverse)


def norm_back(grad_normed, normed, inverse):
    first = jnp.mean(grad_normed, axis=-1, keepdims=True)
    second = jnp.mean(grad_normed * normed, axis=-1, keepdims=True)
    return inverse * (grad_normed - first - normed * second)


def mul(left, right):
    return jnp.dot(left, right, preferred_element_type=F32)


def mul_rt(left, right):
    return lax.dot_general(left, right, (((1,), (1,)), ((), ())), preferred_element_type=F32)


def mul_lt(left, right):
    return lax.dot_general(left, right, (((0,), (0,)), ((), ())), preferred_element_type=F32)


def half_masks(value):
    lane = lax.broadcasted_iota(jnp.int32, (1, PAIR), 1)
    low = jnp.where(lane < HEAD_DIM, value, 0.0)
    return (low.astype(BF), (value - low).astype(BF))


def same_patch():
    rows = lax.broadcasted_iota(jnp.int32, (ROWS, ROWS), 0)
    cols = lax.broadcasted_iota(jnp.int32, (ROWS, ROWS), 1)
    return jnp.bitwise_and(rows, NEAR - 1) == jnp.bitwise_and(cols, NEAR - 1)


def mixer_forward(resid, mods, at, width, weight, out_weight, keep, near):
    packed_ref, mixed_ref, lse_ref, branch_ref = keep
    shift, scale, gate = mods[at : at + 1], mods[at + 1 : at + 2], mods[at + 2 : at + 3]
    normed, _ = layer_norm(resid)
    entry = (normed * (1.0 + scale) + shift).astype(BF)
    for part in range(3):
        packed_ref[0, :, part * width : (part + 1) * width] = mul(
            entry, weight[:, part * width : (part + 1) * width]
        ).astype(BF)
    same = same_patch() if near else None
    lane = lax.broadcasted_iota(jnp.int32, (ROWS, PAIR), 1)
    scaled = half_masks(HEAD_DIM ** (-0.5))
    for pair in range(HEADS // 2):
        at_q = pair * PAIR
        query = packed_ref[0, :, at_q : at_q + PAIR]
        keys = packed_ref[0, :, width + at_q : width + at_q + PAIR]
        values = packed_ref[0, :, 2 * width + at_q : 2 * width + at_q + PAIR]
        halves = []
        for half in range(2):
            scores = mul_rt(keys, query * scaled[half])
            if near:
                scores = jnp.where(same, scores, -jnp.inf)
            highest = jnp.max(scores, axis=0, keepdims=True)
            weights = jnp.exp(scores - highest)
            total = jnp.sum(weights, axis=0, keepdims=True)
            head = 2 * pair + half
            lse_ref[0, head : head + 1, :] = highest + jnp.log(total)
            probs = (weights * (1.0 / total)).astype(BF)
            halves.append(mul_lt(probs, values))
        mixed_ref[0, :, at_q : at_q + PAIR] = jnp.where(
            lane < HEAD_DIM, halves[0], halves[1]
        ).astype(BF)
    branch = mul(mixed_ref[0], out_weight[...])
    branch_ref[0] = branch.astype(BF)
    return resid + gate * branch


def mixer_backward(grad_out, resid, mods, at, width, weight, out_weight, kept, work, near):
    packed_ref, mixed_ref, lse_ref, branch_ref = kept
    entry_ref, packed_grad_ref, branch_grad_ref = work
    shift, scale, gate = mods[at : at + 1], mods[at + 1 : at + 2], mods[at + 2 : at + 3]
    grad_gate = jnp.sum(grad_out * branch_ref[0].astype(F32), axis=0, keepdims=True)
    grad_branch = (gate * grad_out).astype(BF)
    branch_grad_ref[...] = grad_branch
    grad_mixed = mul_rt(grad_branch, out_weight[...]).astype(BF)
    same = same_patch() if near else None
    lane = lax.broadcasted_iota(jnp.int32, (ROWS, PAIR), 1)
    scaled = half_masks(HEAD_DIM ** (-0.5))
    ones = half_masks(1.0)
    for pair in range(HEADS // 2):
        at_q = pair * PAIR
        query = packed_ref[0, :, at_q : at_q + PAIR]
        keys = packed_ref[0, :, width + at_q : width + at_q + PAIR]
        values = packed_ref[0, :, 2 * width + at_q : 2 * width + at_q + PAIR]
        grads = grad_mixed[:, at_q : at_q + PAIR]
        grad_query = []
        grad_keys = None
        grad_values = None
        for half in range(2):
            head = 2 * pair + half
            own_query = query * scaled[half]
            own_grads = grads * ones[half]
            scores = mul_rt(keys, own_query)
            if near:
                scores = jnp.where(same, scores, -jnp.inf)
            probs = jnp.exp(scores - lse_ref[0, head : head + 1, :])
            grad_probs = mul_rt(values, own_grads)
            inner = jnp.sum(probs * grad_probs, axis=0, keepdims=True)
            grad_scores = (probs * (grad_probs - inner)).astype(BF)
            part_values = mul(probs.astype(BF), own_grads)
            part_keys = mul(grad_scores, own_query)
            grad_query.append(mul_lt(grad_scores, keys))
            grad_keys = part_keys if half == 0 else grad_keys + part_keys
            grad_values = part_values if half == 0 else grad_values + part_values
        joined = jnp.where(lane < HEAD_DIM, grad_query[0], grad_query[1])
        packed_grad_ref[:, at_q : at_q + PAIR] = (joined * HEAD_DIM ** (-0.5)).astype(BF)
        packed_grad_ref[:, width + at_q : width + at_q + PAIR] = grad_keys.astype(BF)
        packed_grad_ref[:, 2 * width + at_q : 2 * width + at_q + PAIR] = (
            grad_values.astype(BF)
        )
    grad_entry = mul_rt(packed_grad_ref[...], weight[...])
    normed, inverse = layer_norm(resid)
    entry_ref[...] = (normed * (1.0 + scale) + shift).astype(BF)
    grad_shift = jnp.sum(grad_entry, axis=0, keepdims=True)
    grad_scale = jnp.sum(grad_entry * normed, axis=0, keepdims=True)
    grad_in = grad_out + norm_back(grad_entry * (1.0 + scale), normed, inverse)
    return grad_in, (grad_shift, grad_scale, grad_gate)


def by_distance(me, grad, out, block, shards):
    rows = grad.shape[0] // shards
    for shard in range(shards):
        distance = jnp.bitwise_xor(me, shard)
        out[jnp.bitwise_and(distance, 1), lax.shift_right_logical(distance, 1), block] = grad[
            shard * rows : (shard + 1) * rows
        ]


def fetch_weights(packed, places, sem):
    copies = []
    for shard in range(packed.shape[0]):
        for block in range(packed.shape[1]):
            copies.append(
                pltpu.make_async_copy(packed.at[shard, block], places(shard, block), sem)
            )
    for copy in copies:
        copy.start()
    for copy in copies:
        copy.wait()


def fetch_pieces(me, pieces, weight, out_weight, sem):
    _, rows, width = pieces[0].shape
    copies = []
    for distance, piece in enumerate(pieces):
        first = pl.multiple_of(jnp.bitwise_xor(me, distance) * rows, rows)
        for block in range(3):
            target = weight.at[pl.ds(first, rows), block * width : (block + 1) * width]
            copies.append(pltpu.make_async_copy(piece.at[block], target, sem))
        copies.append(
            pltpu.make_async_copy(piece.at[3], out_weight.at[pl.ds(first, rows), :], sem)
        )
    for copy in copies:
        copy.start()
    for copy in copies:
        copy.wait()


def mixer_weight_grads(entry, packed_grad, mixed, branch_grad, put, width):
    entry_t = entry[...].T
    for block in range(3):
        put(block, mul(entry_t, packed_grad[:, block * width : (block + 1) * width]).astype(BF))
    put(3, mul(mixed.T, branch_grad[...]).astype(BF))


def add_mods(mods_out, clip, grads):
    for at, grad in enumerate(grads):
        mods_out[clip, at : at + 1, :] += grad


def space_forward_kernel(shards, where, frames_ref, mods_ref, *refs):
    pieces = refs[:shards]
    after_ref, packed_ref, mixed_ref, lse_ref, branch_ref = refs[shards : shards + 5]
    weight, out_weight, sem = refs[shards + 5 :]
    step = pl.program_id(0)
    width = frames_ref.shape[-1]

    @pl.when(step == 0)
    def _():
        fetch_pieces(where[pl.num_programs(0)], pieces, weight, out_weight, sem)

    mods = mods_ref[where[step]]
    after = mixer_forward(
        frames_ref[0], mods, 0, width, weight, out_weight,
        (packed_ref, mixed_ref, lse_ref, branch_ref), False,
    )
    after_ref[...] = after.astype(BF).reshape(after_ref.shape)


def space_backward_kernel(
    shards, where, grad_ref, frames_ref, mods_ref, packed_ref, mixed_ref, lse_ref, branch_ref, *refs
):
    pieces = refs[:shards]
    rows_out, mods_out, grads_out = refs[shards : shards + 3]
    weight, out_weight, entry, packed_grad, mixed, branch_grad, sem = refs[shards + 3 :]
    step = pl.program_id(0)
    width = frames_ref.shape[-1]

    @pl.when(step == 0)
    def _():
        fetch_pieces(where[pl.num_programs(0)], pieces, weight, out_weight, sem)
        mods_out[...] = jnp.zeros_like(mods_out)

    clip = where[step]
    me = where[pl.num_programs(0)]
    own = pl.ds(pl.multiple_of(step * ROWS, ROWS), ROWS)
    grad_out = grad_ref[...].reshape(ROWS, width).astype(F32)
    grad_in, grads = mixer_backward(
        grad_out, frames_ref[0], mods_ref[clip], 0, width, weight, out_weight,
        (packed_ref, mixed_ref, lse_ref, branch_ref),
        (entry.at[own], packed_grad.at[own], branch_grad.at[own]), False,
    )
    rows_out[0] = grad_in
    mixed[own] = mixed_ref[0]
    add_mods(mods_out, clip, grads)

    @pl.when(step == pl.num_programs(0) - 1)
    def _():
        def put(block, grad):
            by_distance(me, grad, grads_out, block, shards)

        mixer_weight_grads(entry, packed_grad, mixed[...], branch_grad, put, width)


def load_near(source, inverse, resid, clip, first, frames):
    for frame in range(frames):
        values = source[inverse[clip * frames + frame], pl.ds(first, NEAR), :]
        resid[frame * NEAR : (frame + 1) * NEAR, :] = values.astype(F32)


def store_near(target, inverse, values, clip, first, frames):
    for frame in range(frames):
        own = values[frame * NEAR : (frame + 1) * NEAR]
        target[inverse[clip * frames + frame], pl.ds(first, NEAR), :] = own.astype(BF)


def block_place(columns):
    step = pl.program_id(0)
    per_clip = columns // NEAR
    clip = step // per_clip
    first = pl.multiple_of((step - clip * per_clip) * NEAR, NEAR)
    return step, clip, first


def time_forward_kernel(frames, shards, inverse, source, mods_ref, *refs):
    pieces = refs[:shards]
    resid_ref, after_ref, packed_ref, mixed_ref, lse_ref, branch_ref = refs[shards : shards + 6]
    weight, out_weight, resid, sem = refs[shards + 6 :]
    step, clip, first = block_place(source.shape[1])
    width = source.shape[-1]

    @pl.when(step == 0)
    def _():
        fetch_pieces(inverse[source.shape[0]], pieces, weight, out_weight, sem)

    load_near(source, inverse, resid, clip, first, frames)
    resid_ref[0] = resid[...].astype(BF)
    after_ref[0] = mixer_forward(
        resid[...], mods_ref[clip], 3, width, weight, out_weight,
        (packed_ref, mixed_ref, lse_ref, branch_ref), True,
    )


def time_backward_kernel(
    frames, shards, inverse, grad_ref, resid_ref, mods_ref, packed_ref, mixed_ref, lse_ref,
    branch_ref, *refs
):
    pieces = refs[:shards]
    going, mods_out, grads_out = refs[shards : shards + 3]
    weight, out_weight, entry, packed_grad, mixed, branch_grad, sem = refs[shards + 3 :]
    step, clip, first = block_place(going.shape[1])
    width = going.shape[-1]

    @pl.when(step == 0)
    def _():
        fetch_pieces(inverse[going.shape[0]], pieces, weight, out_weight, sem)
        mods_out[...] = jnp.zeros_like(mods_out)

    own = pl.ds(pl.multiple_of(step * ROWS, ROWS), ROWS)
    grad_in, grads = mixer_backward(
        grad_ref[0], resid_ref[0].astype(F32), mods_ref[clip], 3, width, weight, out_weight,
        (packed_ref, mixed_ref, lse_ref, branch_ref),
        (entry.at[own], packed_grad.at[own], branch_grad.at[own]), True,
    )
    store_near(going, inverse, grad_in, clip, first, frames)
    mixed[own] = mixed_ref[0]
    add_mods(mods_out, clip, grads)

    @pl.when(step == pl.num_programs(0) - 1)
    def _():
        def put(block, grad):
            grads_out[:, block] = grad.reshape(shards, width // shards, width)

        mixer_weight_grads(entry, packed_grad, mixed[...], branch_grad, put, width)


def feed_kernel(
    frames, inverse, after_ref, source, mods_ref, up_bias, down_bias, packed_w, result, grad_ref,
    mods_out, up_bias_out, down_bias_out, grads_out, up, down, entry, active, grad_up_in,
    grad_down_in, grad_result, staged, sem, out_sem,
):
    step, clip, first = block_place(source.shape[1])
    shards, _, rows, width = packed_w.shape
    hidden = up.shape[1]
    chunks = hidden // width

    @pl.when(step == 0)
    def _():
        def places(shard, block):
            if block < chunks:
                return up.at[
                    shard * rows : (shard + 1) * rows, block * width : (block + 1) * width
                ]
            start = (shard * chunks + block - chunks) * rows
            return down.at[start : start + rows, :]

        fetch_weights(packed_w, places, sem)
        mods_out[...] = jnp.zeros_like(mods_out)
        up_bias_out[...] = jnp.zeros_like(up_bias_out)
        down_bias_out[...] = jnp.zeros_like(down_bias_out)

    own = pl.ds(pl.multiple_of(step * ROWS, ROWS), ROWS)
    mods = mods_ref[clip]
    shift, scale, gate = mods[6:7], mods[7:8], mods[8:9]
    load_near(source, inverse, grad_result, clip, first, frames)
    grad_out = grad_result[...]
    down_in = (gate * grad_out).astype(BF)
    grad_down_in[own] = down_in
    down_bias_out[...] += jnp.sum(down_in.astype(F32), axis=0, keepdims=True)
    resid = after_ref[0]
    normed, inverse_std = layer_norm(resid)
    entered = (normed * (1.0 + scale) + shift).astype(BF)
    entry[own] = entered
    downward = jnp.broadcast_to(down_bias[...], (ROWS, width))
    grad_entry = jnp.zeros((ROWS, width), F32)
    for chunk in range(chunks):
        cols = slice(chunk * width, (chunk + 1) * width)
        upward = mul(entered, up[:, cols]) + up_bias[:, cols]
        below = 0.5 + 0.5 * lax.erf(upward * 2.0 ** (-0.5))
        density = jnp.exp(-0.5 * upward * upward) * 0.3989422804014327
        acted = (upward * below).astype(BF)
        active[own, cols] = acted
        downward = downward + mul(acted, down[cols, :])
        grad_active = mul_rt(down_in, down[cols, :])
        up_in = (grad_active * (below + upward * density)).astype(BF)
        grad_up_in[own, cols] = up_in
        up_bias_out[:, cols] += jnp.sum(up_in.astype(F32), axis=0, keepdims=True)
        grad_entry = grad_entry + mul_rt(up_in, up[:, cols])
    store_near(result, inverse, resid + gate * downward, clip, first, frames)
    grad_gate = jnp.sum(grad_out * downward, axis=0, keepdims=True)
    grad_shift = jnp.sum(grad_entry, axis=0, keepdims=True)
    grad_scale = jnp.sum(grad_entry * normed, axis=0, keepdims=True)
    add_mods(mods_out, clip, (grad_shift, grad_scale, grad_gate))
    grad_ref[0] = grad_out + norm_back(grad_entry * (1.0 + scale), normed, inverse_std)

    @pl.when(step == pl.num_programs(0) - 1)
    def _():
        entry_t = entry[...].T
        copies = []
        for chunk in range(chunks):
            grad = mul(entry_t, grad_up_in[:, chunk * width : (chunk + 1) * width]).astype(BF)
            staged[chunk] = grad.reshape(shards, rows, width)
            copies.append(
                pltpu.make_async_copy(staged.at[chunk], grads_out.at[:, chunk], out_sem.at[chunk])
            )
            copies[-1].start()
        group = shards // chunks
        for chunk in range(chunks):
            grad = mul_lt(active[:, chunk * width : (chunk + 1) * width], grad_down_in[...])
            slot = chunks + chunk
            staged[slot] = grad.astype(BF).reshape(shards, rows, width)
            copies.append(
                pltpu.make_async_copy(
                    staged.at[slot].reshape(group, chunks, rows, width),
                    grads_out.at[chunk * group : (chunk + 1) * group, chunks:],
                    out_sem.at[slot],
                )
            )
            copies[-1].start()
        for copy in copies:
            copy.wait()


def whole(shape):
    return pl.BlockSpec(shape, lambda *_: (0,) * len(shape))


def per_step(shape):
    return pl.BlockSpec((1,) + tuple(shape[1:]), lambda step, *_: (step,) + (0,) * (len(shape) - 1))


ANY = pl.BlockSpec(memory_space=pl.ANY)


def run(kernel, steps, table, ins, in_specs, outs, out_specs, scratch, flops, name):
    size = lambda shaped: shaped.size * shaped.dtype.itemsize
    moved = sum(size(a) for a in ins) + sum(size(a) for a in outs)
    return pl.pallas_call(
        kernel,
        grid_spec=pltpu.PrefetchScalarGridSpec(
            num_scalar_prefetch=1, grid=(steps,), in_specs=in_specs, out_specs=out_specs,
            scratch_shapes=scratch,
        ),
        out_shape=outs,
        compiler_params=pltpu.CompilerParams(
            dimension_semantics=("arbitrary",), vmem_limit_bytes=VMEM_LIMIT
        ),
        cost_estimate=pl.CostEstimate(flops=flops, bytes_accessed=moved, transcendentals=0),
        name=name,
    )(table, *ins)


def body(
    frames_in,
    cotangent,
    time_table,
    ada_weight,
    ada_bias,
    space_qkv,
    space_out,
    time_qkv,
    time_out,
    up_weight,
    up_bias,
    down_weight,
    down_bias,
    timesteps,
    task_mask,
    clip_weight,
    frame_table,
):
    shards = lax.axis_size("shard")
    shard_at = lax.axis_index("shard")
    frame_count, patches, width = frames_in.shape
    clips = timesteps.shape[0]
    frames = task_mask.shape[1]
    table = frame_table[0]
    group_frames = table.shape[0]
    columns = patches // shards
    rows = width // shards
    hidden = up_weight.shape[1]
    chunks = hidden // width
    tokens = group_frames * columns
    steps = tokens // ROWS
    shaped = jax.ShapeDtypeStruct

    def column_blocks(weight):
        return jnp.swapaxes(weight.reshape(rows, -1, width), 0, 1)

    def swap(values, distance):
        pairs = [(at, at ^ distance) for at in range(shards)]
        return lax.ppermute(values, "shard", pairs)

    def gather(packed):
        return lax.all_gather(packed[None], "shard", axis=0, tiled=True)

    groups = lax.axis_size("grp")
    group_at = lax.axis_index("grp")

    def swap_group(values, distance):
        pairs = [(at, at ^ distance) for at in range(groups)]
        return lax.ppermute(values, "grp", pairs)

    def every(values):
        stacked = jnp.zeros((groups,) + values.shape, values.dtype)
        for distance in range(groups):
            piece = swap_group(values, distance) if distance else values
            stacked = lax.dynamic_update_index_in_dim(stacked, piece, group_at ^ distance, 0)
        return stacked

    def shard_sum(values):
        distance = 1
        while distance < shards:
            values = values + swap(values, distance)
            distance *= 2
        return values

    def even_pieces(own):
        return [own] + [swap(own, distance) for distance in range(2, shards, 2)]

    def all_pieces(even):
        pieces = []
        for piece in even:
            pieces += [piece, swap(piece, 1)]
        return pieces

    own_space = jnp.concatenate([column_blocks(space_qkv), space_out[None]], axis=0)
    even = even_pieces(own_space)

    embed = jnp.take(time_table, timesteps, axis=0).astype(F32)
    cond = jax.nn.silu(embed).astype(BF)
    mod_local = jnp.dot(cond, ada_weight, preferred_element_type=F32)

    def spread(local):
        full = jnp.zeros((shards, local.shape[0]), F32)
        return lax.dynamic_update_slice_in_dim(
            full, local.astype(F32)[None], shard_at, 0
        ).reshape(-1)

    small = jnp.concatenate(
        [
            (mod_local + spread(ada_bias)[None]).reshape(-1),
            spread(up_bias),
            spread(down_bias),
        ]
    )
    small = lax.all_gather(small.reshape(1, -1, 128), "shard", axis=0, tiled=True)
    small, even[1] = lax.optimization_barrier((small, even[1]))
    small = jnp.sum(small, axis=0).reshape(-1)
    space_w = all_pieces(even)
    own_time = jnp.concatenate([column_blocks(time_qkv), time_out[None]], axis=0)
    own_feed = jnp.concatenate(
        [column_blocks(up_weight), down_weight.reshape(chunks, rows, width)], axis=0
    )
    own_time, own_feed, *_ = lax.optimization_barrier((own_time, own_feed, *even[1:]))
    time_w = all_pieces(even_pieces(own_time))
    feed_w = gather(own_feed)
    mod_size = clips * 9 * width
    modul = small[:mod_size].reshape(clips, 9, width)
    up_bias_full = small[mod_size:-width].reshape(1, hidden)
    down_bias_full = small[-width:].reshape(1, width)

    slot_ids = shard_at * frame_count + jnp.arange(frame_count, dtype=jnp.int32)
    frame_ids = jnp.take(table, slot_ids)
    clip_of = frame_ids // frames
    frame_of = frame_ids % frames
    where = jnp.concatenate([clip_of, shard_at[None].astype(jnp.int32)])
    slots = jnp.arange(group_frames, dtype=jnp.int32)
    inverse = jnp.sum(jnp.where(table[None, :] == slots[:, None], slots[None, :], 0), axis=1)
    inverse = jnp.concatenate([inverse, shard_at[None].astype(jnp.int32)])

    def exchange(parts):
        return lax.all_to_all(parts, "shard", split_axis=0, concat_axis=0, tiled=True)

    row_weights = task_mask[clip_of, frame_of].astype(F32) * clip_weight[clip_of]
    weighted = (cotangent * row_weights[:, None, None]).astype(BF)
    weighted = jnp.swapaxes(weighted.reshape(frame_count, shards, columns, width), 0, 1)
    arriving = exchange(weighted).reshape(group_frames, columns, width)

    own_shape = (shards, frame_count, columns, width)
    own_spec = pl.BlockSpec((shards, 1, columns, width), lambda step, *_: (0, step, 0, 0))
    mods_spec = whole((clips, 9, width))
    mods_out = shaped((clips, 3, width), F32)
    mods_out_spec = whole((clips, 3, width))
    grads_shape = (shards, 4, rows, width)
    split_shape = (2, shards // 2, 4, rows, width)
    weight_scratch = [
        pltpu.VMEM((width, 3 * width), BF),
        pltpu.VMEM((width, width), BF),
    ]
    dma = pltpu.SemaphoreType.DMA

    def kept(count):
        shapes = [
            shaped((count, ROWS, 3 * width), BF),
            shaped((count, ROWS, width), BF),
            shaped((count, 16, ROWS), F32),
            shaped((count, ROWS, width), BF),
        ]
        return shapes, [per_step(one.shape) for one in shapes]

    def back_scratch(count):
        return [
            pltpu.VMEM((count * ROWS, width), BF),
            pltpu.VMEM((count * ROWS, 3 * width), BF),
            pltpu.VMEM((count * ROWS, width), BF),
            pltpu.VMEM((count * ROWS, width), BF),
        ]

    mixer_flops = 2 * tokens * width * 4 * width + 4 * tokens * ROWS * width * 2
    space_keep, space_keep_specs = kept(frame_count)
    after_space, *space_kept = run(
        partial(space_forward_kernel, shards), frame_count, where,
        [frames_in, modul] + space_w,
        [per_step(frames_in.shape), mods_spec] + [ANY] * shards,
        [shaped(own_shape, BF)] + space_keep,
        [own_spec] + space_keep_specs,
        weight_scratch + [dma(())],
        mixer_flops, "space_forward",
    )
    received = exchange(after_space).reshape(group_frames, columns, width)
    own_ids = jnp.concatenate([embed, timesteps.astype(F32)[:, None]], axis=1)
    own_ids, _ = lax.optimization_barrier((own_ids, after_space))
    every_ids = every(own_ids).reshape(-1, own_ids.shape[1])

    cols_spec = whole((group_frames, columns, width))
    cols_shape = shaped((group_frames, columns, width), BF)
    block_shape = (steps, ROWS, width)
    time_keep, time_keep_specs = kept(steps)
    time_resid, after_time, *time_kept = run(
        partial(time_forward_kernel, frames, shards), steps, inverse,
        [received, modul] + time_w,
        [cols_spec, mods_spec] + [ANY] * shards,
        [shaped(block_shape, BF), shaped(block_shape, F32)] + time_keep,
        [per_step(block_shape)] * 2 + time_keep_specs,
        weight_scratch + [pltpu.VMEM((ROWS, width), F32), dma(())],
        mixer_flops, "time_forward",
    )

    result, grad_after_time, mlp_mods, grad_up_bias, grad_down_bias, feed_grads = run(
        partial(feed_kernel, frames), steps, inverse,
        [after_time, arriving, modul, up_bias_full, down_bias_full, feed_w],
        [per_step(block_shape), cols_spec, mods_spec, whole((1, hidden)), whole((1, width)), ANY],
        [
            cols_shape,
            shaped(block_shape, F32),
            mods_out,
            shaped((1, hidden), F32),
            shaped((1, width), F32),
            shaped((shards, 2 * chunks, rows, width), BF),
        ],
        [
            cols_spec, per_step(block_shape), mods_out_spec, whole((1, hidden)),
            whole((1, width)), ANY,
        ],
        [
            pltpu.VMEM((width, hidden), BF),
            pltpu.VMEM((hidden, width), BF),
            pltpu.VMEM((tokens, width), BF),
            pltpu.VMEM((tokens, hidden), BF),
            pltpu.VMEM((tokens, hidden), BF),
            pltpu.VMEM((tokens, width), BF),
            pltpu.VMEM((ROWS, width), F32),
            pltpu.VMEM((2 * chunks, shards, rows, width), BF),
            dma(()),
            dma((2 * chunks,)),
        ],
        6 * 2 * tokens * width * hidden, "feed",
    )

    def to_rows(moved):
        moved = jnp.swapaxes(moved.reshape(own_shape), 0, 1)
        return moved.reshape(frame_count, patches, width).astype(F32)

    def shard_total(packed):
        return lax.psum_scatter(packed, "shard", scatter_dimension=0, tiled=True)[0]

    def parts_of(share):
        parts = share.reshape(groups, -1, width)

        def part(at):
            return lax.dynamic_index_in_dim(parts, at, 0, keepdims=False)

        return [part(group_at)] + [
            swap_group(part(group_at ^ distance), distance) for distance in range(1, groups)
        ]

    def spread_parts(parts, share):
        own = parts[0].astype(F32)
        for piece in parts[1:]:
            own = own + piece.astype(F32)
        own = own.astype(BF)
        near = [own] + [swap_group(own, distance) for distance in range(1, groups)]
        step = 1
        while step < groups:
            odd = jnp.bitwise_and(group_at, step) > 0
            near = [jnp.where(odd, near[at ^ step], near[at]) for at in range(groups)]
            step *= 2
        return jnp.concatenate(near).reshape(share.shape).astype(F32)

    def total(share):
        return spread_parts(parts_of(share), share)

    def halving(values, bits):
        left = [bit for bit in range(shards.bit_length() - 2)]
        blocks = values.shape[1:]
        values = values.reshape((2,) * len(left) + blocks)
        for bit in bits:
            axis = len(left) - 1 - left.index(bit)
            kept, sent = (lax.index_in_dim(values, side, axis, keepdims=False) for side in (0, 1))
            values = (kept.astype(F32) + swap(sent, 2 << bit).astype(F32)).astype(BF)
            left.remove(bit)
        return values

    def near_total(grads):
        return (grads[0].astype(F32) + swap(grads[1], 1).astype(F32)).astype(BF)

    def far_total(kept):
        bits = list(range(shards.bit_length() - 2))
        half = kept.shape[1] // 2
        return jnp.concatenate(
            [halving(kept[:, :half], bits), halving(kept[:, half:], bits[::-1])], axis=0
        )

    feed_share = shard_total(feed_grads)

    going, time_mods, time_grads = run(
        partial(time_backward_kernel, frames, shards), steps, inverse,
        [grad_after_time, time_resid, modul] + time_kept + time_w,
        [per_step(block_shape)] * 2 + [mods_spec] + time_keep_specs + [ANY] * shards,
        [cols_shape, mods_out, shaped(grads_shape, BF)],
        [cols_spec, mods_out_spec, whole(grads_shape)],
        weight_scratch + back_scratch(steps) + [dma(())],
        3 * mixer_flops, "time_backward",
    )
    grad_space = exchange(going.reshape(own_shape))
    time_grads, feed_share, grad_space, result = lax.optimization_barrier(
        (time_grads, feed_share, grad_space, result)
    )
    time_share = shard_total(time_grads)
    feed_parts = parts_of(feed_share)
    arrived = exchange(result.reshape(own_shape))
    grad_rows, space_mods, space_grads = run(
        partial(space_backward_kernel, shards), frame_count, where,
        [grad_space, frames_in, modul] + space_kept + space_w,
        [own_spec, per_step(frames_in.shape), mods_spec] + space_keep_specs + [ANY] * shards,
        [shaped(frames_in.shape, F32), mods_out, shaped(split_shape, BF)],
        [per_step(frames_in.shape), mods_out_spec, whole(split_shape)],
        weight_scratch + back_scratch(frame_count) + [dma(())],
        3 * mixer_flops, "space_backward",
    )
    space_grads, space_mods, arrived, *feed_parts = lax.optimization_barrier(
        (space_grads, space_mods, arrived, *feed_parts)
    )
    space_near = near_total(space_grads)
    feed_share = spread_parts(feed_parts, feed_share)
    frames_out = to_rows(arrived)
    space_near, time_share = lax.optimization_barrier((space_near, time_share))
    space_share = far_total(space_near)
    time_share = total(time_share)
    space_share = total(space_share)

    mod_part = jnp.concatenate([space_mods, time_mods, mlp_mods], axis=1)
    small_grads = jnp.concatenate(
        [mod_part.reshape(-1), grad_up_bias.reshape(-1), grad_down_bias.reshape(-1)]
    )
    small_grads = shard_sum(small_grads.reshape(-1, 128)).reshape(-1)
    up_dev = up_bias.shape[0]
    down_dev = down_bias.shape[0]
    bias_dev = ada_bias.shape[0]
    small_grads = jnp.concatenate(
        [
            small_grads[:mod_size],
            lax.dynamic_slice_in_dim(small_grads, mod_size + shard_at * up_dev, up_dev, 0),
            lax.dynamic_slice_in_dim(
                small_grads, mod_size + shards * up_dev + shard_at * down_dev, down_dev, 0
            ),
        ]
    )
    small_size = small_grads.shape[0]
    small_grads = jnp.pad(small_grads, (0, -small_size % 1024)).reshape(1, -1, 128)
    every_small = every(small_grads).reshape(groups, -1)
    every_modul = every_small[:, :mod_size].reshape(groups * clips, 9 * width).astype(BF)
    bias_sums = jnp.sum(every_small[:, mod_size:small_size], axis=0)
    every_embed = every_ids[:, :-1]
    every_steps = every_ids[:, -1].astype(jnp.int32)
    every_cond = jax.nn.silu(every_embed).astype(BF)
    grad_ada = jnp.einsum("cd,cj->dj", every_cond, every_modul, preferred_element_type=F32)
    grad_ada_bias = lax.dynamic_slice_in_dim(
        jnp.sum(every_modul.astype(F32), axis=0), shard_at * bias_dev, bias_dev, 0
    )
    grad_cond = jnp.einsum("cj,dj->cd", every_modul, ada_weight, preferred_element_type=F32)
    _, silu_back = jax.vjp(jax.nn.silu, every_embed)
    grad_embed = silu_back(grad_cond)[0]
    vocab = time_table.shape[0]
    onehot = (jnp.arange(vocab, dtype=jnp.int32)[:, None] == every_steps[None, :]).astype(F32)
    grad_table = jnp.dot(onehot, grad_embed, precision=HIGH)

    def rows_of(blocks):
        return jnp.swapaxes(blocks, 0, 1).reshape(rows, -1)

    return (
        frames_out,
        grad_rows,
        grad_table,
        grad_ada,
        grad_ada_bias,
        rows_of(space_share[:3]),
        space_share[3],
        rows_of(time_share[:3]),
        time_share[3],
        rows_of(feed_share[:chunks]),
        bias_sums[:up_dev],
        feed_share[chunks:].reshape(chunks * rows, width),
        bias_sums[up_dev:],
    )


def solution(mesh):
    placed = (
        P(("grp", "shard"), None, None),
        P(("grp", "shard"), None, None),
        P(None, "shard"),
        P("shard", None),
        P("shard"),
        P("shard", None),
        P("shard", None),
        P("shard", None),
        P("shard", None),
        P("shard", None),
        P("shard"),
        P("shard", None),
        P("shard"),
        P("grp"),
        P("grp", None),
        P("grp"),
        P("grp", None),
    )
    return jax.shard_map(
        body,
        mesh=mesh,
        in_specs=placed,
        out_specs=(
            P(("grp", "shard"), None, None),
            P(("grp", "shard"), None, None),
            P(None, "shard"),
            P("shard", None),
            P("shard"),
            P("shard", None),
            P("shard", None),
            P("shard", None),
            P("shard", None),
            P("shard", None),
            P("shard"),
            P("shard", None),
            P("shard"),
        ),
        check_vma=False,
    )
```

```python
from functools import partial

import jax
import jax.numpy as jnp
from jax import lax
from jax.experimental import pallas as pl
from jax.experimental.pallas import tpu as pltpu
from jax.sharding import PartitionSpec as P

HEADS = 12
HEAD_DIM = 64
PAIR = 2 * HEAD_DIM
ROWS = 256
NEAR = 16
HIGH = lax.Precision.HIGHEST
EPSILON = 1e-06
BF = jnp.bfloat16
F32 = jnp.float32
VMEM_LIMIT = 60 * 1024 * 1024


def layer_norm(values):
    center = values - jnp.mean(values, axis=-1, keepdims=True)
    spread = jnp.mean(center * center, axis=-1, keepdims=True)
    inverse = lax.rsqrt(spread + EPSILON)
    return (center * inverse, inverse)


def norm_back(grad_normed, normed, inverse):
    first = jnp.mean(grad_normed, axis=-1, keepdims=True)
    second = jnp.mean(grad_normed * normed, axis=-1, keepdims=True)
    return inverse * (grad_normed - first - normed * second)


def mul(left, right):
    return jnp.dot(left, right, preferred_element_type=F32)


def mul_rt(left, right):
    return lax.dot_general(left, right, (((1,), (1,)), ((), ())), preferred_element_type=F32)


def mul_lt(left, right):
    return lax.dot_general(left, right, (((0,), (0,)), ((), ())), preferred_element_type=F32)


def half_masks(value):
    lane = lax.broadcasted_iota(jnp.int32, (1, PAIR), 1)
    low = jnp.where(lane < HEAD_DIM, value, 0.0)
    return (low.astype(BF), (value - low).astype(BF))


def same_patch():
    rows = lax.broadcasted_iota(jnp.int32, (ROWS, ROWS), 0)
    cols = lax.broadcasted_iota(jnp.int32, (ROWS, ROWS), 1)
    return jnp.bitwise_and(rows, NEAR - 1) == jnp.bitwise_and(cols, NEAR - 1)


def mixer_forward(resid, mods, at, width, weight, out_weight, keep, near):
    packed_ref, mixed_ref, lse_ref, branch_ref = keep
    shift, scale, gate = mods[at : at + 1], mods[at + 1 : at + 2], mods[at + 2 : at + 3]
    normed, _ = layer_norm(resid)
    entry = (normed * (1.0 + scale) + shift).astype(BF)
    for part in range(3):
        packed_ref[0, :, part * width : (part + 1) * width] = mul(
            entry, weight[:, part * width : (part + 1) * width]
        ).astype(BF)
    same = same_patch() if near else None
    lane = lax.broadcasted_iota(jnp.int32, (ROWS, PAIR), 1)
    scaled = half_masks(HEAD_DIM ** (-0.5))
    for pair in range(HEADS // 2):
        at_q = pair * PAIR
        query = packed_ref[0, :, at_q : at_q + PAIR]
        keys = packed_ref[0, :, width + at_q : width + at_q + PAIR]
        values = packed_ref[0, :, 2 * width + at_q : 2 * width + at_q + PAIR]
        halves = []
        for half in range(2):
            scores = mul_rt(keys, query * scaled[half])
            if near:
                scores = jnp.where(same, scores, -jnp.inf)
            highest = jnp.max(scores, axis=0, keepdims=True)
            weights = jnp.exp(scores - highest)
            total = jnp.sum(weights, axis=0, keepdims=True)
            head = 2 * pair + half
            lse_ref[0, head : head + 1, :] = highest + jnp.log(total)
            probs = (weights * (1.0 / total)).astype(BF)
            halves.append(mul_lt(probs, values))
        mixed_ref[0, :, at_q : at_q + PAIR] = jnp.where(
            lane < HEAD_DIM, halves[0], halves[1]
        ).astype(BF)
    branch = mul(mixed_ref[0], out_weight[...])
    branch_ref[0] = branch.astype(BF)
    return resid + gate * branch


def mixer_backward(grad_out, resid, mods, at, width, weight, out_weight, kept, work, near):
    packed_ref, mixed_ref, lse_ref, branch_ref = kept
    entry_ref, packed_grad_ref, branch_grad_ref = work
    shift, scale, gate = mods[at : at + 1], mods[at + 1 : at + 2], mods[at + 2 : at + 3]
    grad_gate = jnp.sum(grad_out * branch_ref[0].astype(F32), axis=0, keepdims=True)
    grad_branch = (gate * grad_out).astype(BF)
    branch_grad_ref[...] = grad_branch
    grad_mixed = mul_rt(grad_branch, out_weight[...]).astype(BF)
    same = same_patch() if near else None
    lane = lax.broadcasted_iota(jnp.int32, (ROWS, PAIR), 1)
    scaled = half_masks(HEAD_DIM ** (-0.5))
    ones = half_masks(1.0)
    for pair in range(HEADS // 2):
        at_q = pair * PAIR
        query = packed_ref[0, :, at_q : at_q + PAIR]
        keys = packed_ref[0, :, width + at_q : width + at_q + PAIR]
        values = packed_ref[0, :, 2 * width + at_q : 2 * width + at_q + PAIR]
        grads = grad_mixed[:, at_q : at_q + PAIR]
        grad_query = []
        grad_keys = None
        grad_values = None
        for half in range(2):
            head = 2 * pair + half
            own_query = query * scaled[half]
            own_grads = grads * ones[half]
            scores = mul_rt(keys, own_query)
            if near:
                scores = jnp.where(same, scores, -jnp.inf)
            probs = jnp.exp(scores - lse_ref[0, head : head + 1, :])
            grad_probs = mul_rt(values, own_grads)
            inner = jnp.sum(probs * grad_probs, axis=0, keepdims=True)
            grad_scores = (probs * (grad_probs - inner)).astype(BF)
            part_values = mul(probs.astype(BF), own_grads)
            part_keys = mul(grad_scores, own_query)
            grad_query.append(mul_lt(grad_scores, keys))
            grad_keys = part_keys if half == 0 else grad_keys + part_keys
            grad_values = part_values if half == 0 else grad_values + part_values
        joined = jnp.where(lane < HEAD_DIM, grad_query[0], grad_query[1])
        packed_grad_ref[:, at_q : at_q + PAIR] = (joined * HEAD_DIM ** (-0.5)).astype(BF)
        packed_grad_ref[:, width + at_q : width + at_q + PAIR] = grad_keys.astype(BF)
        packed_grad_ref[:, 2 * width + at_q : 2 * width + at_q + PAIR] = (
            grad_values.astype(BF)
        )
    grad_entry = mul_rt(packed_grad_ref[...], weight[...])
    normed, inverse = layer_norm(resid)
    entry_ref[...] = (normed * (1.0 + scale) + shift).astype(BF)
    grad_shift = jnp.sum(grad_entry, axis=0, keepdims=True)
    grad_scale = jnp.sum(grad_entry * normed, axis=0, keepdims=True)
    grad_in = grad_out + norm_back(grad_entry * (1.0 + scale), normed, inverse)
    return grad_in, (grad_shift, grad_scale, grad_gate)


def by_distance(me, grad, out, block, shards):
    rows = grad.shape[0] // shards
    for shard in range(shards):
        distance = jnp.bitwise_xor(me, shard)
        out[jnp.bitwise_and(distance, 1), lax.shift_right_logical(distance, 1), block] = grad[
            shard * rows : (shard + 1) * rows
        ]


def fetch_weights(packed, places, sem):
    copies = []
    for shard in range(packed.shape[0]):
        for block in range(packed.shape[1]):
            copies.append(
                pltpu.make_async_copy(packed.at[shard, block], places(shard, block), sem)
            )
    for copy in copies:
        copy.start()
    for copy in copies:
        copy.wait()


def fetch_pieces(me, pieces, weight, out_weight, sem):
    _, rows, width = pieces[0].shape
    copies = []
    for distance, piece in enumerate(pieces):
        first = pl.multiple_of(jnp.bitwise_xor(me, distance) * rows, rows)
        for block in range(3):
            target = weight.at[pl.ds(first, rows), block * width : (block + 1) * width]
            copies.append(pltpu.make_async_copy(piece.at[block], target, sem))
        copies.append(
            pltpu.make_async_copy(piece.at[3], out_weight.at[pl.ds(first, rows), :], sem)
        )
    for copy in copies:
        copy.start()
    for copy in copies:
        copy.wait()


def mixer_weight_grads(entry, packed_grad, mixed, branch_grad, put, width):
    entry_t = entry[...].T
    for block in range(3):
        put(block, mul(entry_t, packed_grad[:, block * width : (block + 1) * width]).astype(BF))
    put(3, mul(mixed.T, branch_grad[...]).astype(BF))


def add_mods(mods_out, clip, grads):
    for at, grad in enumerate(grads):
        mods_out[clip, at : at + 1, :] += grad


def space_forward_kernel(shards, where, frames_ref, mods_ref, *refs):
    pieces = refs[:shards]
    after_ref, packed_ref, mixed_ref, lse_ref, branch_ref = refs[shards : shards + 5]
    weight, out_weight, sem = refs[shards + 5 :]
    step = pl.program_id(0)
    width = frames_ref.shape[-1]

    @pl.when(step == 0)
    def _():
        fetch_pieces(where[pl.num_programs(0)], pieces, weight, out_weight, sem)

    mods = mods_ref[where[step]]
    after = mixer_forward(
        frames_ref[0], mods, 0, width, weight, out_weight,
        (packed_ref, mixed_ref, lse_ref, branch_ref), False,
    )
    after_ref[...] = after.astype(BF).reshape(after_ref.shape)


def space_backward_kernel(
    shards, where, grad_ref, frames_ref, mods_ref, packed_ref, mixed_ref, lse_ref, branch_ref, *refs
):
    pieces = refs[:shards]
    rows_out, mods_out, grads_out = refs[shards : shards + 3]
    weight, out_weight, entry, packed_grad, mixed, branch_grad, sem = refs[shards + 3 :]
    step = pl.program_id(0)
    width = frames_ref.shape[-1]

    @pl.when(step == 0)
    def _():
        fetch_pieces(where[pl.num_programs(0)], pieces, weight, out_weight, sem)
        mods_out[...] = jnp.zeros_like(mods_out)

    clip = where[step]
    me = where[pl.num_programs(0)]
    own = pl.ds(pl.multiple_of(step * ROWS, ROWS), ROWS)
    grad_out = grad_ref[...].reshape(ROWS, width).astype(F32)
    grad_in, grads = mixer_backward(
        grad_out, frames_ref[0], mods_ref[clip], 0, width, weight, out_weight,
        (packed_ref, mixed_ref, lse_ref, branch_ref),
        (entry.at[own], packed_grad.at[own], branch_grad.at[own]), False,
    )
    rows_out[0] = grad_in
    mixed[own] = mixed_ref[0]
    add_mods(mods_out, clip, grads)

    @pl.when(step == pl.num_programs(0) - 1)
    def _():
        def put(block, grad):
            by_distance(me, grad, grads_out, block, shards)

        mixer_weight_grads(entry, packed_grad, mixed[...], branch_grad, put, width)


def load_near(source, inverse, resid, clip, first, frames):
    for frame in range(frames):
        values = source[inverse[clip * frames + frame], pl.ds(first, NEAR), :]
        resid[frame * NEAR : (frame + 1) * NEAR, :] = values.astype(F32)


def store_near(target, inverse, values, clip, first, frames):
    for frame in range(frames):
        own = values[frame * NEAR : (frame + 1) * NEAR]
        target[inverse[clip * frames + frame], pl.ds(first, NEAR), :] = own.astype(BF)


def block_place(columns):
    step = pl.program_id(0)
    per_clip = columns // NEAR
    clip = step // per_clip
    first = pl.multiple_of((step - clip * per_clip) * NEAR, NEAR)
    return step, clip, first


def time_forward_kernel(frames, shards, inverse, source, mods_ref, *refs):
    pieces = refs[:shards]
    resid_ref, after_ref, packed_ref, mixed_ref, lse_ref, branch_ref = refs[shards : shards + 6]
    weight, out_weight, resid, sem = refs[shards + 6 :]
    step, clip, first = block_place(source.shape[1])
    width = source.shape[-1]

    @pl.when(step == 0)
    def _():
        fetch_pieces(inverse[source.shape[0]], pieces, weight, out_weight, sem)

    load_near(source, inverse, resid, clip, first, frames)
    resid_ref[0] = resid[...].astype(BF)
    after_ref[0] = mixer_forward(
        resid[...], mods_ref[clip], 3, width, weight, out_weight,
        (packed_ref, mixed_ref, lse_ref, branch_ref), True,
    )


def time_backward_kernel(
    frames, shards, inverse, grad_ref, resid_ref, mods_ref, packed_ref, mixed_ref, lse_ref,
    branch_ref, *refs
):
    pieces = refs[:shards]
    going, mods_out, grads_out = refs[shards : shards + 3]
    weight, out_weight, entry, packed_grad, mixed, branch_grad, sem = refs[shards + 3 :]
    step, clip, first = block_place(going.shape[1])
    width = going.shape[-1]

    @pl.when(step == 0)
    def _():
        fetch_pieces(inverse[going.shape[0]], pieces, weight, out_weight, sem)
        mods_out[...] = jnp.zeros_like(mods_out)

    own = pl.ds(pl.multiple_of(step * ROWS, ROWS), ROWS)
    grad_in, grads = mixer_backward(
        grad_ref[0], resid_ref[0].astype(F32), mods_ref[clip], 3, width, weight, out_weight,
        (packed_ref, mixed_ref, lse_ref, branch_ref),
        (entry.at[own], packed_grad.at[own], branch_grad.at[own]), True,
    )
    store_near(going, inverse, grad_in, clip, first, frames)
    mixed[own] = mixed_ref[0]
    add_mods(mods_out, clip, grads)

    @pl.when(step == pl.num_programs(0) - 1)
    def _():
        def put(block, grad):
            grads_out[:, block] = grad.reshape(shards, width // shards, width)

        mixer_weight_grads(entry, packed_grad, mixed[...], branch_grad, put, width)


def feed_kernel(
    frames, inverse, after_ref, source, mods_ref, up_bias, down_bias, packed_w, result, grad_ref,
    mods_out, up_bias_out, down_bias_out, up_out, down_out, up, down, entry, active, grad_up_in,
    grad_down_in, grad_result, staged, sem, out_sem,
):
    step, clip, first = block_place(source.shape[1])
    shards, _, rows, width = packed_w.shape
    hidden = up.shape[1]
    chunks = hidden // width

    @pl.when(step == 0)
    def _():
        def places(shard, block):
            if block < chunks:
                return up.at[
                    shard * rows : (shard + 1) * rows, block * width : (block + 1) * width
                ]
            start = (shard * chunks + block - chunks) * rows
            return down.at[start : start + rows, :]

        fetch_weights(packed_w, places, sem)
        mods_out[...] = jnp.zeros_like(mods_out)
        up_bias_out[...] = jnp.zeros_like(up_bias_out)
        down_bias_out[...] = jnp.zeros_like(down_bias_out)

    own = pl.ds(pl.multiple_of(step * ROWS, ROWS), ROWS)
    mods = mods_ref[clip]
    shift, scale, gate = mods[6:7], mods[7:8], mods[8:9]
    load_near(source, inverse, grad_result, clip, first, frames)
    grad_out = grad_result[...]
    down_in = (gate * grad_out).astype(BF)
    grad_down_in[own] = down_in
    down_bias_out[...] += jnp.sum(down_in.astype(F32), axis=0, keepdims=True)
    resid = after_ref[0]
    normed, inverse_std = layer_norm(resid)
    entered = (normed * (1.0 + scale) + shift).astype(BF)
    entry[own] = entered
    downward = jnp.broadcast_to(down_bias[...], (ROWS, width))
    grad_entry = jnp.zeros((ROWS, width), F32)
    for chunk in range(chunks):
        cols = slice(chunk * width, (chunk + 1) * width)
        upward = mul(entered, up[:, cols]) + up_bias[:, cols]
        below = 0.5 + 0.5 * lax.erf(upward * 2.0 ** (-0.5))
        density = jnp.exp(-0.5 * upward * upward) * 0.3989422804014327
        acted = (upward * below).astype(BF)
        active[own, cols] = acted
        downward = downward + mul(acted, down[cols, :])
        grad_active = mul_rt(down_in, down[cols, :])
        up_in = (grad_active * (below + upward * density)).astype(BF)
        grad_up_in[own, cols] = up_in
        up_bias_out[:, cols] += jnp.sum(up_in.astype(F32), axis=0, keepdims=True)
        grad_entry = grad_entry + mul_rt(up_in, up[:, cols])
    store_near(result, inverse, resid + gate * downward, clip, first, frames)
    grad_gate = jnp.sum(grad_out * downward, axis=0, keepdims=True)
    grad_shift = jnp.sum(grad_entry, axis=0, keepdims=True)
    grad_scale = jnp.sum(grad_entry * normed, axis=0, keepdims=True)
    add_mods(mods_out, clip, (grad_shift, grad_scale, grad_gate))
    grad_ref[0] = grad_out + norm_back(grad_entry * (1.0 + scale), normed, inverse_std)

    @pl.when(step == pl.num_programs(0) - 1)
    def _():
        entry_t = entry[...].T
        copies = []
        for chunk in range(chunks):
            grad = mul(entry_t, grad_up_in[:, chunk * width : (chunk + 1) * width]).astype(BF)
            staged[chunk] = grad.reshape(shards, rows, width)
            copies.append(
                pltpu.make_async_copy(staged.at[chunk], up_out.at[:, chunk], out_sem.at[chunk])
            )
            copies[-1].start()
        group = shards // chunks
        me = inverse[source.shape[0]]
        for chunk in range(chunks):
            grad = mul_lt(active[:, chunk * width : (chunk + 1) * width], grad_down_in[...])
            slot = chunks + chunk
            staged[slot] = grad.astype(BF).reshape(shards, rows, width)
            for part in range(group):
                shard = chunk * group + part
                distance = jnp.bitwise_xor(me, shard)
                place = jnp.bitwise_and(distance, 1), lax.shift_right_logical(distance, 1)
                copies.append(
                    pltpu.make_async_copy(
                        staged.at[slot, part * chunks : (part + 1) * chunks],
                        down_out.at[place],
                        out_sem.at[chunks + shard],
                    )
                )
                copies[-1].start()
        for copy in copies:
            copy.wait()


def whole(shape):
    return pl.BlockSpec(shape, lambda *_: (0,) * len(shape))


def per_step(shape):
    return pl.BlockSpec((1,) + tuple(shape[1:]), lambda step, *_: (step,) + (0,) * (len(shape) - 1))


ANY = pl.BlockSpec(memory_space=pl.ANY)


def run(kernel, steps, table, ins, in_specs, outs, out_specs, scratch, flops, name):
    size = lambda shaped: shaped.size * shaped.dtype.itemsize
    moved = sum(size(a) for a in ins) + sum(size(a) for a in outs)
    return pl.pallas_call(
        kernel,
        grid_spec=pltpu.PrefetchScalarGridSpec(
            num_scalar_prefetch=1, grid=(steps,), in_specs=in_specs, out_specs=out_specs,
            scratch_shapes=scratch,
        ),
        out_shape=outs,
        compiler_params=pltpu.CompilerParams(
            dimension_semantics=("arbitrary",), vmem_limit_bytes=VMEM_LIMIT
        ),
        cost_estimate=pl.CostEstimate(flops=flops, bytes_accessed=moved, transcendentals=0),
        name=name,
    )(table, *ins)


def body(
    frames_in,
    cotangent,
    time_table,
    ada_weight,
    ada_bias,
    space_qkv,
    space_out,
    time_qkv,
    time_out,
    up_weight,
    up_bias,
    down_weight,
    down_bias,
    timesteps,
    task_mask,
    clip_weight,
    frame_table,
):
    shards = lax.axis_size("shard")
    shard_at = lax.axis_index("shard")
    frame_count, patches, width = frames_in.shape
    clips = timesteps.shape[0]
    frames = task_mask.shape[1]
    table = frame_table[0]
    group_frames = table.shape[0]
    columns = patches // shards
    rows = width // shards
    hidden = up_weight.shape[1]
    chunks = hidden // width
    tokens = group_frames * columns
    steps = tokens // ROWS
    shaped = jax.ShapeDtypeStruct

    def column_blocks(weight):
        return jnp.swapaxes(weight.reshape(rows, -1, width), 0, 1)

    def swap(values, distance):
        pairs = [(at, at ^ distance) for at in range(shards)]
        return lax.ppermute(values, "shard", pairs)

    def gather(packed):
        return lax.all_gather(packed[None], "shard", axis=0, tiled=True)

    groups = lax.axis_size("grp")
    group_at = lax.axis_index("grp")

    def swap_group(values, distance):
        pairs = [(at, at ^ distance) for at in range(groups)]
        return lax.ppermute(values, "grp", pairs)

    def every(values):
        stacked = jnp.zeros((groups,) + values.shape, values.dtype)
        for distance in range(groups):
            piece = swap_group(values, distance) if distance else values
            stacked = lax.dynamic_update_index_in_dim(stacked, piece, group_at ^ distance, 0)
        return stacked

    def shard_sum(values):
        distance = 1
        while distance < shards:
            values = values + swap(values, distance)
            distance *= 2
        return values

    def even_pieces(own):
        return [own] + [swap(own, distance) for distance in range(2, shards, 2)]

    def all_pieces(even):
        pieces = []
        for piece in even:
            pieces += [piece, swap(piece, 1)]
        return pieces

    own_space = jnp.concatenate([column_blocks(space_qkv), space_out[None]], axis=0)
    even = even_pieces(own_space)

    embed = jnp.take(time_table, timesteps, axis=0).astype(F32)
    cond = jax.nn.silu(embed).astype(BF)
    mod_local = jnp.dot(cond, ada_weight, preferred_element_type=F32)

    def spread(local):
        full = jnp.zeros((shards, local.shape[0]), F32)
        return lax.dynamic_update_slice_in_dim(
            full, local.astype(F32)[None], shard_at, 0
        ).reshape(-1)

    small = jnp.concatenate(
        [
            (mod_local + spread(ada_bias)[None]).reshape(-1),
            spread(up_bias),
            spread(down_bias),
        ]
    )
    small = lax.all_gather(small.reshape(1, -1, 128), "shard", axis=0, tiled=True)
    small, even[1] = lax.optimization_barrier((small, even[1]))
    small = jnp.sum(small, axis=0).reshape(-1)
    space_w = all_pieces(even)
    own_time = jnp.concatenate([column_blocks(time_qkv), time_out[None]], axis=0)
    own_feed = jnp.concatenate(
        [column_blocks(up_weight), down_weight.reshape(chunks, rows, width)], axis=0
    )
    own_time, own_feed, *_ = lax.optimization_barrier((own_time, own_feed, *even[1:]))
    time_w = all_pieces(even_pieces(own_time))
    feed_w = gather(own_feed)
    mod_size = clips * 9 * width
    modul = small[:mod_size].reshape(clips, 9, width)
    up_bias_full = small[mod_size:-width].reshape(1, hidden)
    down_bias_full = small[-width:].reshape(1, width)

    slot_ids = shard_at * frame_count + jnp.arange(frame_count, dtype=jnp.int32)
    frame_ids = jnp.take(table, slot_ids)
    clip_of = frame_ids // frames
    frame_of = frame_ids % frames
    where = jnp.concatenate([clip_of, shard_at[None].astype(jnp.int32)])
    slots = jnp.arange(group_frames, dtype=jnp.int32)
    inverse = jnp.sum(jnp.where(table[None, :] == slots[:, None], slots[None, :], 0), axis=1)
    inverse = jnp.concatenate([inverse, shard_at[None].astype(jnp.int32)])

    def exchange(parts):
        return lax.all_to_all(parts, "shard", split_axis=0, concat_axis=0, tiled=True)

    row_weights = task_mask[clip_of, frame_of].astype(F32) * clip_weight[clip_of]
    weighted = (cotangent * row_weights[:, None, None]).astype(BF)
    weighted = jnp.swapaxes(weighted.reshape(frame_count, shards, columns, width), 0, 1)
    arriving = exchange(weighted).reshape(group_frames, columns, width)

    own_shape = (shards, frame_count, columns, width)
    own_spec = pl.BlockSpec((shards, 1, columns, width), lambda step, *_: (0, step, 0, 0))
    mods_spec = whole((clips, 9, width))
    mods_out = shaped((clips, 3, width), F32)
    mods_out_spec = whole((clips, 3, width))
    grads_shape = (shards, 4, rows, width)
    split_shape = (2, shards // 2, 4, rows, width)
    weight_scratch = [
        pltpu.VMEM((width, 3 * width), BF),
        pltpu.VMEM((width, width), BF),
    ]
    dma = pltpu.SemaphoreType.DMA

    def kept(count):
        shapes = [
            shaped((count, ROWS, 3 * width), BF),
            shaped((count, ROWS, width), BF),
            shaped((count, 16, ROWS), F32),
            shaped((count, ROWS, width), BF),
        ]
        return shapes, [per_step(one.shape) for one in shapes]

    def back_scratch(count):
        return [
            pltpu.VMEM((count * ROWS, width), BF),
            pltpu.VMEM((count * ROWS, 3 * width), BF),
            pltpu.VMEM((count * ROWS, width), BF),
            pltpu.VMEM((count * ROWS, width), BF),
        ]

    mixer_flops = 2 * tokens * width * 4 * width + 4 * tokens * ROWS * width * 2
    space_keep, space_keep_specs = kept(frame_count)
    after_space, *space_kept = run(
        partial(space_forward_kernel, shards), frame_count, where,
        [frames_in, modul] + space_w,
        [per_step(frames_in.shape), mods_spec] + [ANY] * shards,
        [shaped(own_shape, BF)] + space_keep,
        [own_spec] + space_keep_specs,
        weight_scratch + [dma(())],
        mixer_flops, "space_forward",
    )
    received = exchange(after_space).reshape(group_frames, columns, width)
    own_ids = jnp.concatenate([embed, timesteps.astype(F32)[:, None]], axis=1)
    own_ids, _ = lax.optimization_barrier((own_ids, after_space))
    every_ids = every(own_ids).reshape(-1, own_ids.shape[1])

    cols_spec = whole((group_frames, columns, width))
    cols_shape = shaped((group_frames, columns, width), BF)
    block_shape = (steps, ROWS, width)
    time_keep, time_keep_specs = kept(steps)
    time_resid, after_time, *time_kept = run(
        partial(time_forward_kernel, frames, shards), steps, inverse,
        [received, modul] + time_w,
        [cols_spec, mods_spec] + [ANY] * shards,
        [shaped(block_shape, BF), shaped(block_shape, F32)] + time_keep,
        [per_step(block_shape)] * 2 + time_keep_specs,
        weight_scratch + [pltpu.VMEM((ROWS, width), F32), dma(())],
        mixer_flops, "time_forward",
    )

    result, grad_after_time, mlp_mods, grad_up_bias, grad_down_bias, up_grads, down_grads = run(
        partial(feed_kernel, frames), steps, inverse,
        [after_time, arriving, modul, up_bias_full, down_bias_full, feed_w],
        [per_step(block_shape), cols_spec, mods_spec, whole((1, hidden)), whole((1, width)), ANY],
        [
            cols_shape,
            shaped(block_shape, F32),
            mods_out,
            shaped((1, hidden), F32),
            shaped((1, width), F32),
            shaped((shards, chunks, rows, width), BF),
            shaped((2, shards // 2, chunks, rows, width), BF),
        ],
        [
            cols_spec, per_step(block_shape), mods_out_spec, whole((1, hidden)),
            whole((1, width)), ANY, ANY,
        ],
        [
            pltpu.VMEM((width, hidden), BF),
            pltpu.VMEM((hidden, width), BF),
            pltpu.VMEM((tokens, width), BF),
            pltpu.VMEM((tokens, hidden), BF),
            pltpu.VMEM((tokens, hidden), BF),
            pltpu.VMEM((tokens, width), BF),
            pltpu.VMEM((ROWS, width), F32),
            pltpu.VMEM((2 * chunks, shards, rows, width), BF),
            dma(()),
            dma((chunks + shards,)),
        ],
        6 * 2 * tokens * width * hidden, "feed",
    )

    def to_rows(moved):
        moved = jnp.swapaxes(moved.reshape(own_shape), 0, 1)
        return moved.reshape(frame_count, patches, width).astype(F32)

    def shard_total(packed):
        return lax.psum_scatter(packed, "shard", scatter_dimension=0, tiled=True)[0]

    def parts_of(share):
        parts = share.reshape(groups, -1, width)

        def part(at):
            return lax.dynamic_index_in_dim(parts, at, 0, keepdims=False)

        return [part(group_at)] + [
            swap_group(part(group_at ^ distance), distance) for distance in range(1, groups)
        ]

    def spread_parts(parts, share):
        own = parts[0].astype(F32)
        for piece in parts[1:]:
            own = own + piece.astype(F32)
        own = own.astype(BF)
        near = [own] + [swap_group(own, distance) for distance in range(1, groups)]
        step = 1
        while step < groups:
            odd = jnp.bitwise_and(group_at, step) > 0
            near = [jnp.where(odd, near[at ^ step], near[at]) for at in range(groups)]
            step *= 2
        return jnp.concatenate(near).reshape(share.shape).astype(F32)

    def total(share):
        return spread_parts(parts_of(share), share)

    far_bits = list(range(shards.bit_length() - 2))

    def halve(values, left, bit):
        axis = len(left) - 1 - left.index(bit)
        kept, sent = (lax.index_in_dim(values, side, axis, keepdims=False) for side in (0, 1))
        return (kept.astype(F32) + swap(sent, 2 << bit).astype(F32)).astype(BF)

    def near_total(grads):
        return (grads[0].astype(F32) + swap(grads[1], 1).astype(F32)).astype(BF)

    def far_start(kept):
        half = kept.shape[1] // 2
        folded = (2,) * len(far_bits)
        return [
            halve(part.reshape(folded + part.shape[1:]), far_bits, bit)
            for part, bit in ((kept[:, :half], far_bits[0]), (kept[:, half:], far_bits[-1]))
        ]

    def far_finish(parts):
        done = []
        for values, order in zip(parts, (far_bits, far_bits[::-1])):
            left = [bit for bit in far_bits if bit != order[0]]
            for bit in order[1:]:
                values = halve(values, left, bit)
                left = [other for other in left if other != bit]
            done.append(values)
        return jnp.concatenate(done, axis=0)

    up_share = shard_total(up_grads)
    down_far = far_start(near_total(down_grads))

    going, time_mods, time_grads = run(
        partial(time_backward_kernel, frames, shards), steps, inverse,
        [grad_after_time, time_resid, modul] + time_kept + time_w,
        [per_step(block_shape)] * 2 + [mods_spec] + time_keep_specs + [ANY] * shards,
        [cols_shape, mods_out, shaped(grads_shape, BF)],
        [cols_spec, mods_out_spec, whole(grads_shape)],
        weight_scratch + back_scratch(steps) + [dma(())],
        3 * mixer_flops, "time_backward",
    )
    grad_space = exchange(going.reshape(own_shape))
    time_grads, up_share, grad_space, result, *down_far = lax.optimization_barrier(
        (time_grads, up_share, grad_space, result, *down_far)
    )
    time_share = shard_total(time_grads)
    up_parts = parts_of(up_share)
    down_share = far_finish(down_far)
    arrived = exchange(result.reshape(own_shape))
    grad_rows, space_mods, space_grads = run(
        partial(space_backward_kernel, shards), frame_count, where,
        [grad_space, frames_in, modul] + space_kept + space_w,
        [own_spec, per_step(frames_in.shape), mods_spec] + space_keep_specs + [ANY] * shards,
        [shaped(frames_in.shape, F32), mods_out, shaped(split_shape, BF)],
        [per_step(frames_in.shape), mods_out_spec, whole(split_shape)],
        weight_scratch + back_scratch(frame_count) + [dma(())],
        3 * mixer_flops, "space_backward",
    )
    space_grads, space_mods, arrived, down_share, *up_parts = lax.optimization_barrier(
        (space_grads, space_mods, arrived, down_share, *up_parts)
    )
    space_near = near_total(space_grads)
    up_share = spread_parts(up_parts, up_share)
    frames_out = to_rows(arrived)
    space_near, time_share = lax.optimization_barrier((space_near, time_share))
    space_share = far_finish(far_start(space_near))
    pair = total(jnp.stack([down_share, time_share], axis=1))
    down_share, time_share = pair[:, 0], pair[:, 1]

    mod_part = jnp.concatenate([space_mods, time_mods, mlp_mods], axis=1)
    small_grads = jnp.concatenate(
        [mod_part.reshape(-1), grad_up_bias.reshape(-1), grad_down_bias.reshape(-1)]
    )
    small_grads = shard_sum(small_grads.reshape(-1, 128)).reshape(-1)
    up_dev = up_bias.shape[0]
    down_dev = down_bias.shape[0]
    bias_dev = ada_bias.shape[0]
    small_grads = jnp.concatenate(
        [
            small_grads[:mod_size],
            lax.dynamic_slice_in_dim(small_grads, mod_size + shard_at * up_dev, up_dev, 0),
            lax.dynamic_slice_in_dim(
                small_grads, mod_size + shards * up_dev + shard_at * down_dev, down_dev, 0
            ),
        ]
    )
    small_size = small_grads.shape[0]
    small_grads = jnp.pad(small_grads, (0, -small_size % 1024)).reshape(1, -1, 128)
    small_grads, space_share = lax.optimization_barrier((small_grads, space_share))
    space_share = total(space_share)
    every_small = every(small_grads).reshape(groups, -1)
    every_modul = every_small[:, :mod_size].reshape(groups * clips, 9 * width).astype(BF)
    bias_sums = jnp.sum(every_small[:, mod_size:small_size], axis=0)
    every_embed = every_ids[:, :-1]
    every_steps = every_ids[:, -1].astype(jnp.int32)
    every_cond = jax.nn.silu(every_embed).astype(BF)
    grad_ada = jnp.einsum("cd,cj->dj", every_cond, every_modul, preferred_element_type=F32)
    grad_ada_bias = lax.dynamic_slice_in_dim(
        jnp.sum(every_modul.astype(F32), axis=0), shard_at * bias_dev, bias_dev, 0
    )
    grad_cond = jnp.einsum("cj,dj->cd", every_modul, ada_weight, preferred_element_type=F32)
    _, silu_back = jax.vjp(jax.nn.silu, every_embed)
    grad_embed = silu_back(grad_cond)[0]
    vocab = time_table.shape[0]
    onehot = (jnp.arange(vocab, dtype=jnp.int32)[:, None] == every_steps[None, :]).astype(F32)
    grad_table = jnp.dot(onehot, grad_embed, precision=HIGH)

    def rows_of(blocks):
        return jnp.swapaxes(blocks, 0, 1).reshape(rows, -1)

    return (
        frames_out,
        grad_rows,
        grad_table,
        grad_ada,
        grad_ada_bias,
        rows_of(space_share[:3]),
        space_share[3],
        rows_of(time_share[:3]),
        time_share[3],
        rows_of(up_share),
        bias_sums[:up_dev],
        down_share.reshape(chunks * rows, width),
        bias_sums[up_dev:],
    )


def solution(mesh):
    placed = (
        P(("grp", "shard"), None, None),
        P(("grp", "shard"), None, None),
        P(None, "shard"),
        P("shard", None),
        P("shard"),
        P("shard", None),
        P("shard", None),
        P("shard", None),
        P("shard", None),
        P("shard", None),
        P("shard"),
        P("shard", None),
        P("shard"),
        P("grp"),
        P("grp", None),
        P("grp"),
        P("grp", None),
    )
    return jax.shard_map(
        body,
        mesh=mesh,
        in_specs=placed,
        out_specs=(
            P(("grp", "shard"), None, None),
            P(("grp", "shard"), None, None),
            P(None, "shard"),
            P("shard", None),
            P("shard"),
            P("shard", None),
            P("shard", None),
            P("shard", None),
            P("shard", None),
            P("shard", None),
            P("shard"),
            P("shard", None),
            P("shard"),
        ),
        check_vma=False,
    )
```

```python
from functools import partial

import jax
import jax.numpy as jnp
from jax import lax
from jax.experimental import pallas as pl
from jax.experimental.pallas import tpu as pltpu
from jax.sharding import PartitionSpec as P

HEADS = 12
HEAD_DIM = 64
PAIR = 2 * HEAD_DIM
ROWS = 256
NEAR = 16
HIGH = lax.Precision.HIGHEST
EPSILON = 1e-06
BF = jnp.bfloat16
F32 = jnp.float32
VMEM_LIMIT = 60 * 1024 * 1024


def layer_norm(values):
    center = values - jnp.mean(values, axis=-1, keepdims=True)
    spread = jnp.mean(center * center, axis=-1, keepdims=True)
    inverse = lax.rsqrt(spread + EPSILON)
    return (center * inverse, inverse)


def norm_back(grad_normed, normed, inverse):
    first = jnp.mean(grad_normed, axis=-1, keepdims=True)
    second = jnp.mean(grad_normed * normed, axis=-1, keepdims=True)
    return inverse * (grad_normed - first - normed * second)


def mul(left, right):
    return jnp.dot(left, right, preferred_element_type=F32)


def mul_rt(left, right):
    return lax.dot_general(left, right, (((1,), (1,)), ((), ())), preferred_element_type=F32)


def mul_lt(left, right):
    return lax.dot_general(left, right, (((0,), (0,)), ((), ())), preferred_element_type=F32)


def half_masks(value):
    lane = lax.broadcasted_iota(jnp.int32, (1, PAIR), 1)
    low = jnp.where(lane < HEAD_DIM, value, 0.0)
    return (low.astype(BF), (value - low).astype(BF))


def same_patch():
    rows = lax.broadcasted_iota(jnp.int32, (ROWS, ROWS), 0)
    cols = lax.broadcasted_iota(jnp.int32, (ROWS, ROWS), 1)
    return jnp.bitwise_and(rows, NEAR - 1) == jnp.bitwise_and(cols, NEAR - 1)


def mixer_forward(resid, mods, at, width, weight, out_weight, keep, near):
    packed_ref, mixed_ref, lse_ref, branch_ref = keep
    shift, scale, gate = mods[at : at + 1], mods[at + 1 : at + 2], mods[at + 2 : at + 3]
    normed, _ = layer_norm(resid)
    entry = (normed * (1.0 + scale) + shift).astype(BF)
    for part in range(3):
        packed_ref[0, :, part * width : (part + 1) * width] = mul(
            entry, weight[:, part * width : (part + 1) * width]
        ).astype(BF)
    same = same_patch() if near else None
    lane = lax.broadcasted_iota(jnp.int32, (ROWS, PAIR), 1)
    scaled = half_masks(HEAD_DIM ** (-0.5))
    for pair in range(HEADS // 2):
        at_q = pair * PAIR
        query = packed_ref[0, :, at_q : at_q + PAIR]
        keys = packed_ref[0, :, width + at_q : width + at_q + PAIR]
        values = packed_ref[0, :, 2 * width + at_q : 2 * width + at_q + PAIR]
        halves = []
        for half in range(2):
            scores = mul_rt(keys, query * scaled[half])
            if near:
                scores = jnp.where(same, scores, -jnp.inf)
            highest = jnp.max(scores, axis=0, keepdims=True)
            weights = jnp.exp(scores - highest)
            total = jnp.sum(weights, axis=0, keepdims=True)
            head = 2 * pair + half
            lse_ref[0, head : head + 1, :] = highest + jnp.log(total)
            probs = (weights * (1.0 / total)).astype(BF)
            halves.append(mul_lt(probs, values))
        mixed_ref[0, :, at_q : at_q + PAIR] = jnp.where(
            lane < HEAD_DIM, halves[0], halves[1]
        ).astype(BF)
    branch = mul(mixed_ref[0], out_weight[...])
    branch_ref[0] = branch.astype(BF)
    return resid + gate * branch


def mixer_backward(grad_out, resid, mods, at, width, weight, out_weight, kept, work, near):
    packed_ref, mixed_ref, lse_ref, branch_ref = kept
    entry_ref, packed_grad_ref, branch_grad_ref = work
    shift, scale, gate = mods[at : at + 1], mods[at + 1 : at + 2], mods[at + 2 : at + 3]
    grad_gate = jnp.sum(grad_out * branch_ref[0].astype(F32), axis=0, keepdims=True)
    grad_branch = (gate * grad_out).astype(BF)
    branch_grad_ref[...] = grad_branch
    grad_mixed = mul_rt(grad_branch, out_weight[...]).astype(BF)
    same = same_patch() if near else None
    lane = lax.broadcasted_iota(jnp.int32, (ROWS, PAIR), 1)
    scaled = half_masks(HEAD_DIM ** (-0.5))
    ones = half_masks(1.0)
    for pair in range(HEADS // 2):
        at_q = pair * PAIR
        query = packed_ref[0, :, at_q : at_q + PAIR]
        keys = packed_ref[0, :, width + at_q : width + at_q + PAIR]
        values = packed_ref[0, :, 2 * width + at_q : 2 * width + at_q + PAIR]
        grads = grad_mixed[:, at_q : at_q + PAIR]
        grad_query = []
        grad_keys = None
        grad_values = None
        for half in range(2):
            head = 2 * pair + half
            own_query = query * scaled[half]
            own_grads = grads * ones[half]
            scores = mul_rt(keys, own_query)
            if near:
                scores = jnp.where(same, scores, -jnp.inf)
            probs = jnp.exp(scores - lse_ref[0, head : head + 1, :])
            grad_probs = mul_rt(values, own_grads)
            inner = jnp.sum(probs * grad_probs, axis=0, keepdims=True)
            grad_scores = (probs * (grad_probs - inner)).astype(BF)
            part_values = mul(probs.astype(BF), own_grads)
            part_keys = mul(grad_scores, own_query)
            grad_query.append(mul_lt(grad_scores, keys))
            grad_keys = part_keys if half == 0 else grad_keys + part_keys
            grad_values = part_values if half == 0 else grad_values + part_values
        joined = jnp.where(lane < HEAD_DIM, grad_query[0], grad_query[1])
        packed_grad_ref[:, at_q : at_q + PAIR] = (joined * HEAD_DIM ** (-0.5)).astype(BF)
        packed_grad_ref[:, width + at_q : width + at_q + PAIR] = grad_keys.astype(BF)
        packed_grad_ref[:, 2 * width + at_q : 2 * width + at_q + PAIR] = (
            grad_values.astype(BF)
        )
    grad_entry = mul_rt(packed_grad_ref[...], weight[...])
    normed, inverse = layer_norm(resid)
    entry_ref[...] = (normed * (1.0 + scale) + shift).astype(BF)
    grad_shift = jnp.sum(grad_entry, axis=0, keepdims=True)
    grad_scale = jnp.sum(grad_entry * normed, axis=0, keepdims=True)
    grad_in = grad_out + norm_back(grad_entry * (1.0 + scale), normed, inverse)
    return grad_in, (grad_shift, grad_scale, grad_gate)


def by_distance(me, grad, out, block, shards):
    rows = grad.shape[0] // shards
    for shard in range(shards):
        distance = jnp.bitwise_xor(me, shard)
        out[jnp.bitwise_and(distance, 1), lax.shift_right_logical(distance, 1), block] = grad[
            shard * rows : (shard + 1) * rows
        ]


def fetch_weights(packed, places, sem):
    copies = []
    for shard in range(packed.shape[0]):
        for block in range(packed.shape[1]):
            copies.append(
                pltpu.make_async_copy(packed.at[shard, block], places(shard, block), sem)
            )
    for copy in copies:
        copy.start()
    for copy in copies:
        copy.wait()


def fetch_pieces(me, pieces, weight, out_weight, sem):
    _, rows, width = pieces[0].shape
    copies = []
    for distance, piece in enumerate(pieces):
        first = pl.multiple_of(jnp.bitwise_xor(me, distance) * rows, rows)
        for block in range(3):
            target = weight.at[pl.ds(first, rows), block * width : (block + 1) * width]
            copies.append(pltpu.make_async_copy(piece.at[block], target, sem))
        copies.append(
            pltpu.make_async_copy(piece.at[3], out_weight.at[pl.ds(first, rows), :], sem)
        )
    for copy in copies:
        copy.start()
    for copy in copies:
        copy.wait()


def fetch_spread(me, group, pieces, both, sem):
    count, rows, cols = pieces[0].shape
    copies = []
    for at, piece in enumerate(pieces):
        left = pl.multiple_of(jnp.bitwise_xor(group, at // 2) * cols, cols)
        for k in range(count):
            first = pl.multiple_of(jnp.bitwise_xor(me, 2 * k + at % 2) * rows, rows)
            target = both.at[pl.ds(first, rows), pl.ds(left, cols)]
            copies.append(pltpu.make_async_copy(piece.at[k], target, sem))
    for copy in copies:
        copy.start()
    for copy in copies:
        copy.wait()


def mixer_weight_grads(entry, packed_grad, mixed, branch_grad, put, width):
    entry_t = entry[...].T
    for block in range(3):
        put(block, mul(entry_t, packed_grad[:, block * width : (block + 1) * width]).astype(BF))
    put(3, mul(mixed.T, branch_grad[...]).astype(BF))


def add_mods(mods_out, clip, grads):
    for at, grad in enumerate(grads):
        mods_out[clip, at : at + 1, :] += grad


def space_forward_kernel(shards, where, frames_ref, mods_ref, *refs):
    pieces = refs[:shards]
    after_ref, packed_ref, mixed_ref, lse_ref, branch_ref = refs[shards : shards + 5]
    weight, out_weight, sem = refs[shards + 5 :]
    step = pl.program_id(0)
    width = frames_ref.shape[-1]

    @pl.when(step == 0)
    def _():
        fetch_pieces(where[pl.num_programs(0)], pieces, weight, out_weight, sem)

    mods = mods_ref[where[step]]
    after = mixer_forward(
        frames_ref[0], mods, 0, width, weight, out_weight,
        (packed_ref, mixed_ref, lse_ref, branch_ref), False,
    )
    after_ref[...] = after.astype(BF).reshape(after_ref.shape)


def space_backward_kernel(
    shards, where, grad_ref, frames_ref, mods_ref, packed_ref, mixed_ref, lse_ref, branch_ref, *refs
):
    pieces = refs[:shards]
    rows_out, mods_out, grads_out = refs[shards : shards + 3]
    weight, out_weight, entry, packed_grad, mixed, branch_grad, sem = refs[shards + 3 :]
    step = pl.program_id(0)
    width = frames_ref.shape[-1]

    @pl.when(step == 0)
    def _():
        fetch_pieces(where[pl.num_programs(0)], pieces, weight, out_weight, sem)
        mods_out[...] = jnp.zeros_like(mods_out)

    clip = where[step]
    me = where[pl.num_programs(0)]
    own = pl.ds(pl.multiple_of(step * ROWS, ROWS), ROWS)
    grad_out = grad_ref[...].reshape(ROWS, width).astype(F32)
    grad_in, grads = mixer_backward(
        grad_out, frames_ref[0], mods_ref[clip], 0, width, weight, out_weight,
        (packed_ref, mixed_ref, lse_ref, branch_ref),
        (entry.at[own], packed_grad.at[own], branch_grad.at[own]), False,
    )
    rows_out[0] = grad_in
    mixed[own] = mixed_ref[0]
    add_mods(mods_out, clip, grads)

    @pl.when(step == pl.num_programs(0) - 1)
    def _():
        def put(block, grad):
            by_distance(me, grad, grads_out, block, shards)

        mixer_weight_grads(entry, packed_grad, mixed[...], branch_grad, put, width)


def load_near(source, inverse, resid, clip, first, frames):
    for frame in range(frames):
        values = source[inverse[clip * frames + frame], pl.ds(first, NEAR), :]
        resid[frame * NEAR : (frame + 1) * NEAR, :] = values.astype(F32)


def store_near(target, inverse, values, clip, first, frames):
    for frame in range(frames):
        own = values[frame * NEAR : (frame + 1) * NEAR]
        target[inverse[clip * frames + frame], pl.ds(first, NEAR), :] = own.astype(BF)


def block_place(columns):
    step = pl.program_id(0)
    per_clip = columns // NEAR
    clip = step // per_clip
    first = pl.multiple_of((step - clip * per_clip) * NEAR, NEAR)
    return step, clip, first


def time_forward_kernel(frames, count, inverse, source, mods_ref, *refs):
    pieces = refs[:count]
    resid_ref, after_ref, packed_ref, mixed_ref, lse_ref, branch_ref = refs[count : count + 6]
    both, resid, sem = refs[count + 6 :]
    step, clip, first = block_place(source.shape[1])
    width = source.shape[-1]

    @pl.when(step == 0)
    def _():
        slots = source.shape[0]
        fetch_spread(inverse[slots], inverse[slots + 1], pieces, both, sem)

    weight, out_weight = both.at[:, : 3 * width], both.at[:, 3 * width :]
    load_near(source, inverse, resid, clip, first, frames)
    resid_ref[0] = resid[...].astype(BF)
    after_ref[0] = mixer_forward(
        resid[...], mods_ref[clip], 3, width, weight, out_weight,
        (packed_ref, mixed_ref, lse_ref, branch_ref), True,
    )


def time_backward_kernel(
    frames, shards, count, inverse, grad_ref, resid_ref, mods_ref, packed_ref, mixed_ref, lse_ref,
    branch_ref, *refs
):
    pieces = refs[:count]
    going, mods_out, grads_out = refs[count : count + 3]
    both, entry, packed_grad, mixed, branch_grad, sem = refs[count + 3 :]
    step, clip, first = block_place(going.shape[1])
    width = going.shape[-1]
    weight, out_weight = both.at[:, : 3 * width], both.at[:, 3 * width :]

    @pl.when(step == 0)
    def _():
        slots = going.shape[0]
        fetch_spread(inverse[slots], inverse[slots + 1], pieces, both, sem)
        mods_out[...] = jnp.zeros_like(mods_out)

    own = pl.ds(pl.multiple_of(step * ROWS, ROWS), ROWS)
    grad_in, grads = mixer_backward(
        grad_ref[0], resid_ref[0].astype(F32), mods_ref[clip], 3, width, weight, out_weight,
        (packed_ref, mixed_ref, lse_ref, branch_ref),
        (entry.at[own], packed_grad.at[own], branch_grad.at[own]), True,
    )
    store_near(going, inverse, grad_in, clip, first, frames)
    mixed[own] = mixed_ref[0]
    add_mods(mods_out, clip, grads)

    @pl.when(step == pl.num_programs(0) - 1)
    def _():
        def put(block, grad):
            grads_out[:, block] = grad.reshape(shards, width // shards, width)

        mixer_weight_grads(entry, packed_grad, mixed[...], branch_grad, put, width)


def feed_kernel(
    frames, inverse, after_ref, source, mods_ref, up_bias, down_bias, packed_w, result, grad_ref,
    mods_out, up_bias_out, down_bias_out, up_out, down_out, up, down, entry, active, grad_up_in,
    grad_down_in, grad_result, staged, sem, out_sem,
):
    step, clip, first = block_place(source.shape[1])
    shards, _, rows, width = packed_w.shape
    hidden = up.shape[1]
    chunks = hidden // width

    @pl.when(step == 0)
    def _():
        def places(shard, block):
            if block < chunks:
                return up.at[
                    shard * rows : (shard + 1) * rows, block * width : (block + 1) * width
                ]
            start = (shard * chunks + block - chunks) * rows
            return down.at[start : start + rows, :]

        fetch_weights(packed_w, places, sem)
        mods_out[...] = jnp.zeros_like(mods_out)
        up_bias_out[...] = jnp.zeros_like(up_bias_out)
        down_bias_out[...] = jnp.zeros_like(down_bias_out)

    own = pl.ds(pl.multiple_of(step * ROWS, ROWS), ROWS)
    mods = mods_ref[clip]
    shift, scale, gate = mods[6:7], mods[7:8], mods[8:9]
    load_near(source, inverse, grad_result, clip, first, frames)
    grad_out = grad_result[...]
    down_in = (gate * grad_out).astype(BF)
    grad_down_in[own] = down_in
    down_bias_out[...] += jnp.sum(down_in.astype(F32), axis=0, keepdims=True)
    resid = after_ref[0]
    normed, inverse_std = layer_norm(resid)
    entered = (normed * (1.0 + scale) + shift).astype(BF)
    entry[own] = entered
    downward = jnp.broadcast_to(down_bias[...], (ROWS, width))
    grad_entry = jnp.zeros((ROWS, width), F32)
    for chunk in range(chunks):
        cols = slice(chunk * width, (chunk + 1) * width)
        upward = mul(entered, up[:, cols]) + up_bias[:, cols]
        below = 0.5 + 0.5 * lax.erf(upward * 2.0 ** (-0.5))
        density = jnp.exp(-0.5 * upward * upward) * 0.3989422804014327
        acted = (upward * below).astype(BF)
        active[own, cols] = acted
        downward = downward + mul(acted, down[cols, :])
        grad_active = mul_rt(down_in, down[cols, :])
        up_in = (grad_active * (below + upward * density)).astype(BF)
        grad_up_in[own, cols] = up_in
        up_bias_out[:, cols] += jnp.sum(up_in.astype(F32), axis=0, keepdims=True)
        grad_entry = grad_entry + mul_rt(up_in, up[:, cols])
    store_near(result, inverse, resid + gate * downward, clip, first, frames)
    grad_gate = jnp.sum(grad_out * downward, axis=0, keepdims=True)
    grad_shift = jnp.sum(grad_entry, axis=0, keepdims=True)
    grad_scale = jnp.sum(grad_entry * normed, axis=0, keepdims=True)
    add_mods(mods_out, clip, (grad_shift, grad_scale, grad_gate))
    grad_ref[0] = grad_out + norm_back(grad_entry * (1.0 + scale), normed, inverse_std)

    @pl.when(step == pl.num_programs(0) - 1)
    def _():
        entry_t = entry[...].T
        copies = []
        for chunk in range(chunks):
            grad = mul(entry_t, grad_up_in[:, chunk * width : (chunk + 1) * width]).astype(BF)
            staged[chunk] = grad.reshape(shards, rows, width)
            copies.append(
                pltpu.make_async_copy(staged.at[chunk], up_out.at[:, chunk], out_sem.at[chunk])
            )
            copies[-1].start()
        group = shards // chunks
        me = inverse[source.shape[0]]
        for chunk in range(chunks):
            grad = mul_lt(active[:, chunk * width : (chunk + 1) * width], grad_down_in[...])
            slot = chunks + chunk
            staged[slot] = grad.astype(BF).reshape(shards, rows, width)
            for part in range(group):
                shard = chunk * group + part
                distance = jnp.bitwise_xor(me, shard)
                place = jnp.bitwise_and(distance, 1), lax.shift_right_logical(distance, 1)
                copies.append(
                    pltpu.make_async_copy(
                        staged.at[slot, part * chunks : (part + 1) * chunks],
                        down_out.at[place],
                        out_sem.at[chunks + shard],
                    )
                )
                copies[-1].start()
        for copy in copies:
            copy.wait()


def whole(shape):
    return pl.BlockSpec(shape, lambda *_: (0,) * len(shape))


def per_step(shape):
    return pl.BlockSpec((1,) + tuple(shape[1:]), lambda step, *_: (step,) + (0,) * (len(shape) - 1))


ANY = pl.BlockSpec(memory_space=pl.ANY)


def run(kernel, steps, table, ins, in_specs, outs, out_specs, scratch, flops, name):
    size = lambda shaped: shaped.size * shaped.dtype.itemsize
    moved = sum(size(a) for a in ins) + sum(size(a) for a in outs)
    return pl.pallas_call(
        kernel,
        grid_spec=pltpu.PrefetchScalarGridSpec(
            num_scalar_prefetch=1, grid=(steps,), in_specs=in_specs, out_specs=out_specs,
            scratch_shapes=scratch,
        ),
        out_shape=outs,
        compiler_params=pltpu.CompilerParams(
            dimension_semantics=("arbitrary",), vmem_limit_bytes=VMEM_LIMIT
        ),
        cost_estimate=pl.CostEstimate(flops=flops, bytes_accessed=moved, transcendentals=0),
        name=name,
    )(table, *ins)


def body(
    frames_in,
    cotangent,
    time_table,
    ada_weight,
    ada_bias,
    space_qkv,
    space_out,
    time_qkv,
    time_out,
    up_weight,
    up_bias,
    down_weight,
    down_bias,
    timesteps,
    task_mask,
    clip_weight,
    frame_table,
):
    shards = lax.axis_size("shard")
    shard_at = lax.axis_index("shard")
    frame_count, patches, width = frames_in.shape
    clips = timesteps.shape[0]
    frames = task_mask.shape[1]
    table = frame_table[0]
    group_frames = table.shape[0]
    columns = patches // shards
    rows = width // shards
    hidden = up_weight.shape[1]
    chunks = hidden // width
    tokens = group_frames * columns
    steps = tokens // ROWS
    shaped = jax.ShapeDtypeStruct

    def column_blocks(weight):
        return jnp.swapaxes(weight.reshape(rows, -1, width), 0, 1)

    def swap(values, distance):
        pairs = [(at, at ^ distance) for at in range(shards)]
        return lax.ppermute(values, "shard", pairs)

    def gather(packed):
        return lax.all_gather(packed[None], "shard", axis=0, tiled=True)

    groups = lax.axis_size("grp")
    group_at = lax.axis_index("grp")

    def swap_group(values, distance):
        pairs = [(at, at ^ distance) for at in range(groups)]
        return lax.ppermute(values, "grp", pairs)

    def every(values):
        stacked = jnp.zeros((groups,) + values.shape, values.dtype)
        for distance in range(groups):
            piece = swap_group(values, distance) if distance else values
            stacked = lax.dynamic_update_index_in_dim(stacked, piece, group_at ^ distance, 0)
        return stacked

    def shard_sum(values):
        distance = 1
        while distance < shards:
            values = values + swap(values, distance)
            distance *= 2
        return values

    def even_pieces(own):
        return [own] + [swap(own, distance) for distance in range(2, shards, 2)]

    def all_pieces(even):
        pieces = []
        for piece in even:
            pieces += [piece, swap(piece, 1)]
        return pieces

    own_time = jnp.concatenate([time_qkv, time_out], axis=1)
    part_cols = own_time.shape[1] // groups
    own_time = lax.dynamic_slice_in_dim(own_time, group_at * part_cols, part_cols, 1)
    own_space = jnp.concatenate([column_blocks(space_qkv), space_out[None]], axis=0)
    even_time, own_space = lax.optimization_barrier((even_pieces(own_time), own_space))
    even_time = jnp.stack(even_time)
    even_time = [even_time] + [swap_group(even_time, distance) for distance in range(1, groups)]
    even = even_pieces(own_space)

    embed = jnp.take(time_table, timesteps, axis=0).astype(F32)
    cond = jax.nn.silu(embed).astype(BF)
    mod_local = jnp.dot(cond, ada_weight, preferred_element_type=F32)

    def spread(local):
        full = jnp.zeros((shards, local.shape[0]), F32)
        return lax.dynamic_update_slice_in_dim(
            full, local.astype(F32)[None], shard_at, 0
        ).reshape(-1)

    small = jnp.concatenate(
        [
            (mod_local + spread(ada_bias)[None]).reshape(-1),
            spread(up_bias),
            spread(down_bias),
        ]
    )
    small = lax.all_gather(small.reshape(1, -1, 128), "shard", axis=0, tiled=True)
    small, even[1:], even_time[2:3] = lax.optimization_barrier((small, even[1:], even_time[2:3]))
    small = jnp.sum(small, axis=0).reshape(-1)
    space_w = all_pieces(even)
    own_feed = jnp.concatenate(
        [column_blocks(up_weight), down_weight.reshape(chunks, rows, width)], axis=0
    )
    own_feed, *_ = lax.optimization_barrier((own_feed, *even[1:]))
    feed_w = gather(own_feed)
    mod_size = clips * 9 * width
    modul = small[:mod_size].reshape(clips, 9, width)
    up_bias_full = small[mod_size:-width].reshape(1, hidden)
    down_bias_full = small[-width:].reshape(1, width)

    slot_ids = shard_at * frame_count + jnp.arange(frame_count, dtype=jnp.int32)
    frame_ids = jnp.take(table, slot_ids)
    clip_of = frame_ids // frames
    frame_of = frame_ids % frames
    where = jnp.concatenate([clip_of, shard_at[None].astype(jnp.int32)])
    slots = jnp.arange(group_frames, dtype=jnp.int32)
    inverse = jnp.sum(jnp.where(table[None, :] == slots[:, None], slots[None, :], 0), axis=1)
    inverse = jnp.concatenate([inverse, jnp.stack([shard_at, group_at]).astype(jnp.int32)])

    def exchange(parts):
        return lax.all_to_all(parts, "shard", split_axis=0, concat_axis=0, tiled=True)

    row_weights = task_mask[clip_of, frame_of].astype(F32) * clip_weight[clip_of]
    weighted = (cotangent * row_weights[:, None, None]).astype(BF)
    weighted = jnp.swapaxes(weighted.reshape(frame_count, shards, columns, width), 0, 1)
    arriving = exchange(weighted).reshape(group_frames, columns, width)

    own_shape = (shards, frame_count, columns, width)
    own_spec = pl.BlockSpec((shards, 1, columns, width), lambda step, *_: (0, step, 0, 0))
    mods_spec = whole((clips, 9, width))
    mods_out = shaped((clips, 3, width), F32)
    mods_out_spec = whole((clips, 3, width))
    grads_shape = (shards, 4, rows, width)
    split_shape = (2, shards // 2, 4, rows, width)
    weight_scratch = [
        pltpu.VMEM((width, 3 * width), BF),
        pltpu.VMEM((width, width), BF),
    ]
    both_scratch = pltpu.VMEM((width, 4 * width), BF)
    dma = pltpu.SemaphoreType.DMA

    def kept(count):
        shapes = [
            shaped((count, ROWS, 3 * width), BF),
            shaped((count, ROWS, width), BF),
            shaped((count, 16, ROWS), F32),
            shaped((count, ROWS, width), BF),
        ]
        return shapes, [per_step(one.shape) for one in shapes]

    def back_scratch(count):
        return [
            pltpu.VMEM((count * ROWS, width), BF),
            pltpu.VMEM((count * ROWS, 3 * width), BF),
            pltpu.VMEM((count * ROWS, width), BF),
            pltpu.VMEM((count * ROWS, width), BF),
        ]

    mixer_flops = 2 * tokens * width * 4 * width + 4 * tokens * ROWS * width * 2
    space_keep, space_keep_specs = kept(frame_count)
    after_space, *space_kept = run(
        partial(space_forward_kernel, shards), frame_count, where,
        [frames_in, modul] + space_w,
        [per_step(frames_in.shape), mods_spec] + [ANY] * shards,
        [shaped(own_shape, BF)] + space_keep,
        [own_spec] + space_keep_specs,
        weight_scratch + [dma(())],
        mixer_flops, "space_forward",
    )
    after_space, even_time = lax.optimization_barrier((after_space, even_time))
    time_w = all_pieces(even_time)
    received = exchange(after_space).reshape(group_frames, columns, width)
    own_ids = jnp.concatenate([embed, timesteps.astype(F32)[:, None]], axis=1)
    own_ids, _ = lax.optimization_barrier((own_ids, after_space))
    every_ids = every(own_ids).reshape(-1, own_ids.shape[1])

    cols_spec = whole((group_frames, columns, width))
    cols_shape = shaped((group_frames, columns, width), BF)
    block_shape = (steps, ROWS, width)
    time_keep, time_keep_specs = kept(steps)
    time_resid, after_time, *time_kept = run(
        partial(time_forward_kernel, frames, 2 * groups), steps, inverse,
        [received, modul] + time_w,
        [cols_spec, mods_spec] + [ANY] * (2 * groups),
        [shaped(block_shape, BF), shaped(block_shape, F32)] + time_keep,
        [per_step(block_shape)] * 2 + time_keep_specs,
        [both_scratch, pltpu.VMEM((ROWS, width), F32), dma(())],
        mixer_flops, "time_forward",
    )

    result, grad_after_time, mlp_mods, grad_up_bias, grad_down_bias, up_grads, down_grads = run(
        partial(feed_kernel, frames), steps, inverse,
        [after_time, arriving, modul, up_bias_full, down_bias_full, feed_w],
        [per_step(block_shape), cols_spec, mods_spec, whole((1, hidden)), whole((1, width)), ANY],
        [
            cols_shape,
            shaped(block_shape, F32),
            mods_out,
            shaped((1, hidden), F32),
            shaped((1, width), F32),
            shaped((shards, chunks, rows, width), BF),
            shaped((2, shards // 2, chunks, rows, width), BF),
        ],
        [
            cols_spec, per_step(block_shape), mods_out_spec, whole((1, hidden)),
            whole((1, width)), ANY, ANY,
        ],
        [
            pltpu.VMEM((width, hidden), BF),
            pltpu.VMEM((hidden, width), BF),
            pltpu.VMEM((tokens, width), BF),
            pltpu.VMEM((tokens, hidden), BF),
            pltpu.VMEM((tokens, hidden), BF),
            pltpu.VMEM((tokens, width), BF),
            pltpu.VMEM((ROWS, width), F32),
            pltpu.VMEM((2 * chunks, shards, rows, width), BF),
            dma(()),
            dma((chunks + shards,)),
        ],
        6 * 2 * tokens * width * hidden, "feed",
    )

    def to_rows(moved):
        moved = jnp.swapaxes(moved.reshape(own_shape), 0, 1)
        return moved.reshape(frame_count, patches, width).astype(F32)

    def shard_total(packed):
        return lax.psum_scatter(packed, "shard", scatter_dimension=0, tiled=True)[0]

    def parts_of(share):
        parts = share.reshape(groups, -1, width)

        def part(at):
            return lax.dynamic_index_in_dim(parts, at, 0, keepdims=False)

        return [part(group_at)] + [
            swap_group(part(group_at ^ distance), distance) for distance in range(1, groups)
        ]

    def spread_parts(parts, share):
        own = parts[0].astype(F32)
        for piece in parts[1:]:
            own = own + piece.astype(F32)
        own = own.astype(BF)
        near = [own] + [swap_group(own, distance) for distance in range(1, groups)]
        step = 1
        while step < groups:
            odd = jnp.bitwise_and(group_at, step) > 0
            near = [jnp.where(odd, near[at ^ step], near[at]) for at in range(groups)]
            step *= 2
        return jnp.concatenate(near).reshape(share.shape).astype(F32)

    def total(share):
        return spread_parts(parts_of(share), share)

    far_bits = list(range(shards.bit_length() - 2))

    def halve(values, left, bit):
        axis = len(left) - 1 - left.index(bit)
        kept, sent = (lax.index_in_dim(values, side, axis, keepdims=False) for side in (0, 1))
        return (kept.astype(F32) + swap(sent, 2 << bit).astype(F32)).astype(BF)

    def near_total(grads):
        return (grads[0].astype(F32) + swap(grads[1], 1).astype(F32)).astype(BF)

    def far_start(kept):
        half = kept.shape[1] // 2
        folded = (2,) * len(far_bits)
        return [
            halve(part.reshape(folded + part.shape[1:]), far_bits, bit)
            for part, bit in ((kept[:, :half], far_bits[0]), (kept[:, half:], far_bits[-1]))
        ]

    def far_finish(parts):
        done = []
        for values, order in zip(parts, (far_bits, far_bits[::-1])):
            left = [bit for bit in far_bits if bit != order[0]]
            for bit in order[1:]:
                values = halve(values, left, bit)
                left = [other for other in left if other != bit]
            done.append(values)
        return jnp.concatenate(done, axis=0)

    up_share = shard_total(up_grads)
    down_far = far_start(near_total(down_grads))

    going, time_mods, time_grads = run(
        partial(time_backward_kernel, frames, shards, 2 * groups), steps, inverse,
        [grad_after_time, time_resid, modul] + time_kept + time_w,
        [per_step(block_shape)] * 2 + [mods_spec] + time_keep_specs + [ANY] * (2 * groups),
        [cols_shape, mods_out, shaped(grads_shape, BF)],
        [cols_spec, mods_out_spec, whole(grads_shape)],
        [both_scratch] + back_scratch(steps) + [dma(())],
        3 * mixer_flops, "time_backward",
    )
    grad_space = exchange(going.reshape(own_shape))
    time_grads, up_share, grad_space, result, *down_far = lax.optimization_barrier(
        (time_grads, up_share, grad_space, result, *down_far)
    )
    time_share = shard_total(time_grads)
    up_parts = parts_of(up_share)
    down_share = far_finish(down_far)
    arrived = exchange(result.reshape(own_shape))
    grad_rows, space_mods, space_grads = run(
        partial(space_backward_kernel, shards), frame_count, where,
        [grad_space, frames_in, modul] + space_kept + space_w,
        [own_spec, per_step(frames_in.shape), mods_spec] + space_keep_specs + [ANY] * shards,
        [shaped(frames_in.shape, F32), mods_out, shaped(split_shape, BF)],
        [per_step(frames_in.shape), mods_out_spec, whole(split_shape)],
        weight_scratch + back_scratch(frame_count) + [dma(())],
        3 * mixer_flops, "space_backward",
    )
    space_grads, space_mods, arrived, down_share, *up_parts = lax.optimization_barrier(
        (space_grads, space_mods, arrived, down_share, *up_parts)
    )
    space_near = near_total(space_grads)
    up_share = spread_parts(up_parts, up_share)
    frames_out = to_rows(arrived)
    space_near, time_share = lax.optimization_barrier((space_near, time_share))
    space_share = far_finish(far_start(space_near))
    pair = lax.psum(jnp.stack([down_share, time_share], axis=1), "grp").astype(F32)
    down_share, time_share = pair[:, 0], pair[:, 1]

    mod_part = jnp.concatenate([space_mods, time_mods, mlp_mods], axis=1)
    small_grads = jnp.concatenate(
        [mod_part.reshape(-1), grad_up_bias.reshape(-1), grad_down_bias.reshape(-1)]
    )
    small_grads = shard_sum(small_grads.reshape(-1, 128)).reshape(-1)
    up_dev = up_bias.shape[0]
    down_dev = down_bias.shape[0]
    bias_dev = ada_bias.shape[0]
    small_grads = jnp.concatenate(
        [
            small_grads[:mod_size],
            lax.dynamic_slice_in_dim(small_grads, mod_size + shard_at * up_dev, up_dev, 0),
            lax.dynamic_slice_in_dim(
                small_grads, mod_size + shards * up_dev + shard_at * down_dev, down_dev, 0
            ),
        ]
    )
    small_size = small_grads.shape[0]
    small_grads = jnp.pad(small_grads, (0, -small_size % 1024)).reshape(1, -1, 128)
    small_grads, space_share = lax.optimization_barrier((small_grads, space_share))
    space_share = total(space_share)
    every_small = every(small_grads).reshape(groups, -1)
    every_modul = every_small[:, :mod_size].reshape(groups * clips, 9 * width).astype(BF)
    bias_sums = jnp.sum(every_small[:, mod_size:small_size], axis=0)
    every_embed = every_ids[:, :-1]
    every_steps = every_ids[:, -1].astype(jnp.int32)
    every_cond = jax.nn.silu(every_embed).astype(BF)
    grad_ada = jnp.einsum("cd,cj->dj", every_cond, every_modul, preferred_element_type=F32)
    grad_ada_bias = lax.dynamic_slice_in_dim(
        jnp.sum(every_modul.astype(F32), axis=0), shard_at * bias_dev, bias_dev, 0
    )
    grad_cond = jnp.einsum("cj,dj->cd", every_modul, ada_weight, preferred_element_type=F32)
    _, silu_back = jax.vjp(jax.nn.silu, every_embed)
    grad_embed = silu_back(grad_cond)[0]
    vocab = time_table.shape[0]
    onehot = (jnp.arange(vocab, dtype=jnp.int32)[:, None] == every_steps[None, :]).astype(F32)
    grad_table = jnp.dot(onehot, grad_embed, precision=HIGH)

    def rows_of(blocks):
        return jnp.swapaxes(blocks, 0, 1).reshape(rows, -1)

    return (
        frames_out,
        grad_rows,
        grad_table,
        grad_ada,
        grad_ada_bias,
        rows_of(space_share[:3]),
        space_share[3],
        rows_of(time_share[:3]),
        time_share[3],
        rows_of(up_share),
        bias_sums[:up_dev],
        down_share.reshape(chunks * rows, width),
        bias_sums[up_dev:],
    )


def solution(mesh):
    placed = (
        P(("grp", "shard"), None, None),
        P(("grp", "shard"), None, None),
        P(None, "shard"),
        P("shard", None),
        P("shard"),
        P("shard", None),
        P("shard", None),
        P("shard", None),
        P("shard", None),
        P("shard", None),
        P("shard"),
        P("shard", None),
        P("shard"),
        P("grp"),
        P("grp", None),
        P("grp"),
        P("grp", None),
    )
    return jax.shard_map(
        body,
        mesh=mesh,
        in_specs=placed,
        out_specs=(
            P(("grp", "shard"), None, None),
            P(("grp", "shard"), None, None),
            P(None, "shard"),
            P("shard", None),
            P("shard"),
            P("shard", None),
            P("shard", None),
            P("shard", None),
            P("shard", None),
            P("shard", None),
            P("shard"),
            P("shard", None),
            P("shard"),
        ),
        check_vma=False,
    )
```

```python
from functools import partial

import jax
import jax.numpy as jnp
from jax import lax
from jax.experimental import pallas as pl
from jax.experimental.pallas import tpu as pltpu
from jax.sharding import PartitionSpec as P

HEADS = 12
HEAD_DIM = 64
PAIR = 2 * HEAD_DIM
ROWS = 256
NEAR = 16
HIGH = lax.Precision.HIGHEST
EPSILON = 1e-06
BF = jnp.bfloat16
F32 = jnp.float32
VMEM_LIMIT = 60 * 1024 * 1024


def layer_norm(values):
    center = values - jnp.mean(values, axis=-1, keepdims=True)
    spread = jnp.mean(center * center, axis=-1, keepdims=True)
    inverse = lax.rsqrt(spread + EPSILON)
    return (center * inverse, inverse)


def norm_back(grad_normed, normed, inverse):
    first = jnp.mean(grad_normed, axis=-1, keepdims=True)
    second = jnp.mean(grad_normed * normed, axis=-1, keepdims=True)
    return inverse * (grad_normed - first - normed * second)


def mul(left, right):
    return jnp.dot(left, right, preferred_element_type=F32)


def mul_rt(left, right):
    return lax.dot_general(left, right, (((1,), (1,)), ((), ())), preferred_element_type=F32)


def mul_lt(left, right):
    return lax.dot_general(left, right, (((0,), (0,)), ((), ())), preferred_element_type=F32)


def half_masks(value):
    lane = lax.broadcasted_iota(jnp.int32, (1, PAIR), 1)
    low = jnp.where(lane < HEAD_DIM, value, 0.0)
    return (low.astype(BF), (value - low).astype(BF))


def same_patch():
    rows = lax.broadcasted_iota(jnp.int32, (ROWS, ROWS), 0)
    cols = lax.broadcasted_iota(jnp.int32, (ROWS, ROWS), 1)
    return jnp.bitwise_and(rows, NEAR - 1) == jnp.bitwise_and(cols, NEAR - 1)


def mixer_forward(resid, mods, at, width, weight, out_weight, keep, near):
    packed_ref, mixed_ref, lse_ref, branch_ref = keep
    shift, scale, gate = mods[at : at + 1], mods[at + 1 : at + 2], mods[at + 2 : at + 3]
    normed, _ = layer_norm(resid)
    entry = (normed * (1.0 + scale) + shift).astype(BF)
    for part in range(3):
        packed_ref[0, :, part * width : (part + 1) * width] = mul(
            entry, weight[:, part * width : (part + 1) * width]
        ).astype(BF)
    same = same_patch() if near else None
    lane = lax.broadcasted_iota(jnp.int32, (ROWS, PAIR), 1)
    scaled = half_masks(HEAD_DIM ** (-0.5))
    for pair in range(HEADS // 2):
        at_q = pair * PAIR
        query = packed_ref[0, :, at_q : at_q + PAIR]
        keys = packed_ref[0, :, width + at_q : width + at_q + PAIR]
        values = packed_ref[0, :, 2 * width + at_q : 2 * width + at_q + PAIR]
        halves = []
        for half in range(2):
            scores = mul_rt(keys, query * scaled[half])
            if near:
                scores = jnp.where(same, scores, -jnp.inf)
            highest = jnp.max(scores, axis=0, keepdims=True)
            weights = jnp.exp(scores - highest)
            total = jnp.sum(weights, axis=0, keepdims=True)
            head = 2 * pair + half
            lse_ref[0, head : head + 1, :] = highest + jnp.log(total)
            probs = (weights * (1.0 / total)).astype(BF)
            halves.append(mul_lt(probs, values))
        mixed_ref[0, :, at_q : at_q + PAIR] = jnp.where(
            lane < HEAD_DIM, halves[0], halves[1]
        ).astype(BF)
    branch = mul(mixed_ref[0], out_weight[...])
    branch_ref[0] = branch.astype(BF)
    return resid + gate * branch


def mixer_backward(grad_out, resid, mods, at, width, weight, out_weight, kept, work, near):
    packed_ref, mixed_ref, lse_ref, branch_ref = kept
    entry_ref, packed_grad_ref, branch_grad_ref = work
    shift, scale, gate = mods[at : at + 1], mods[at + 1 : at + 2], mods[at + 2 : at + 3]
    grad_gate = jnp.sum(grad_out * branch_ref[0].astype(F32), axis=0, keepdims=True)
    grad_branch = (gate * grad_out).astype(BF)
    branch_grad_ref[...] = grad_branch
    grad_mixed = mul_rt(grad_branch, out_weight[...]).astype(BF)
    same = same_patch() if near else None
    lane = lax.broadcasted_iota(jnp.int32, (ROWS, PAIR), 1)
    scaled = half_masks(HEAD_DIM ** (-0.5))
    ones = half_masks(1.0)
    for pair in range(HEADS // 2):
        at_q = pair * PAIR
        query = packed_ref[0, :, at_q : at_q + PAIR]
        keys = packed_ref[0, :, width + at_q : width + at_q + PAIR]
        values = packed_ref[0, :, 2 * width + at_q : 2 * width + at_q + PAIR]
        grads = grad_mixed[:, at_q : at_q + PAIR]
        grad_query = []
        grad_keys = None
        grad_values = None
        for half in range(2):
            head = 2 * pair + half
            own_query = query * scaled[half]
            own_grads = grads * ones[half]
            scores = mul_rt(keys, own_query)
            if near:
                scores = jnp.where(same, scores, -jnp.inf)
            probs = jnp.exp(scores - lse_ref[0, head : head + 1, :])
            grad_probs = mul_rt(values, own_grads)
            inner = jnp.sum(probs * grad_probs, axis=0, keepdims=True)
            grad_scores = (probs * (grad_probs - inner)).astype(BF)
            part_values = mul(probs.astype(BF), own_grads)
            part_keys = mul(grad_scores, own_query)
            grad_query.append(mul_lt(grad_scores, keys))
            grad_keys = part_keys if half == 0 else grad_keys + part_keys
            grad_values = part_values if half == 0 else grad_values + part_values
        joined = jnp.where(lane < HEAD_DIM, grad_query[0], grad_query[1])
        packed_grad_ref[:, at_q : at_q + PAIR] = (joined * HEAD_DIM ** (-0.5)).astype(BF)
        packed_grad_ref[:, width + at_q : width + at_q + PAIR] = grad_keys.astype(BF)
        packed_grad_ref[:, 2 * width + at_q : 2 * width + at_q + PAIR] = (
            grad_values.astype(BF)
        )
    grad_entry = mul_rt(packed_grad_ref[...], weight[...])
    normed, inverse = layer_norm(resid)
    entry_ref[...] = (normed * (1.0 + scale) + shift).astype(BF)
    grad_shift = jnp.sum(grad_entry, axis=0, keepdims=True)
    grad_scale = jnp.sum(grad_entry * normed, axis=0, keepdims=True)
    grad_in = grad_out + norm_back(grad_entry * (1.0 + scale), normed, inverse)
    return grad_in, (grad_shift, grad_scale, grad_gate)


def by_distance(me, grad, out, block, shards):
    rows = grad.shape[0] // shards
    for shard in range(shards):
        distance = jnp.bitwise_xor(me, shard)
        out[jnp.bitwise_and(distance, 1), lax.shift_right_logical(distance, 1), block] = grad[
            shard * rows : (shard + 1) * rows
        ]


def fetch_weights(packed, places, sem):
    copies = []
    for shard in range(packed.shape[0]):
        for block in range(packed.shape[1]):
            copies.append(
                pltpu.make_async_copy(packed.at[shard, block], places(shard, block), sem)
            )
    for copy in copies:
        copy.start()
    for copy in copies:
        copy.wait()


def fetch_pieces(me, pieces, weight, out_weight, sem):
    _, rows, width = pieces[0].shape
    copies = []
    for distance, piece in enumerate(pieces):
        first = pl.multiple_of(jnp.bitwise_xor(me, distance) * rows, rows)
        for block in range(3):
            target = weight.at[pl.ds(first, rows), block * width : (block + 1) * width]
            copies.append(pltpu.make_async_copy(piece.at[block], target, sem))
        copies.append(
            pltpu.make_async_copy(piece.at[3], out_weight.at[pl.ds(first, rows), :], sem)
        )
    for copy in copies:
        copy.start()
    for copy in copies:
        copy.wait()


def mixer_weight_grads(entry, packed_grad, mixed, branch_grad, put, width):
    entry_t = entry[...].T
    for block in range(3):
        put(block, mul(entry_t, packed_grad[:, block * width : (block + 1) * width]).astype(BF))
    put(3, mul(mixed.T, branch_grad[...]).astype(BF))


def add_mods(mods_out, clip, grads):
    for at, grad in enumerate(grads):
        mods_out[clip, at : at + 1, :] += grad


def space_forward_kernel(shards, where, frames_ref, mods_ref, *refs):
    pieces = refs[:shards]
    after_ref, packed_ref, mixed_ref, lse_ref, branch_ref = refs[shards : shards + 5]
    weight, out_weight, sem = refs[shards + 5 :]
    step = pl.program_id(0)
    width = frames_ref.shape[-1]

    @pl.when(step == 0)
    def _():
        fetch_pieces(where[pl.num_programs(0)], pieces, weight, out_weight, sem)

    mods = mods_ref[where[step]]
    after = mixer_forward(
        frames_ref[0], mods, 0, width, weight, out_weight,
        (packed_ref, mixed_ref, lse_ref, branch_ref), False,
    )
    after_ref[...] = after.astype(BF).reshape(after_ref.shape)


def space_backward_kernel(
    shards, where, grad_ref, frames_ref, mods_ref, packed_ref, mixed_ref, lse_ref, branch_ref, *refs
):
    pieces = refs[:shards]
    rows_out, mods_out, grads_out = refs[shards : shards + 3]
    weight, out_weight, entry, packed_grad, mixed, branch_grad, sem = refs[shards + 3 :]
    step = pl.program_id(0)
    width = frames_ref.shape[-1]

    @pl.when(step == 0)
    def _():
        fetch_pieces(where[pl.num_programs(0)], pieces, weight, out_weight, sem)
        mods_out[...] = jnp.zeros_like(mods_out)

    clip = where[step]
    me = where[pl.num_programs(0)]
    own = pl.ds(pl.multiple_of(step * ROWS, ROWS), ROWS)
    grad_out = grad_ref[...].reshape(ROWS, width).astype(F32)
    grad_in, grads = mixer_backward(
        grad_out, frames_ref[0], mods_ref[clip], 0, width, weight, out_weight,
        (packed_ref, mixed_ref, lse_ref, branch_ref),
        (entry.at[own], packed_grad.at[own], branch_grad.at[own]), False,
    )
    rows_out[0] = grad_in
    mixed[own] = mixed_ref[0]
    add_mods(mods_out, clip, grads)

    @pl.when(step == pl.num_programs(0) - 1)
    def _():
        def put(block, grad):
            by_distance(me, grad, grads_out, block, shards)

        mixer_weight_grads(entry, packed_grad, mixed[...], branch_grad, put, width)


def load_near(source, inverse, resid, clip, first, frames):
    for frame in range(frames):
        values = source[inverse[clip * frames + frame], pl.ds(first, NEAR), :]
        resid[frame * NEAR : (frame + 1) * NEAR, :] = values.astype(F32)


def store_near(target, inverse, values, clip, first, frames):
    for frame in range(frames):
        own = values[frame * NEAR : (frame + 1) * NEAR]
        target[inverse[clip * frames + frame], pl.ds(first, NEAR), :] = own.astype(BF)


def block_place(columns):
    step = pl.program_id(0)
    per_clip = columns // NEAR
    clip = step // per_clip
    first = pl.multiple_of((step - clip * per_clip) * NEAR, NEAR)
    return step, clip, first


def time_forward_kernel(frames, shards, inverse, source, mods_ref, *refs):
    pieces = refs[:shards]
    resid_ref, after_ref, packed_ref, mixed_ref, lse_ref, branch_ref = refs[shards : shards + 6]
    weight, out_weight, resid, sem = refs[shards + 6 :]
    step, clip, first = block_place(source.shape[1])
    width = source.shape[-1]

    @pl.when(step == 0)
    def _():
        fetch_pieces(inverse[source.shape[0]], pieces, weight, out_weight, sem)

    load_near(source, inverse, resid, clip, first, frames)
    resid_ref[0] = resid[...].astype(BF)
    after_ref[0] = mixer_forward(
        resid[...], mods_ref[clip], 3, width, weight, out_weight,
        (packed_ref, mixed_ref, lse_ref, branch_ref), True,
    )


def time_backward_kernel(
    frames, shards, inverse, grad_ref, resid_ref, mods_ref, packed_ref, mixed_ref, lse_ref,
    branch_ref, *refs
):
    pieces = refs[:shards]
    going, mods_out, grads_out = refs[shards : shards + 3]
    weight, out_weight, entry, packed_grad, mixed, branch_grad, sem = refs[shards + 3 :]
    step, clip, first = block_place(going.shape[1])
    width = going.shape[-1]

    @pl.when(step == 0)
    def _():
        fetch_pieces(inverse[going.shape[0]], pieces, weight, out_weight, sem)
        mods_out[...] = jnp.zeros_like(mods_out)

    own = pl.ds(pl.multiple_of(step * ROWS, ROWS), ROWS)
    grad_in, grads = mixer_backward(
        grad_ref[0], resid_ref[0].astype(F32), mods_ref[clip], 3, width, weight, out_weight,
        (packed_ref, mixed_ref, lse_ref, branch_ref),
        (entry.at[own], packed_grad.at[own], branch_grad.at[own]), True,
    )
    store_near(going, inverse, grad_in, clip, first, frames)
    mixed[own] = mixed_ref[0]
    add_mods(mods_out, clip, grads)

    @pl.when(step == pl.num_programs(0) - 1)
    def _():
        def put(block, grad):
            grads_out[:, block] = grad.reshape(shards, width // shards, width)

        mixer_weight_grads(entry, packed_grad, mixed[...], branch_grad, put, width)


def feed_kernel(
    frames, inverse, after_ref, source, mods_ref, up_bias, down_bias, packed_w, result, grad_ref,
    mods_out, up_bias_out, down_bias_out, up_out, down_out, up, down, entry, active, grad_up_in,
    grad_down_in, grad_result, staged, sem, out_sem,
):
    step, clip, first = block_place(source.shape[1])
    shards, _, rows, width = packed_w.shape
    hidden = up.shape[1]
    chunks = hidden // width

    @pl.when(step == 0)
    def _():
        def places(shard, block):
            if block < chunks:
                return up.at[
                    shard * rows : (shard + 1) * rows, block * width : (block + 1) * width
                ]
            start = (shard * chunks + block - chunks) * rows
            return down.at[start : start + rows, :]

        fetch_weights(packed_w, places, sem)
        mods_out[...] = jnp.zeros_like(mods_out)
        up_bias_out[...] = jnp.zeros_like(up_bias_out)
        down_bias_out[...] = jnp.zeros_like(down_bias_out)

    own = pl.ds(pl.multiple_of(step * ROWS, ROWS), ROWS)
    mods = mods_ref[clip]
    shift, scale, gate = mods[6:7], mods[7:8], mods[8:9]
    load_near(source, inverse, grad_result, clip, first, frames)
    grad_out = grad_result[...]
    down_in = (gate * grad_out).astype(BF)
    grad_down_in[own] = down_in
    down_bias_out[...] += jnp.sum(down_in.astype(F32), axis=0, keepdims=True)
    resid = after_ref[0]
    normed, inverse_std = layer_norm(resid)
    entered = (normed * (1.0 + scale) + shift).astype(BF)
    entry[own] = entered
    downward = jnp.broadcast_to(down_bias[...], (ROWS, width))
    grad_entry = jnp.zeros((ROWS, width), F32)
    for chunk in range(chunks):
        cols = slice(chunk * width, (chunk + 1) * width)
        upward = mul(entered, up[:, cols]) + up_bias[:, cols]
        below = 0.5 + 0.5 * lax.erf(upward * 2.0 ** (-0.5))
        density = jnp.exp(-0.5 * upward * upward) * 0.3989422804014327
        acted = (upward * below).astype(BF)
        active[own, cols] = acted
        downward = downward + mul(acted, down[cols, :])
        grad_active = mul_rt(down_in, down[cols, :])
        up_in = (grad_active * (below + upward * density)).astype(BF)
        grad_up_in[own, cols] = up_in
        up_bias_out[:, cols] += jnp.sum(up_in.astype(F32), axis=0, keepdims=True)
        grad_entry = grad_entry + mul_rt(up_in, up[:, cols])
    store_near(result, inverse, resid + gate * downward, clip, first, frames)
    grad_gate = jnp.sum(grad_out * downward, axis=0, keepdims=True)
    grad_shift = jnp.sum(grad_entry, axis=0, keepdims=True)
    grad_scale = jnp.sum(grad_entry * normed, axis=0, keepdims=True)
    add_mods(mods_out, clip, (grad_shift, grad_scale, grad_gate))
    grad_ref[0] = grad_out + norm_back(grad_entry * (1.0 + scale), normed, inverse_std)

    @pl.when(step == pl.num_programs(0) - 1)
    def _():
        entry_t = entry[...].T
        copies = []
        for chunk in range(chunks):
            grad = mul(entry_t, grad_up_in[:, chunk * width : (chunk + 1) * width]).astype(BF)
            staged[chunk] = grad.reshape(shards, rows, width)
            copies.append(
                pltpu.make_async_copy(staged.at[chunk], up_out.at[:, chunk], out_sem.at[chunk])
            )
            copies[-1].start()
        group = shards // chunks
        me = inverse[source.shape[0]]
        for chunk in range(chunks):
            grad = mul_lt(active[:, chunk * width : (chunk + 1) * width], grad_down_in[...])
            slot = chunks + chunk
            staged[slot] = grad.astype(BF).reshape(shards, rows, width)
            for part in range(group):
                shard = chunk * group + part
                distance = jnp.bitwise_xor(me, shard)
                place = jnp.bitwise_and(distance, 1), lax.shift_right_logical(distance, 1)
                copies.append(
                    pltpu.make_async_copy(
                        staged.at[slot, part * chunks : (part + 1) * chunks],
                        down_out.at[place],
                        out_sem.at[chunks + shard],
                    )
                )
                copies[-1].start()
        for copy in copies:
            copy.wait()


def whole(shape):
    return pl.BlockSpec(shape, lambda *_: (0,) * len(shape))


def per_step(shape):
    return pl.BlockSpec((1,) + tuple(shape[1:]), lambda step, *_: (step,) + (0,) * (len(shape) - 1))


ANY = pl.BlockSpec(memory_space=pl.ANY)


def run(kernel, steps, table, ins, in_specs, outs, out_specs, scratch, flops, name):
    size = lambda shaped: shaped.size * shaped.dtype.itemsize
    moved = sum(size(a) for a in ins) + sum(size(a) for a in outs)
    return pl.pallas_call(
        kernel,
        grid_spec=pltpu.PrefetchScalarGridSpec(
            num_scalar_prefetch=1, grid=(steps,), in_specs=in_specs, out_specs=out_specs,
            scratch_shapes=scratch,
        ),
        out_shape=outs,
        compiler_params=pltpu.CompilerParams(
            dimension_semantics=("arbitrary",), vmem_limit_bytes=VMEM_LIMIT
        ),
        cost_estimate=pl.CostEstimate(flops=flops, bytes_accessed=moved, transcendentals=0),
        name=name,
    )(table, *ins)


def body(
    frames_in,
    cotangent,
    time_table,
    ada_weight,
    ada_bias,
    space_qkv,
    space_out,
    time_qkv,
    time_out,
    up_weight,
    up_bias,
    down_weight,
    down_bias,
    timesteps,
    task_mask,
    clip_weight,
    frame_table,
):
    shards = lax.axis_size("shard")
    shard_at = lax.axis_index("shard")
    frame_count, patches, width = frames_in.shape
    clips = timesteps.shape[0]
    frames = task_mask.shape[1]
    table = frame_table[0]
    group_frames = table.shape[0]
    columns = patches // shards
    rows = width // shards
    hidden = up_weight.shape[1]
    chunks = hidden // width
    tokens = group_frames * columns
    steps = tokens // ROWS
    shaped = jax.ShapeDtypeStruct

    def column_blocks(weight):
        return jnp.swapaxes(weight.reshape(rows, -1, width), 0, 1)

    def swap(values, distance):
        pairs = [(at, at ^ distance) for at in range(shards)]
        return lax.ppermute(values, "shard", pairs)

    def gather(packed):
        return lax.all_gather(packed[None], "shard", axis=0, tiled=True)

    groups = lax.axis_size("grp")
    group_at = lax.axis_index("grp")

    def swap_group(values, distance):
        pairs = [(at, at ^ distance) for at in range(groups)]
        return lax.ppermute(values, "grp", pairs)

    def every(values):
        stacked = jnp.zeros((groups,) + values.shape, values.dtype)
        for distance in range(groups):
            piece = swap_group(values, distance) if distance else values
            stacked = lax.dynamic_update_index_in_dim(stacked, piece, group_at ^ distance, 0)
        return stacked

    def shard_sum(values):
        distance = 1
        while distance < shards:
            values = values + swap(values, distance)
            distance *= 2
        return values

    def even_pieces(own):
        return [own] + [swap(own, distance) for distance in range(2, shards, 2)]

    def all_pieces(even):
        pieces = []
        for piece in even:
            pieces += [piece, swap(piece, 1)]
        return pieces

    own_space = jnp.concatenate([column_blocks(space_qkv), space_out[None]], axis=0)
    even = even_pieces(own_space)

    embed = jnp.take(time_table, timesteps, axis=0).astype(F32)
    cond = jax.nn.silu(embed).astype(BF)
    mod_local = jnp.dot(cond, ada_weight, preferred_element_type=F32)

    def spread(local):
        full = jnp.zeros((shards, local.shape[0]), F32)
        return lax.dynamic_update_slice_in_dim(
            full, local.astype(F32)[None], shard_at, 0
        ).reshape(-1)

    small = jnp.concatenate(
        [
            (mod_local + spread(ada_bias)[None]).reshape(-1),
            spread(up_bias),
            spread(down_bias),
        ]
    )
    small = lax.all_gather(small.reshape(1, -1, 128), "shard", axis=0, tiled=True)
    small, even[1] = lax.optimization_barrier((small, even[1]))
    small = jnp.sum(small, axis=0).reshape(-1)
    space_w = all_pieces(even)
    own_time = jnp.concatenate([column_blocks(time_qkv), time_out[None]], axis=0)
    own_feed = jnp.concatenate(
        [column_blocks(up_weight), down_weight.reshape(chunks, rows, width)], axis=0
    )
    own_time, own_feed, *_ = lax.optimization_barrier((own_time, own_feed, *even[1:]))
    time_w = all_pieces(even_pieces(own_time))
    feed_w = gather(own_feed)
    mod_size = clips * 9 * width
    modul = small[:mod_size].reshape(clips, 9, width)
    up_bias_full = small[mod_size:-width].reshape(1, hidden)
    down_bias_full = small[-width:].reshape(1, width)

    slot_ids = shard_at * frame_count + jnp.arange(frame_count, dtype=jnp.int32)
    frame_ids = jnp.take(table, slot_ids)
    clip_of = frame_ids // frames
    frame_of = frame_ids % frames
    where = jnp.concatenate([clip_of, shard_at[None].astype(jnp.int32)])
    slots = jnp.arange(group_frames, dtype=jnp.int32)
    inverse = jnp.sum(jnp.where(table[None, :] == slots[:, None], slots[None, :], 0), axis=1)
    inverse = jnp.concatenate([inverse, shard_at[None].astype(jnp.int32)])

    def exchange(parts):
        return lax.all_to_all(parts, "shard", split_axis=0, concat_axis=0, tiled=True)

    row_weights = task_mask[clip_of, frame_of].astype(F32) * clip_weight[clip_of]
    weighted = (cotangent * row_weights[:, None, None]).astype(BF)
    weighted = jnp.swapaxes(weighted.reshape(frame_count, shards, columns, width), 0, 1)
    arriving = exchange(weighted).reshape(group_frames, columns, width)

    own_shape = (shards, frame_count, columns, width)
    own_spec = pl.BlockSpec((shards, 1, columns, width), lambda step, *_: (0, step, 0, 0))
    mods_spec = whole((clips, 9, width))
    mods_out = shaped((clips, 3, width), F32)
    mods_out_spec = whole((clips, 3, width))
    grads_shape = (shards, 4, rows, width)
    split_shape = (2, shards // 2, 4, rows, width)
    weight_scratch = [
        pltpu.VMEM((width, 3 * width), BF),
        pltpu.VMEM((width, width), BF),
    ]
    dma = pltpu.SemaphoreType.DMA

    def kept(count):
        shapes = [
            shaped((count, ROWS, 3 * width), BF),
            shaped((count, ROWS, width), BF),
            shaped((count, 16, ROWS), F32),
            shaped((count, ROWS, width), BF),
        ]
        return shapes, [per_step(one.shape) for one in shapes]

    def back_scratch(count):
        return [
            pltpu.VMEM((count * ROWS, width), BF),
            pltpu.VMEM((count * ROWS, 3 * width), BF),
            pltpu.VMEM((count * ROWS, width), BF),
            pltpu.VMEM((count * ROWS, width), BF),
        ]

    mixer_flops = 2 * tokens * width * 4 * width + 4 * tokens * ROWS * width * 2
    space_keep, space_keep_specs = kept(frame_count)
    after_space, *space_kept = run(
        partial(space_forward_kernel, shards), frame_count, where,
        [frames_in, modul] + space_w,
        [per_step(frames_in.shape), mods_spec] + [ANY] * shards,
        [shaped(own_shape, BF)] + space_keep,
        [own_spec] + space_keep_specs,
        weight_scratch + [dma(())],
        mixer_flops, "space_forward",
    )
    received = exchange(after_space).reshape(group_frames, columns, width)
    own_ids = jnp.concatenate([embed, timesteps.astype(F32)[:, None]], axis=1)
    own_ids, _ = lax.optimization_barrier((own_ids, after_space))
    every_ids = every(own_ids).reshape(-1, own_ids.shape[1])

    cols_spec = whole((group_frames, columns, width))
    cols_shape = shaped((group_frames, columns, width), BF)
    block_shape = (steps, ROWS, width)
    time_keep, time_keep_specs = kept(steps)
    time_resid, after_time, *time_kept = run(
        partial(time_forward_kernel, frames, shards), steps, inverse,
        [received, modul] + time_w,
        [cols_spec, mods_spec] + [ANY] * shards,
        [shaped(block_shape, BF), shaped(block_shape, F32)] + time_keep,
        [per_step(block_shape)] * 2 + time_keep_specs,
        weight_scratch + [pltpu.VMEM((ROWS, width), F32), dma(())],
        mixer_flops, "time_forward",
    )

    result, grad_after_time, mlp_mods, grad_up_bias, grad_down_bias, up_grads, down_grads = run(
        partial(feed_kernel, frames), steps, inverse,
        [after_time, arriving, modul, up_bias_full, down_bias_full, feed_w],
        [per_step(block_shape), cols_spec, mods_spec, whole((1, hidden)), whole((1, width)), ANY],
        [
            cols_shape,
            shaped(block_shape, F32),
            mods_out,
            shaped((1, hidden), F32),
            shaped((1, width), F32),
            shaped((shards, chunks, rows, width), BF),
            shaped((2, shards // 2, chunks, rows, width), BF),
        ],
        [
            cols_spec, per_step(block_shape), mods_out_spec, whole((1, hidden)),
            whole((1, width)), ANY, ANY,
        ],
        [
            pltpu.VMEM((width, hidden), BF),
            pltpu.VMEM((hidden, width), BF),
            pltpu.VMEM((tokens, width), BF),
            pltpu.VMEM((tokens, hidden), BF),
            pltpu.VMEM((tokens, hidden), BF),
            pltpu.VMEM((tokens, width), BF),
            pltpu.VMEM((ROWS, width), F32),
            pltpu.VMEM((2 * chunks, shards, rows, width), BF),
            dma(()),
            dma((chunks + shards,)),
        ],
        6 * 2 * tokens * width * hidden, "feed",
    )

    def to_rows(moved):
        moved = jnp.swapaxes(moved.reshape(own_shape), 0, 1)
        return moved.reshape(frame_count, patches, width).astype(F32)

    def shard_total(packed):
        return lax.psum_scatter(packed, "shard", scatter_dimension=0, tiled=True)[0]

    def parts_of(share):
        parts = share.reshape(groups, -1, width)

        def part(at):
            return lax.dynamic_index_in_dim(parts, at, 0, keepdims=False)

        return [part(group_at)] + [
            swap_group(part(group_at ^ distance), distance) for distance in range(1, groups)
        ]

    def spread_parts(parts, share):
        own = parts[0].astype(F32)
        for piece in parts[1:]:
            own = own + piece.astype(F32)
        own = own.astype(BF)
        near = [own] + [swap_group(own, distance) for distance in range(1, groups)]
        step = 1
        while step < groups:
            odd = jnp.bitwise_and(group_at, step) > 0
            near = [jnp.where(odd, near[at ^ step], near[at]) for at in range(groups)]
            step *= 2
        return jnp.concatenate(near).reshape(share.shape).astype(F32)

    def total(share):
        return spread_parts(parts_of(share), share)

    far_bits = list(range(shards.bit_length() - 2))

    def halve(values, left, bit):
        axis = len(left) - 1 - left.index(bit)
        kept, sent = (lax.index_in_dim(values, side, axis, keepdims=False) for side in (0, 1))
        return (kept.astype(F32) + swap(sent, 2 << bit).astype(F32)).astype(BF)

    def near_total(grads):
        return (grads[0].astype(F32) + swap(grads[1], 1).astype(F32)).astype(BF)

    def far_start(kept):
        half = kept.shape[1] // 2
        folded = (2,) * len(far_bits)
        return [
            halve(part.reshape(folded + part.shape[1:]), far_bits, bit)
            for part, bit in ((kept[:, :half], far_bits[0]), (kept[:, half:], far_bits[-1]))
        ]

    def far_finish(parts):
        done = []
        for values, order in zip(parts, (far_bits, far_bits[::-1])):
            left = [bit for bit in far_bits if bit != order[0]]
            for bit in order[1:]:
                values = halve(values, left, bit)
                left = [other for other in left if other != bit]
            done.append(values)
        return jnp.concatenate(done, axis=0)

    up_share = shard_total(up_grads)
    down_far = far_start(near_total(down_grads))

    going, time_mods, time_grads = run(
        partial(time_backward_kernel, frames, shards), steps, inverse,
        [grad_after_time, time_resid, modul] + time_kept + time_w,
        [per_step(block_shape)] * 2 + [mods_spec] + time_keep_specs + [ANY] * shards,
        [cols_shape, mods_out, shaped(grads_shape, BF)],
        [cols_spec, mods_out_spec, whole(grads_shape)],
        weight_scratch + back_scratch(steps) + [dma(())],
        3 * mixer_flops, "time_backward",
    )
    grad_space = exchange(going.reshape(own_shape))
    up_share = lax.psum(up_share, "grp")
    time_grads, up_share, grad_space, result, *down_far = lax.optimization_barrier(
        (time_grads, up_share, grad_space, result, *down_far)
    )
    time_share = shard_total(time_grads)
    down_share = far_finish(down_far)
    arrived = exchange(result.reshape(own_shape))
    grad_rows, space_mods, space_grads = run(
        partial(space_backward_kernel, shards), frame_count, where,
        [grad_space, frames_in, modul] + space_kept + space_w,
        [own_spec, per_step(frames_in.shape), mods_spec] + space_keep_specs + [ANY] * shards,
        [shaped(frames_in.shape, F32), mods_out, shaped(split_shape, BF)],
        [per_step(frames_in.shape), mods_out_spec, whole(split_shape)],
        weight_scratch + back_scratch(frame_count) + [dma(())],
        3 * mixer_flops, "space_backward",
    )
    space_grads, space_mods, arrived, down_share = lax.optimization_barrier(
        (space_grads, space_mods, arrived, down_share)
    )
    space_near = near_total(space_grads)
    up_share = up_share.astype(F32)
    frames_out = to_rows(arrived)
    space_near, time_share = lax.optimization_barrier((space_near, time_share))
    space_far = far_start(space_near)
    space_far, space_mods = lax.optimization_barrier((space_far, space_mods))
    space_share = far_finish(space_far)
    pair = total(jnp.stack([down_share, time_share], axis=1))
    down_share, time_share = pair[:, 0], pair[:, 1]

    mod_part = jnp.concatenate([space_mods, time_mods, mlp_mods], axis=1)
    small_grads = jnp.concatenate(
        [mod_part.reshape(-1), grad_up_bias.reshape(-1), grad_down_bias.reshape(-1)]
    )
    small_grads = shard_sum(small_grads.reshape(-1, 128)).reshape(-1)
    up_dev = up_bias.shape[0]
    down_dev = down_bias.shape[0]
    bias_dev = ada_bias.shape[0]
    small_grads = jnp.concatenate(
        [
            small_grads[:mod_size],
            lax.dynamic_slice_in_dim(small_grads, mod_size + shard_at * up_dev, up_dev, 0),
            lax.dynamic_slice_in_dim(
                small_grads, mod_size + shards * up_dev + shard_at * down_dev, down_dev, 0
            ),
        ]
    )
    small_size = small_grads.shape[0]
    small_grads = jnp.pad(small_grads, (0, -small_size % 1024)).reshape(1, -1, 128)
    small_grads, space_share = lax.optimization_barrier((small_grads, space_share))
    space_share = total(space_share)
    every_small = every(small_grads).reshape(groups, -1)
    every_modul = every_small[:, :mod_size].reshape(groups * clips, 9 * width).astype(BF)
    bias_sums = jnp.sum(every_small[:, mod_size:small_size], axis=0)
    every_embed = every_ids[:, :-1]
    every_steps = every_ids[:, -1].astype(jnp.int32)
    every_cond = jax.nn.silu(every_embed).astype(BF)
    grad_ada = jnp.einsum("cd,cj->dj", every_cond, every_modul, preferred_element_type=F32)
    grad_ada_bias = lax.dynamic_slice_in_dim(
        jnp.sum(every_modul.astype(F32), axis=0), shard_at * bias_dev, bias_dev, 0
    )
    grad_cond = jnp.einsum("cj,dj->cd", every_modul, ada_weight, preferred_element_type=F32)
    _, silu_back = jax.vjp(jax.nn.silu, every_embed)
    grad_embed = silu_back(grad_cond)[0]
    vocab = time_table.shape[0]
    onehot = (jnp.arange(vocab, dtype=jnp.int32)[:, None] == every_steps[None, :]).astype(F32)
    grad_table = jnp.dot(onehot, grad_embed, precision=HIGH)

    def rows_of(blocks):
        return jnp.swapaxes(blocks, 0, 1).reshape(rows, -1)

    return (
        frames_out,
        grad_rows,
        grad_table,
        grad_ada,
        grad_ada_bias,
        rows_of(space_share[:3]),
        space_share[3],
        rows_of(time_share[:3]),
        time_share[3],
        rows_of(up_share),
        bias_sums[:up_dev],
        down_share.reshape(chunks * rows, width),
        bias_sums[up_dev:],
    )


def solution(mesh):
    placed = (
        P(("grp", "shard"), None, None),
        P(("grp", "shard"), None, None),
        P(None, "shard"),
        P("shard", None),
        P("shard"),
        P("shard", None),
        P("shard", None),
        P("shard", None),
        P("shard", None),
        P("shard", None),
        P("shard"),
        P("shard", None),
        P("shard"),
        P("grp"),
        P("grp", None),
        P("grp"),
        P("grp", None),
    )
    return jax.shard_map(
        body,
        mesh=mesh,
        in_specs=placed,
        out_specs=(
            P(("grp", "shard"), None, None),
            P(("grp", "shard"), None, None),
            P(None, "shard"),
            P("shard", None),
            P("shard"),
            P("shard", None),
            P("shard", None),
            P("shard", None),
            P("shard", None),
            P("shard", None),
            P("shard"),
            P("shard", None),
            P("shard"),
        ),
        check_vma=False,
    )
```

```python
from functools import partial

import jax
import jax.numpy as jnp
from jax import lax
from jax.experimental import pallas as pl
from jax.experimental.pallas import tpu as pltpu
from jax.sharding import PartitionSpec as P

HEADS = 12
HEAD_DIM = 64
PAIR = 2 * HEAD_DIM
ROWS = 256
NEAR = 16
HIGH = lax.Precision.HIGHEST
EPSILON = 1e-06
BF = jnp.bfloat16
F32 = jnp.float32
VMEM_LIMIT = 60 * 1024 * 1024


def layer_norm(values):
    center = values - jnp.mean(values, axis=-1, keepdims=True)
    spread = jnp.mean(center * center, axis=-1, keepdims=True)
    inverse = lax.rsqrt(spread + EPSILON)
    return (center * inverse, inverse)


def norm_back(grad_normed, normed, inverse):
    first = jnp.mean(grad_normed, axis=-1, keepdims=True)
    second = jnp.mean(grad_normed * normed, axis=-1, keepdims=True)
    return inverse * (grad_normed - first - normed * second)


def mul(left, right):
    return jnp.dot(left, right, preferred_element_type=F32)


def mul_rt(left, right):
    return lax.dot_general(left, right, (((1,), (1,)), ((), ())), preferred_element_type=F32)


def mul_lt(left, right):
    return lax.dot_general(left, right, (((0,), (0,)), ((), ())), preferred_element_type=F32)


def half_masks(value):
    lane = lax.broadcasted_iota(jnp.int32, (1, PAIR), 1)
    low = jnp.where(lane < HEAD_DIM, value, 0.0)
    return (low.astype(BF), (value - low).astype(BF))


def same_patch():
    rows = lax.broadcasted_iota(jnp.int32, (ROWS, ROWS), 0)
    cols = lax.broadcasted_iota(jnp.int32, (ROWS, ROWS), 1)
    return jnp.bitwise_and(rows, NEAR - 1) == jnp.bitwise_and(cols, NEAR - 1)


def mixer_forward(resid, mods, at, width, weight, out_weight, keep, near):
    packed_ref, mixed_ref, lse_ref, branch_ref = keep
    shift, scale, gate = mods[at : at + 1], mods[at + 1 : at + 2], mods[at + 2 : at + 3]
    normed, _ = layer_norm(resid)
    entry = (normed * (1.0 + scale) + shift).astype(BF)
    for part in range(3):
        packed_ref[0, :, part * width : (part + 1) * width] = mul(
            entry, weight[:, part * width : (part + 1) * width]
        ).astype(BF)
    same = same_patch() if near else None
    lane = lax.broadcasted_iota(jnp.int32, (ROWS, PAIR), 1)
    scaled = half_masks(HEAD_DIM ** (-0.5))
    for pair in range(HEADS // 2):
        at_q = pair * PAIR
        query = packed_ref[0, :, at_q : at_q + PAIR]
        keys = packed_ref[0, :, width + at_q : width + at_q + PAIR]
        values = packed_ref[0, :, 2 * width + at_q : 2 * width + at_q + PAIR]
        halves = []
        for half in range(2):
            scores = mul_rt(keys, query * scaled[half])
            if near:
                scores = jnp.where(same, scores, -jnp.inf)
            highest = jnp.max(scores, axis=0, keepdims=True)
            weights = jnp.exp(scores - highest)
            total = jnp.sum(weights, axis=0, keepdims=True)
            head = 2 * pair + half
            lse_ref[0, head : head + 1, :] = highest + jnp.log(total)
            probs = (weights * (1.0 / total)).astype(BF)
            halves.append(mul_lt(probs, values))
        mixed_ref[0, :, at_q : at_q + PAIR] = jnp.where(
            lane < HEAD_DIM, halves[0], halves[1]
        ).astype(BF)
    branch = mul(mixed_ref[0], out_weight[...])
    branch_ref[0] = branch.astype(BF)
    return resid + gate * branch


def mixer_backward(grad_out, resid, mods, at, width, weight, out_weight, kept, work, near):
    packed_ref, mixed_ref, lse_ref, branch_ref = kept
    entry_ref, packed_grad_ref, branch_grad_ref = work
    shift, scale, gate = mods[at : at + 1], mods[at + 1 : at + 2], mods[at + 2 : at + 3]
    grad_gate = jnp.sum(grad_out * branch_ref[0].astype(F32), axis=0, keepdims=True)
    grad_branch = (gate * grad_out).astype(BF)
    branch_grad_ref[...] = grad_branch
    grad_mixed = mul_rt(grad_branch, out_weight[...]).astype(BF)
    same = same_patch() if near else None
    lane = lax.broadcasted_iota(jnp.int32, (ROWS, PAIR), 1)
    scaled = half_masks(HEAD_DIM ** (-0.5))
    ones = half_masks(1.0)
    for pair in range(HEADS // 2):
        at_q = pair * PAIR
        query = packed_ref[0, :, at_q : at_q + PAIR]
        keys = packed_ref[0, :, width + at_q : width + at_q + PAIR]
        values = packed_ref[0, :, 2 * width + at_q : 2 * width + at_q + PAIR]
        grads = grad_mixed[:, at_q : at_q + PAIR]
        grad_query = []
        grad_keys = None
        grad_values = None
        for half in range(2):
            head = 2 * pair + half
            own_query = query * scaled[half]
            own_grads = grads * ones[half]
            scores = mul_rt(keys, own_query)
            if near:
                scores = jnp.where(same, scores, -jnp.inf)
            probs = jnp.exp(scores - lse_ref[0, head : head + 1, :])
            grad_probs = mul_rt(values, own_grads)
            inner = jnp.sum(probs * grad_probs, axis=0, keepdims=True)
            grad_scores = (probs * (grad_probs - inner)).astype(BF)
            part_values = mul(probs.astype(BF), own_grads)
            part_keys = mul(grad_scores, own_query)
            grad_query.append(mul_lt(grad_scores, keys))
            grad_keys = part_keys if half == 0 else grad_keys + part_keys
            grad_values = part_values if half == 0 else grad_values + part_values
        joined = jnp.where(lane < HEAD_DIM, grad_query[0], grad_query[1])
        packed_grad_ref[:, at_q : at_q + PAIR] = (joined * HEAD_DIM ** (-0.5)).astype(BF)
        packed_grad_ref[:, width + at_q : width + at_q + PAIR] = grad_keys.astype(BF)
        packed_grad_ref[:, 2 * width + at_q : 2 * width + at_q + PAIR] = (
            grad_values.astype(BF)
        )
    grad_entry = mul_rt(packed_grad_ref[...], weight[...])
    normed, inverse = layer_norm(resid)
    entry_ref[...] = (normed * (1.0 + scale) + shift).astype(BF)
    grad_shift = jnp.sum(grad_entry, axis=0, keepdims=True)
    grad_scale = jnp.sum(grad_entry * normed, axis=0, keepdims=True)
    grad_in = grad_out + norm_back(grad_entry * (1.0 + scale), normed, inverse)
    return grad_in, (grad_shift, grad_scale, grad_gate)


def fetch_weights(packed, places, sem):
    copies = []
    for shard in range(packed.shape[0]):
        for block in range(packed.shape[1]):
            copies.append(
                pltpu.make_async_copy(packed.at[shard, block], places(shard, block), sem)
            )
    for copy in copies:
        copy.start()
    for copy in copies:
        copy.wait()


def fetch_pieces(me, pieces, weight, out_weight, sem):
    _, rows, width = pieces[0].shape
    copies = []
    for distance, piece in enumerate(pieces):
        first = pl.multiple_of(jnp.bitwise_xor(me, distance) * rows, rows)
        for block in range(3):
            target = weight.at[pl.ds(first, rows), block * width : (block + 1) * width]
            copies.append(pltpu.make_async_copy(piece.at[block], target, sem))
        copies.append(
            pltpu.make_async_copy(piece.at[3], out_weight.at[pl.ds(first, rows), :], sem)
        )
    for copy in copies:
        copy.start()
    for copy in copies:
        copy.wait()


def mixer_weight_grads(entry, packed_grad, mixed, branch_grad, put, width):
    entry_t = entry[...].T
    for block in range(3):
        put(block, mul(entry_t, packed_grad[:, block * width : (block + 1) * width]).astype(BF))
    put(3, mul(mixed.T, branch_grad[...]).astype(BF))


def add_mods(mods_out, clip, grads):
    for at, grad in enumerate(grads):
        mods_out[clip, at : at + 1, :] += grad


def space_forward_kernel(shards, where, frames_ref, mods_ref, *refs):
    pieces = refs[:shards]
    after_ref, packed_ref, mixed_ref, lse_ref, branch_ref = refs[shards : shards + 5]
    weight, out_weight, sem = refs[shards + 5 :]
    step = pl.program_id(0)
    width = frames_ref.shape[-1]

    @pl.when(step == 0)
    def _():
        fetch_pieces(where[pl.num_programs(0)], pieces, weight, out_weight, sem)

    mods = mods_ref[where[step]]
    after = mixer_forward(
        frames_ref[0], mods, 0, width, weight, out_weight,
        (packed_ref, mixed_ref, lse_ref, branch_ref), False,
    )
    after_ref[...] = after.astype(BF).reshape(after_ref.shape)


def space_backward_kernel(
    shards, where, grad_ref, frames_ref, mods_ref, packed_ref, mixed_ref, lse_ref, branch_ref, *refs
):
    pieces = refs[:shards]
    rows_out, mods_out, grads_out = refs[shards : shards + 3]
    weight, out_weight, entry, packed_grad, mixed, branch_grad, sem = refs[shards + 3 :]
    step = pl.program_id(0)
    width = frames_ref.shape[-1]

    @pl.when(step == 0)
    def _():
        fetch_pieces(where[pl.num_programs(0)], pieces, weight, out_weight, sem)
        mods_out[...] = jnp.zeros_like(mods_out)

    clip = where[step]
    own = pl.ds(pl.multiple_of(step * ROWS, ROWS), ROWS)
    grad_out = grad_ref[...].reshape(ROWS, width).astype(F32)
    grad_in, grads = mixer_backward(
        grad_out, frames_ref[0], mods_ref[clip], 0, width, weight, out_weight,
        (packed_ref, mixed_ref, lse_ref, branch_ref),
        (entry.at[own], packed_grad.at[own], branch_grad.at[own]), False,
    )
    rows_out[0] = grad_in
    mixed[own] = mixed_ref[0]
    add_mods(mods_out, clip, grads)

    @pl.when(step == pl.num_programs(0) - 1)
    def _():
        def put(block, grad):
            grads_out[:, block] = grad.reshape(shards, width // shards, width)

        mixer_weight_grads(entry, packed_grad, mixed[...], branch_grad, put, width)


def load_near(source, inverse, resid, clip, first, frames):
    for frame in range(frames):
        values = source[inverse[clip * frames + frame], pl.ds(first, NEAR), :]
        resid[frame * NEAR : (frame + 1) * NEAR, :] = values.astype(F32)


def store_near(target, inverse, values, clip, first, frames):
    for frame in range(frames):
        own = values[frame * NEAR : (frame + 1) * NEAR]
        target[inverse[clip * frames + frame], pl.ds(first, NEAR), :] = own.astype(BF)


def block_place(columns):
    step = pl.program_id(0)
    per_clip = columns // NEAR
    clip = step // per_clip
    first = pl.multiple_of((step - clip * per_clip) * NEAR, NEAR)
    return step, clip, first


def time_forward_kernel(frames, shards, inverse, source, mods_ref, *refs):
    pieces = refs[:shards]
    resid_ref, after_ref, packed_ref, mixed_ref, lse_ref, branch_ref = refs[shards : shards + 6]
    weight, out_weight, resid, sem = refs[shards + 6 :]
    step, clip, first = block_place(source.shape[1])
    width = source.shape[-1]

    @pl.when(step == 0)
    def _():
        fetch_pieces(inverse[source.shape[0]], pieces, weight, out_weight, sem)

    load_near(source, inverse, resid, clip, first, frames)
    resid_ref[0] = resid[...].astype(BF)
    after_ref[0] = mixer_forward(
        resid[...], mods_ref[clip], 3, width, weight, out_weight,
        (packed_ref, mixed_ref, lse_ref, branch_ref), True,
    )


def time_backward_kernel(
    frames, shards, inverse, grad_ref, resid_ref, mods_ref, packed_ref, mixed_ref, lse_ref,
    branch_ref, *refs
):
    pieces = refs[:shards]
    going, mods_out, grads_out = refs[shards : shards + 3]
    weight, out_weight, entry, packed_grad, mixed, branch_grad, sem = refs[shards + 3 :]
    step, clip, first = block_place(going.shape[1])
    width = going.shape[-1]

    @pl.when(step == 0)
    def _():
        fetch_pieces(inverse[going.shape[0]], pieces, weight, out_weight, sem)
        mods_out[...] = jnp.zeros_like(mods_out)

    own = pl.ds(pl.multiple_of(step * ROWS, ROWS), ROWS)
    grad_in, grads = mixer_backward(
        grad_ref[0], resid_ref[0].astype(F32), mods_ref[clip], 3, width, weight, out_weight,
        (packed_ref, mixed_ref, lse_ref, branch_ref),
        (entry.at[own], packed_grad.at[own], branch_grad.at[own]), True,
    )
    store_near(going, inverse, grad_in, clip, first, frames)
    mixed[own] = mixed_ref[0]
    add_mods(mods_out, clip, grads)

    @pl.when(step == pl.num_programs(0) - 1)
    def _():
        def put(block, grad):
            grads_out[:, block] = grad.reshape(shards, width // shards, width)

        mixer_weight_grads(entry, packed_grad, mixed[...], branch_grad, put, width)


def feed_kernel(
    frames, inverse, after_ref, source, mods_ref, up_bias, down_bias, packed_w, result, grad_ref,
    mods_out, up_bias_out, down_bias_out, up_out, down_out, up, down, entry, active, grad_up_in,
    grad_down_in, grad_result, staged, sem, out_sem,
):
    step, clip, first = block_place(source.shape[1])
    shards, _, rows, width = packed_w.shape
    hidden = up.shape[1]
    chunks = hidden // width

    @pl.when(step == 0)
    def _():
        def places(shard, block):
            if block < chunks:
                return up.at[
                    shard * rows : (shard + 1) * rows, block * width : (block + 1) * width
                ]
            start = (shard * chunks + block - chunks) * rows
            return down.at[start : start + rows, :]

        fetch_weights(packed_w, places, sem)
        mods_out[...] = jnp.zeros_like(mods_out)
        up_bias_out[...] = jnp.zeros_like(up_bias_out)
        down_bias_out[...] = jnp.zeros_like(down_bias_out)

    own = pl.ds(pl.multiple_of(step * ROWS, ROWS), ROWS)
    mods = mods_ref[clip]
    shift, scale, gate = mods[6:7], mods[7:8], mods[8:9]
    load_near(source, inverse, grad_result, clip, first, frames)
    grad_out = grad_result[...]
    down_in = (gate * grad_out).astype(BF)
    grad_down_in[own] = down_in
    down_bias_out[...] += jnp.sum(down_in.astype(F32), axis=0, keepdims=True)
    resid = after_ref[0]
    normed, inverse_std = layer_norm(resid)
    entered = (normed * (1.0 + scale) + shift).astype(BF)
    entry[own] = entered
    downward = jnp.broadcast_to(down_bias[...], (ROWS, width))
    grad_entry = jnp.zeros((ROWS, width), F32)
    for chunk in range(chunks):
        cols = slice(chunk * width, (chunk + 1) * width)
        upward = mul(entered, up[:, cols]) + up_bias[:, cols]
        below = 0.5 + 0.5 * lax.erf(upward * 2.0 ** (-0.5))
        density = jnp.exp(-0.5 * upward * upward) * 0.3989422804014327
        acted = (upward * below).astype(BF)
        active[own, cols] = acted
        downward = downward + mul(acted, down[cols, :])
        grad_active = mul_rt(down_in, down[cols, :])
        up_in = (grad_active * (below + upward * density)).astype(BF)
        grad_up_in[own, cols] = up_in
        up_bias_out[:, cols] += jnp.sum(up_in.astype(F32), axis=0, keepdims=True)
        grad_entry = grad_entry + mul_rt(up_in, up[:, cols])
    store_near(result, inverse, resid + gate * downward, clip, first, frames)
    grad_gate = jnp.sum(grad_out * downward, axis=0, keepdims=True)
    grad_shift = jnp.sum(grad_entry, axis=0, keepdims=True)
    grad_scale = jnp.sum(grad_entry * normed, axis=0, keepdims=True)
    add_mods(mods_out, clip, (grad_shift, grad_scale, grad_gate))
    grad_ref[0] = grad_out + norm_back(grad_entry * (1.0 + scale), normed, inverse_std)

    @pl.when(step == pl.num_programs(0) - 1)
    def _():
        entry_t = entry[...].T
        copies = []
        for chunk in range(chunks):
            grad = mul(entry_t, grad_up_in[:, chunk * width : (chunk + 1) * width]).astype(BF)
            staged[chunk] = grad.reshape(shards, rows, width)
            copies.append(
                pltpu.make_async_copy(staged.at[chunk], up_out.at[:, chunk], out_sem.at[chunk])
            )
            copies[-1].start()
        group = shards // chunks
        me = inverse[source.shape[0]]
        for chunk in range(chunks):
            grad = mul_lt(active[:, chunk * width : (chunk + 1) * width], grad_down_in[...])
            slot = chunks + chunk
            staged[slot] = grad.astype(BF).reshape(shards, rows, width)
            for part in range(group):
                shard = chunk * group + part
                distance = jnp.bitwise_xor(me, shard)
                place = jnp.bitwise_and(distance, 1), lax.shift_right_logical(distance, 1)
                copies.append(
                    pltpu.make_async_copy(
                        staged.at[slot, part * chunks : (part + 1) * chunks],
                        down_out.at[place],
                        out_sem.at[chunks + shard],
                    )
                )
                copies[-1].start()
        for copy in copies:
            copy.wait()


def whole(shape):
    return pl.BlockSpec(shape, lambda *_: (0,) * len(shape))


def per_step(shape):
    return pl.BlockSpec((1,) + tuple(shape[1:]), lambda step, *_: (step,) + (0,) * (len(shape) - 1))


ANY = pl.BlockSpec(memory_space=pl.ANY)


def run(kernel, steps, table, ins, in_specs, outs, out_specs, scratch, flops, name):
    size = lambda shaped: shaped.size * shaped.dtype.itemsize
    moved = sum(size(a) for a in ins) + sum(size(a) for a in outs)
    return pl.pallas_call(
        kernel,
        grid_spec=pltpu.PrefetchScalarGridSpec(
            num_scalar_prefetch=1, grid=(steps,), in_specs=in_specs, out_specs=out_specs,
            scratch_shapes=scratch,
        ),
        out_shape=outs,
        compiler_params=pltpu.CompilerParams(
            dimension_semantics=("arbitrary",), vmem_limit_bytes=VMEM_LIMIT
        ),
        cost_estimate=pl.CostEstimate(flops=flops, bytes_accessed=moved, transcendentals=0),
        name=name,
    )(table, *ins)


def body(
    frames_in,
    cotangent,
    time_table,
    ada_weight,
    ada_bias,
    space_qkv,
    space_out,
    time_qkv,
    time_out,
    up_weight,
    up_bias,
    down_weight,
    down_bias,
    timesteps,
    task_mask,
    clip_weight,
    frame_table,
):
    shards = lax.axis_size("shard")
    shard_at = lax.axis_index("shard")
    frame_count, patches, width = frames_in.shape
    clips = timesteps.shape[0]
    frames = task_mask.shape[1]
    table = frame_table[0]
    group_frames = table.shape[0]
    columns = patches // shards
    rows = width // shards
    hidden = up_weight.shape[1]
    chunks = hidden // width
    tokens = group_frames * columns
    steps = tokens // ROWS
    shaped = jax.ShapeDtypeStruct

    def column_blocks(weight):
        return jnp.swapaxes(weight.reshape(rows, -1, width), 0, 1)

    def swap(values, distance):
        pairs = [(at, at ^ distance) for at in range(shards)]
        return lax.ppermute(values, "shard", pairs)

    def gather(packed):
        return lax.all_gather(packed[None], "shard", axis=0, tiled=True)

    groups = lax.axis_size("grp")
    group_at = lax.axis_index("grp")

    def swap_group(values, distance):
        pairs = [(at, at ^ distance) for at in range(groups)]
        return lax.ppermute(values, "grp", pairs)

    def every(values):
        stacked = jnp.zeros((groups,) + values.shape, values.dtype)
        for distance in range(groups):
            piece = swap_group(values, distance) if distance else values
            stacked = lax.dynamic_update_index_in_dim(stacked, piece, group_at ^ distance, 0)
        return stacked

    def shard_sum(values):
        distance = 1
        while distance < shards:
            values = values + swap(values, distance)
            distance *= 2
        return values

    def even_pieces(own):
        return [own] + [swap(own, distance) for distance in range(2, shards, 2)]

    def all_pieces(even):
        pieces = []
        for piece in even:
            pieces += [piece, swap(piece, 1)]
        return pieces

    own_space = jnp.concatenate([column_blocks(space_qkv), space_out[None]], axis=0)
    even = even_pieces(own_space)

    embed = jnp.take(time_table, timesteps, axis=0).astype(F32)
    cond = jax.nn.silu(embed).astype(BF)
    mod_local = jnp.dot(cond, ada_weight, preferred_element_type=F32)

    def spread(local):
        full = jnp.zeros((shards, local.shape[0]), F32)
        return lax.dynamic_update_slice_in_dim(
            full, local.astype(F32)[None], shard_at, 0
        ).reshape(-1)

    small = jnp.concatenate(
        [
            (mod_local + spread(ada_bias)[None]).reshape(-1),
            spread(up_bias),
            spread(down_bias),
        ]
    )
    small = lax.all_gather(small.reshape(1, -1, 128), "shard", axis=0, tiled=True)
    small, even[1] = lax.optimization_barrier((small, even[1]))
    small = jnp.sum(small, axis=0).reshape(-1)
    space_w = all_pieces(even)
    own_time = jnp.concatenate([column_blocks(time_qkv), time_out[None]], axis=0)
    own_feed = jnp.concatenate(
        [column_blocks(up_weight), down_weight.reshape(chunks, rows, width)], axis=0
    )
    own_time, own_feed, *_ = lax.optimization_barrier((own_time, own_feed, *even[1:]))
    time_w = all_pieces(even_pieces(own_time))
    feed_w = gather(own_feed)
    mod_size = clips * 9 * width
    modul = small[:mod_size].reshape(clips, 9, width)
    up_bias_full = small[mod_size:-width].reshape(1, hidden)
    down_bias_full = small[-width:].reshape(1, width)

    slot_ids = shard_at * frame_count + jnp.arange(frame_count, dtype=jnp.int32)
    frame_ids = jnp.take(table, slot_ids)
    clip_of = frame_ids // frames
    frame_of = frame_ids % frames
    where = jnp.concatenate([clip_of, shard_at[None].astype(jnp.int32)])
    slots = jnp.arange(group_frames, dtype=jnp.int32)
    inverse = jnp.sum(jnp.where(table[None, :] == slots[:, None], slots[None, :], 0), axis=1)
    inverse = jnp.concatenate([inverse, shard_at[None].astype(jnp.int32)])

    def exchange(parts):
        return lax.all_to_all(parts, "shard", split_axis=0, concat_axis=0, tiled=True)

    row_weights = task_mask[clip_of, frame_of].astype(F32) * clip_weight[clip_of]
    weighted = (cotangent * row_weights[:, None, None]).astype(BF)
    weighted = jnp.swapaxes(weighted.reshape(frame_count, shards, columns, width), 0, 1)
    arriving = exchange(weighted).reshape(group_frames, columns, width)

    own_shape = (shards, frame_count, columns, width)
    own_spec = pl.BlockSpec((shards, 1, columns, width), lambda step, *_: (0, step, 0, 0))
    mods_spec = whole((clips, 9, width))
    mods_out = shaped((clips, 3, width), F32)
    mods_out_spec = whole((clips, 3, width))
    grads_shape = (shards, 4, rows, width)
    weight_scratch = [
        pltpu.VMEM((width, 3 * width), BF),
        pltpu.VMEM((width, width), BF),
    ]
    dma = pltpu.SemaphoreType.DMA

    def kept(count):
        shapes = [
            shaped((count, ROWS, 3 * width), BF),
            shaped((count, ROWS, width), BF),
            shaped((count, 16, ROWS), F32),
            shaped((count, ROWS, width), BF),
        ]
        return shapes, [per_step(one.shape) for one in shapes]

    def back_scratch(count):
        return [
            pltpu.VMEM((count * ROWS, width), BF),
            pltpu.VMEM((count * ROWS, 3 * width), BF),
            pltpu.VMEM((count * ROWS, width), BF),
            pltpu.VMEM((count * ROWS, width), BF),
        ]

    mixer_flops = 2 * tokens * width * 4 * width + 4 * tokens * ROWS * width * 2
    space_keep, space_keep_specs = kept(frame_count)
    after_space, *space_kept = run(
        partial(space_forward_kernel, shards), frame_count, where,
        [frames_in, modul] + space_w,
        [per_step(frames_in.shape), mods_spec] + [ANY] * shards,
        [shaped(own_shape, BF)] + space_keep,
        [own_spec] + space_keep_specs,
        weight_scratch + [dma(())],
        mixer_flops, "space_forward",
    )
    received = exchange(after_space).reshape(group_frames, columns, width)
    own_ids = jnp.concatenate([embed, timesteps.astype(F32)[:, None]], axis=1)
    own_ids, _ = lax.optimization_barrier((own_ids, after_space))
    every_ids = every(own_ids).reshape(-1, own_ids.shape[1])

    cols_spec = whole((group_frames, columns, width))
    cols_shape = shaped((group_frames, columns, width), BF)
    block_shape = (steps, ROWS, width)
    time_keep, time_keep_specs = kept(steps)
    time_resid, after_time, *time_kept = run(
        partial(time_forward_kernel, frames, shards), steps, inverse,
        [received, modul] + time_w,
        [cols_spec, mods_spec] + [ANY] * shards,
        [shaped(block_shape, BF), shaped(block_shape, F32)] + time_keep,
        [per_step(block_shape)] * 2 + time_keep_specs,
        weight_scratch + [pltpu.VMEM((ROWS, width), F32), dma(())],
        mixer_flops, "time_forward",
    )

    result, grad_after_time, mlp_mods, grad_up_bias, grad_down_bias, up_grads, down_grads = run(
        partial(feed_kernel, frames), steps, inverse,
        [after_time, arriving, modul, up_bias_full, down_bias_full, feed_w],
        [per_step(block_shape), cols_spec, mods_spec, whole((1, hidden)), whole((1, width)), ANY],
        [
            cols_shape,
            shaped(block_shape, F32),
            mods_out,
            shaped((1, hidden), F32),
            shaped((1, width), F32),
            shaped((shards, chunks, rows, width), BF),
            shaped((2, shards // 2, chunks, rows, width), BF),
        ],
        [
            cols_spec, per_step(block_shape), mods_out_spec, whole((1, hidden)),
            whole((1, width)), ANY, ANY,
        ],
        [
            pltpu.VMEM((width, hidden), BF),
            pltpu.VMEM((hidden, width), BF),
            pltpu.VMEM((tokens, width), BF),
            pltpu.VMEM((tokens, hidden), BF),
            pltpu.VMEM((tokens, hidden), BF),
            pltpu.VMEM((tokens, width), BF),
            pltpu.VMEM((ROWS, width), F32),
            pltpu.VMEM((2 * chunks, shards, rows, width), BF),
            dma(()),
            dma((chunks + shards,)),
        ],
        6 * 2 * tokens * width * hidden, "feed",
    )

    def to_rows(moved):
        moved = jnp.swapaxes(moved.reshape(own_shape), 0, 1)
        return moved.reshape(frame_count, patches, width).astype(F32)

    def shard_total(packed):
        return lax.psum_scatter(packed, "shard", scatter_dimension=0, tiled=True)[0]

    def parts_of(share):
        parts = share.reshape(groups, -1, width)

        def part(at):
            return lax.dynamic_index_in_dim(parts, at, 0, keepdims=False)

        return [part(group_at)] + [
            swap_group(part(group_at ^ distance), distance) for distance in range(1, groups)
        ]

    def spread_parts(parts, share):
        own = parts[0].astype(F32)
        for piece in parts[1:]:
            own = own + piece.astype(F32)
        own = own.astype(BF)
        near = [own] + [swap_group(own, distance) for distance in range(1, groups)]
        step = 1
        while step < groups:
            odd = jnp.bitwise_and(group_at, step) > 0
            near = [jnp.where(odd, near[at ^ step], near[at]) for at in range(groups)]
            step *= 2
        return jnp.concatenate(near).reshape(share.shape).astype(F32)

    def total(share):
        return spread_parts(parts_of(share), share)

    far_bits = list(range(shards.bit_length() - 2))

    def halve(values, left, bit):
        axis = len(left) - 1 - left.index(bit)
        kept, sent = (lax.index_in_dim(values, side, axis, keepdims=False) for side in (0, 1))
        return (kept.astype(F32) + swap(sent, 2 << bit).astype(F32)).astype(BF)

    def near_total(grads):
        return (grads[0].astype(F32) + swap(grads[1], 1).astype(F32)).astype(BF)

    def far_start(kept):
        half = kept.shape[1] // 2
        folded = (2,) * len(far_bits)
        return [
            halve(part.reshape(folded + part.shape[1:]), far_bits, bit)
            for part, bit in ((kept[:, :half], far_bits[0]), (kept[:, half:], far_bits[-1]))
        ]

    def far_finish(parts):
        done = []
        for values, order in zip(parts, (far_bits, far_bits[::-1])):
            left = [bit for bit in far_bits if bit != order[0]]
            for bit in order[1:]:
                values = halve(values, left, bit)
                left = [other for other in left if other != bit]
            done.append(values)
        return jnp.concatenate(done, axis=0)

    up_share = shard_total(up_grads)
    down_far = far_start(near_total(down_grads))

    going, time_mods, time_grads = run(
        partial(time_backward_kernel, frames, shards), steps, inverse,
        [grad_after_time, time_resid, modul] + time_kept + time_w,
        [per_step(block_shape)] * 2 + [mods_spec] + time_keep_specs + [ANY] * shards,
        [cols_shape, mods_out, shaped(grads_shape, BF)],
        [cols_spec, mods_out_spec, whole(grads_shape)],
        weight_scratch + back_scratch(steps) + [dma(())],
        3 * mixer_flops, "time_backward",
    )
    grad_space = exchange(going.reshape(own_shape))
    time_grads, up_share, grad_space, result, *down_far = lax.optimization_barrier(
        (time_grads, up_share, grad_space, result, *down_far)
    )
    time_share = shard_total(time_grads)
    up_parts = parts_of(up_share)
    down_share = far_finish(down_far)
    arrived = exchange(result.reshape(own_shape))
    grad_rows, space_mods, space_grads = run(
        partial(space_backward_kernel, shards), frame_count, where,
        [grad_space, frames_in, modul] + space_kept + space_w,
        [own_spec, per_step(frames_in.shape), mods_spec] + space_keep_specs + [ANY] * shards,
        [shaped(frames_in.shape, F32), mods_out, shaped(grads_shape, BF)],
        [per_step(frames_in.shape), mods_out_spec, whole(grads_shape)],
        weight_scratch + back_scratch(frame_count) + [dma(())],
        3 * mixer_flops, "space_backward",
    )
    space_grads, space_mods, arrived, down_share, *up_parts = lax.optimization_barrier(
        (space_grads, space_mods, arrived, down_share, *up_parts)
    )
    space_share = shard_total(space_grads)
    up_share = spread_parts(up_parts, up_share)
    frames_out = to_rows(arrived)
    pair = jnp.stack([down_share, time_share], axis=1)
    pair_parts = parts_of(pair)

    mod_part = jnp.concatenate([space_mods, time_mods, mlp_mods], axis=1)
    small_grads = jnp.concatenate(
        [mod_part.reshape(-1), grad_up_bias.reshape(-1), grad_down_bias.reshape(-1)]
    )
    small_grads = shard_sum(small_grads.reshape(-1, 128)).reshape(-1)
    up_dev = up_bias.shape[0]
    down_dev = down_bias.shape[0]
    bias_dev = ada_bias.shape[0]
    small_grads = jnp.concatenate(
        [
            small_grads[:mod_size],
            lax.dynamic_slice_in_dim(small_grads, mod_size + shard_at * up_dev, up_dev, 0),
            lax.dynamic_slice_in_dim(
                small_grads, mod_size + shards * up_dev + shard_at * down_dev, down_dev, 0
            ),
        ]
    )
    small_size = small_grads.shape[0]
    small_grads = jnp.pad(small_grads, (0, -small_size % 1024)).reshape(1, -1, 128)
    small_grads, pair_parts = lax.optimization_barrier((small_grads, pair_parts))
    pair = spread_parts(pair_parts, pair)
    down_share, time_share = pair[:, 0], pair[:, 1]
    space_share = total(space_share)
    every_small = every(small_grads).reshape(groups, -1)
    every_modul = every_small[:, :mod_size].reshape(groups * clips, 9 * width).astype(BF)
    bias_sums = jnp.sum(every_small[:, mod_size:small_size], axis=0)
    every_embed = every_ids[:, :-1]
    every_steps = every_ids[:, -1].astype(jnp.int32)
    every_cond = jax.nn.silu(every_embed).astype(BF)
    grad_ada = jnp.einsum("cd,cj->dj", every_cond, every_modul, preferred_element_type=F32)
    grad_ada_bias = lax.dynamic_slice_in_dim(
        jnp.sum(every_modul.astype(F32), axis=0), shard_at * bias_dev, bias_dev, 0
    )
    grad_cond = jnp.einsum("cj,dj->cd", every_modul, ada_weight, preferred_element_type=F32)
    _, silu_back = jax.vjp(jax.nn.silu, every_embed)
    grad_embed = silu_back(grad_cond)[0]
    vocab = time_table.shape[0]
    onehot = (jnp.arange(vocab, dtype=jnp.int32)[:, None] == every_steps[None, :]).astype(F32)
    grad_table = jnp.dot(onehot, grad_embed, precision=HIGH)

    def rows_of(blocks):
        return jnp.swapaxes(blocks, 0, 1).reshape(rows, -1)

    return (
        frames_out,
        grad_rows,
        grad_table,
        grad_ada,
        grad_ada_bias,
        rows_of(space_share[:3]),
        space_share[3],
        rows_of(time_share[:3]),
        time_share[3],
        rows_of(up_share),
        bias_sums[:up_dev],
        down_share.reshape(chunks * rows, width),
        bias_sums[up_dev:],
    )


def solution(mesh):
    placed = (
        P(("grp", "shard"), None, None),
        P(("grp", "shard"), None, None),
        P(None, "shard"),
        P("shard", None),
        P("shard"),
        P("shard", None),
        P("shard", None),
        P("shard", None),
        P("shard", None),
        P("shard", None),
        P("shard"),
        P("shard", None),
        P("shard"),
        P("grp"),
        P("grp", None),
        P("grp"),
        P("grp", None),
    )
    return jax.shard_map(
        body,
        mesh=mesh,
        in_specs=placed,
        out_specs=(
            P(("grp", "shard"), None, None),
            P(("grp", "shard"), None, None),
            P(None, "shard"),
            P("shard", None),
            P("shard"),
            P("shard", None),
            P("shard", None),
            P("shard", None),
            P("shard", None),
            P("shard", None),
            P("shard"),
            P("shard", None),
            P("shard"),
        ),
        check_vma=False,
    )
```

```python
from functools import partial

import jax
import jax.numpy as jnp
from jax import lax
from jax.experimental import pallas as pl
from jax.experimental.pallas import tpu as pltpu
from jax.sharding import PartitionSpec as P

HEADS = 12
HEAD_DIM = 64
PAIR = 2 * HEAD_DIM
ROWS = 256
NEAR = 16
HIGH = lax.Precision.HIGHEST
EPSILON = 1e-06
BF = jnp.bfloat16
F32 = jnp.float32
VMEM_LIMIT = 60 * 1024 * 1024


def layer_norm(values):
    center = values - jnp.mean(values, axis=-1, keepdims=True)
    spread = jnp.mean(center * center, axis=-1, keepdims=True)
    inverse = lax.rsqrt(spread + EPSILON)
    return (center * inverse, inverse)


def norm_back(grad_normed, normed, inverse):
    first = jnp.mean(grad_normed, axis=-1, keepdims=True)
    second = jnp.mean(grad_normed * normed, axis=-1, keepdims=True)
    return inverse * (grad_normed - first - normed * second)


def mul(left, right):
    return jnp.dot(left, right, preferred_element_type=F32)


def mul_rt(left, right):
    return lax.dot_general(left, right, (((1,), (1,)), ((), ())), preferred_element_type=F32)


def mul_lt(left, right):
    return lax.dot_general(left, right, (((0,), (0,)), ((), ())), preferred_element_type=F32)


def half_masks(value):
    lane = lax.broadcasted_iota(jnp.int32, (1, PAIR), 1)
    low = jnp.where(lane < HEAD_DIM, value, 0.0)
    return (low.astype(BF), (value - low).astype(BF))


def same_patch():
    rows = lax.broadcasted_iota(jnp.int32, (ROWS, ROWS), 0)
    cols = lax.broadcasted_iota(jnp.int32, (ROWS, ROWS), 1)
    return jnp.bitwise_and(rows, NEAR - 1) == jnp.bitwise_and(cols, NEAR - 1)


def mixer_forward(resid, mods, at, width, weight, out_weight, keep, near):
    packed_ref, mixed_ref, lse_ref, branch_ref = keep
    shift, scale, gate = mods[at : at + 1], mods[at + 1 : at + 2], mods[at + 2 : at + 3]
    normed, _ = layer_norm(resid)
    entry = (normed * (1.0 + scale) + shift).astype(BF)
    for part in range(3):
        packed_ref[0, :, part * width : (part + 1) * width] = mul(
            entry, weight[:, part * width : (part + 1) * width]
        ).astype(BF)
    same = same_patch() if near else None
    lane = lax.broadcasted_iota(jnp.int32, (ROWS, PAIR), 1)
    scaled = half_masks(HEAD_DIM ** (-0.5))
    for pair in range(HEADS // 2):
        at_q = pair * PAIR
        query = packed_ref[0, :, at_q : at_q + PAIR]
        keys = packed_ref[0, :, width + at_q : width + at_q + PAIR]
        values = packed_ref[0, :, 2 * width + at_q : 2 * width + at_q + PAIR]
        halves = []
        for half in range(2):
            scores = mul_rt(keys, query * scaled[half])
            if near:
                scores = jnp.where(same, scores, -jnp.inf)
            highest = jnp.max(scores, axis=0, keepdims=True)
            weights = jnp.exp(scores - highest)
            total = jnp.sum(weights, axis=0, keepdims=True)
            head = 2 * pair + half
            lse_ref[0, head : head + 1, :] = highest + jnp.log(total)
            probs = (weights * (1.0 / total)).astype(BF)
            halves.append(mul_lt(probs, values))
        mixed_ref[0, :, at_q : at_q + PAIR] = jnp.where(
            lane < HEAD_DIM, halves[0], halves[1]
        ).astype(BF)
    branch = mul(mixed_ref[0], out_weight[...])
    branch_ref[0] = branch.astype(BF)
    return resid + gate * branch


def mixer_backward(grad_out, resid, mods, at, width, weight, out_weight, kept, work, near):
    packed_ref, mixed_ref, lse_ref, branch_ref = kept
    entry_ref, packed_grad_ref, branch_grad_ref = work
    shift, scale, gate = mods[at : at + 1], mods[at + 1 : at + 2], mods[at + 2 : at + 3]
    grad_gate = jnp.sum(grad_out * branch_ref[0].astype(F32), axis=0, keepdims=True)
    grad_branch = (gate * grad_out).astype(BF)
    branch_grad_ref[...] = grad_branch
    grad_mixed = mul_rt(grad_branch, out_weight[...]).astype(BF)
    same = same_patch() if near else None
    lane = lax.broadcasted_iota(jnp.int32, (ROWS, PAIR), 1)
    scaled = half_masks(HEAD_DIM ** (-0.5))
    ones = half_masks(1.0)
    for pair in range(HEADS // 2):
        at_q = pair * PAIR
        query = packed_ref[0, :, at_q : at_q + PAIR]
        keys = packed_ref[0, :, width + at_q : width + at_q + PAIR]
        values = packed_ref[0, :, 2 * width + at_q : 2 * width + at_q + PAIR]
        grads = grad_mixed[:, at_q : at_q + PAIR]
        grad_query = []
        grad_keys = None
        grad_values = None
        for half in range(2):
            head = 2 * pair + half
            own_query = query * scaled[half]
            own_grads = grads * ones[half]
            scores = mul_rt(keys, own_query)
            if near:
                scores = jnp.where(same, scores, -jnp.inf)
            probs = jnp.exp(scores - lse_ref[0, head : head + 1, :])
            grad_probs = mul_rt(values, own_grads)
            inner = jnp.sum(probs * grad_probs, axis=0, keepdims=True)
            grad_scores = (probs * (grad_probs - inner)).astype(BF)
            part_values = mul(probs.astype(BF), own_grads)
            part_keys = mul(grad_scores, own_query)
            grad_query.append(mul_lt(grad_scores, keys))
            grad_keys = part_keys if half == 0 else grad_keys + part_keys
            grad_values = part_values if half == 0 else grad_values + part_values
        joined = jnp.where(lane < HEAD_DIM, grad_query[0], grad_query[1])
        packed_grad_ref[:, at_q : at_q + PAIR] = (joined * HEAD_DIM ** (-0.5)).astype(BF)
        packed_grad_ref[:, width + at_q : width + at_q + PAIR] = grad_keys.astype(BF)
        packed_grad_ref[:, 2 * width + at_q : 2 * width + at_q + PAIR] = (
            grad_values.astype(BF)
        )
    grad_entry = mul_rt(packed_grad_ref[...], weight[...])
    normed, inverse = layer_norm(resid)
    entry_ref[...] = (normed * (1.0 + scale) + shift).astype(BF)
    grad_shift = jnp.sum(grad_entry, axis=0, keepdims=True)
    grad_scale = jnp.sum(grad_entry * normed, axis=0, keepdims=True)
    grad_in = grad_out + norm_back(grad_entry * (1.0 + scale), normed, inverse)
    return grad_in, (grad_shift, grad_scale, grad_gate)


def fetch_weights(packed, places, sem):
    copies = []
    for shard in range(packed.shape[0]):
        for block in range(packed.shape[1]):
            copies.append(
                pltpu.make_async_copy(packed.at[shard, block], places(shard, block), sem)
            )
    for copy in copies:
        copy.start()
    for copy in copies:
        copy.wait()


def fetch_pieces(me, pieces, weight, out_weight, sem):
    _, rows, width = pieces[0].shape
    copies = []
    for distance, piece in enumerate(pieces):
        first = pl.multiple_of(jnp.bitwise_xor(me, distance) * rows, rows)
        for block in range(3):
            target = weight.at[pl.ds(first, rows), block * width : (block + 1) * width]
            copies.append(pltpu.make_async_copy(piece.at[block], target, sem))
        copies.append(
            pltpu.make_async_copy(piece.at[3], out_weight.at[pl.ds(first, rows), :], sem)
        )
    for copy in copies:
        copy.start()
    for copy in copies:
        copy.wait()


def mixer_weight_grads(entry, packed_grad, mixed, branch_grad, put, width):
    entry_t = entry[...].T
    for block in range(3):
        put(block, mul(entry_t, packed_grad[:, block * width : (block + 1) * width]).astype(BF))
    put(3, mul(mixed.T, branch_grad[...]).astype(BF))


def add_mods(mods_out, clip, grads):
    for at, grad in enumerate(grads):
        mods_out[clip, at : at + 1, :] += grad


def space_forward_kernel(shards, where, frames_ref, mods_ref, *refs):
    pieces = refs[:shards]
    after_ref, packed_ref, mixed_ref, lse_ref, branch_ref = refs[shards : shards + 5]
    weight, out_weight, sem = refs[shards + 5 :]
    step = pl.program_id(0)
    width = frames_ref.shape[-1]

    @pl.when(step == 0)
    def _():
        fetch_pieces(where[pl.num_programs(0)], pieces, weight, out_weight, sem)

    mods = mods_ref[where[step]]
    after = mixer_forward(
        frames_ref[0], mods, 0, width, weight, out_weight,
        (packed_ref, mixed_ref, lse_ref, branch_ref), False,
    )
    after_ref[...] = after.astype(BF).reshape(after_ref.shape)


def space_backward_kernel(
    shards, where, grad_ref, frames_ref, mods_ref, packed_ref, mixed_ref, lse_ref, branch_ref, *refs
):
    pieces = refs[:shards]
    rows_out, mods_out, grads_out = refs[shards : shards + 3]
    weight, out_weight, entry, packed_grad, mixed, branch_grad, sem = refs[shards + 3 :]
    step = pl.program_id(0)
    width = frames_ref.shape[-1]

    @pl.when(step == 0)
    def _():
        fetch_pieces(where[pl.num_programs(0)], pieces, weight, out_weight, sem)
        mods_out[...] = jnp.zeros_like(mods_out)

    clip = where[step]
    own = pl.ds(pl.multiple_of(step * ROWS, ROWS), ROWS)
    grad_out = grad_ref[...].reshape(ROWS, width).astype(F32)
    grad_in, grads = mixer_backward(
        grad_out, frames_ref[0], mods_ref[clip], 0, width, weight, out_weight,
        (packed_ref, mixed_ref, lse_ref, branch_ref),
        (entry.at[own], packed_grad.at[own], branch_grad.at[own]), False,
    )
    rows_out[0] = grad_in
    mixed[own] = mixed_ref[0]
    add_mods(mods_out, clip, grads)

    @pl.when(step == pl.num_programs(0) - 1)
    def _():
        def put(block, grad):
            grads_out[:, block] = grad.reshape(shards, width // shards, width)

        mixer_weight_grads(entry, packed_grad, mixed[...], branch_grad, put, width)


def load_near(source, inverse, resid, clip, first, frames):
    for frame in range(frames):
        values = source[inverse[clip * frames + frame], pl.ds(first, NEAR), :]
        resid[frame * NEAR : (frame + 1) * NEAR, :] = values.astype(F32)


def store_near(target, inverse, values, clip, first, frames):
    for frame in range(frames):
        own = values[frame * NEAR : (frame + 1) * NEAR]
        target[inverse[clip * frames + frame], pl.ds(first, NEAR), :] = own.astype(BF)


def block_place(columns):
    step = pl.program_id(0)
    per_clip = columns // NEAR
    clip = step // per_clip
    first = pl.multiple_of((step - clip * per_clip) * NEAR, NEAR)
    return step, clip, first


def time_forward_kernel(frames, shards, inverse, source, mods_ref, *refs):
    pieces = refs[:shards]
    resid_ref, after_ref, packed_ref, mixed_ref, lse_ref, branch_ref = refs[shards : shards + 6]
    weight, out_weight, resid, sem = refs[shards + 6 :]
    step, clip, first = block_place(source.shape[1])
    width = source.shape[-1]

    @pl.when(step == 0)
    def _():
        fetch_pieces(inverse[source.shape[0]], pieces, weight, out_weight, sem)

    load_near(source, inverse, resid, clip, first, frames)
    resid_ref[0] = resid[...].astype(BF)
    after_ref[0] = mixer_forward(
        resid[...], mods_ref[clip], 3, width, weight, out_weight,
        (packed_ref, mixed_ref, lse_ref, branch_ref), True,
    )


def time_backward_kernel(
    frames, shards, inverse, grad_ref, resid_ref, mods_ref, packed_ref, mixed_ref, lse_ref,
    branch_ref, *refs
):
    pieces = refs[:shards]
    going, mods_out, grads_out = refs[shards : shards + 3]
    weight, out_weight, entry, packed_grad, mixed, branch_grad, sem = refs[shards + 3 :]
    step, clip, first = block_place(going.shape[1])
    width = going.shape[-1]

    @pl.when(step == 0)
    def _():
        fetch_pieces(inverse[going.shape[0]], pieces, weight, out_weight, sem)
        mods_out[...] = jnp.zeros_like(mods_out)

    own = pl.ds(pl.multiple_of(step * ROWS, ROWS), ROWS)
    grad_in, grads = mixer_backward(
        grad_ref[0], resid_ref[0].astype(F32), mods_ref[clip], 3, width, weight, out_weight,
        (packed_ref, mixed_ref, lse_ref, branch_ref),
        (entry.at[own], packed_grad.at[own], branch_grad.at[own]), True,
    )
    store_near(going, inverse, grad_in, clip, first, frames)
    mixed[own] = mixed_ref[0]
    add_mods(mods_out, clip, grads)

    @pl.when(step == pl.num_programs(0) - 1)
    def _():
        def put(block, grad):
            grads_out[:, block] = grad.reshape(shards, width // shards, width)

        mixer_weight_grads(entry, packed_grad, mixed[...], branch_grad, put, width)


def feed_kernel(
    frames, inverse, after_ref, source, mods_ref, up_bias, down_bias, packed_w, result, grad_ref,
    mods_out, up_bias_out, down_bias_out, up_out, down_out, up, down, entry, active, grad_up_in,
    grad_down_in, grad_result, staged, sem, out_sem,
):
    step, clip, first = block_place(source.shape[1])
    shards, _, rows, width = packed_w.shape
    hidden = up.shape[1]
    chunks = hidden // width

    @pl.when(step == 0)
    def _():
        def places(shard, block):
            if block < chunks:
                return up.at[
                    shard * rows : (shard + 1) * rows, block * width : (block + 1) * width
                ]
            start = (shard * chunks + block - chunks) * rows
            return down.at[start : start + rows, :]

        fetch_weights(packed_w, places, sem)
        mods_out[...] = jnp.zeros_like(mods_out)
        up_bias_out[...] = jnp.zeros_like(up_bias_out)
        down_bias_out[...] = jnp.zeros_like(down_bias_out)

    own = pl.ds(pl.multiple_of(step * ROWS, ROWS), ROWS)
    mods = mods_ref[clip]
    shift, scale, gate = mods[6:7], mods[7:8], mods[8:9]
    load_near(source, inverse, grad_result, clip, first, frames)
    grad_out = grad_result[...]
    down_in = (gate * grad_out).astype(BF)
    grad_down_in[own] = down_in
    down_bias_out[...] += jnp.sum(down_in.astype(F32), axis=0, keepdims=True)
    resid = after_ref[0]
    normed, inverse_std = layer_norm(resid)
    entered = (normed * (1.0 + scale) + shift).astype(BF)
    entry[own] = entered
    downward = jnp.broadcast_to(down_bias[...], (ROWS, width))
    grad_entry = jnp.zeros((ROWS, width), F32)
    for chunk in range(chunks):
        cols = slice(chunk * width, (chunk + 1) * width)
        upward = mul(entered, up[:, cols]) + up_bias[:, cols]
        below = 0.5 + 0.5 * lax.erf(upward * 2.0 ** (-0.5))
        density = jnp.exp(-0.5 * upward * upward) * 0.3989422804014327
        acted = (upward * below).astype(BF)
        active[own, cols] = acted
        downward = downward + mul(acted, down[cols, :])
        grad_active = mul_rt(down_in, down[cols, :])
        up_in = (grad_active * (below + upward * density)).astype(BF)
        grad_up_in[own, cols] = up_in
        up_bias_out[:, cols] += jnp.sum(up_in.astype(F32), axis=0, keepdims=True)
        grad_entry = grad_entry + mul_rt(up_in, up[:, cols])
    store_near(result, inverse, resid + gate * downward, clip, first, frames)
    grad_gate = jnp.sum(grad_out * downward, axis=0, keepdims=True)
    grad_shift = jnp.sum(grad_entry, axis=0, keepdims=True)
    grad_scale = jnp.sum(grad_entry * normed, axis=0, keepdims=True)
    add_mods(mods_out, clip, (grad_shift, grad_scale, grad_gate))
    grad_ref[0] = grad_out + norm_back(grad_entry * (1.0 + scale), normed, inverse_std)

    @pl.when(step == pl.num_programs(0) - 1)
    def _():
        entry_t = entry[...].T
        copies = []
        for chunk in range(chunks):
            grad = mul(entry_t, grad_up_in[:, chunk * width : (chunk + 1) * width]).astype(BF)
            staged[chunk] = grad.reshape(shards, rows, width)
            copies.append(
                pltpu.make_async_copy(staged.at[chunk], up_out.at[:, chunk], out_sem.at[chunk])
            )
            copies[-1].start()
        group = shards // chunks
        me = inverse[source.shape[0]]
        for chunk in range(chunks):
            grad = mul_lt(active[:, chunk * width : (chunk + 1) * width], grad_down_in[...])
            slot = chunks + chunk
            staged[slot] = grad.astype(BF).reshape(shards, rows, width)
            for part in range(group):
                shard = chunk * group + part
                distance = jnp.bitwise_xor(me, shard)
                place = jnp.bitwise_and(distance, 1), lax.shift_right_logical(distance, 1)
                copies.append(
                    pltpu.make_async_copy(
                        staged.at[slot, part * chunks : (part + 1) * chunks],
                        down_out.at[place],
                        out_sem.at[chunks + shard],
                    )
                )
                copies[-1].start()
        for copy in copies:
            copy.wait()


def whole(shape):
    return pl.BlockSpec(shape, lambda *_: (0,) * len(shape))


def per_step(shape):
    return pl.BlockSpec((1,) + tuple(shape[1:]), lambda step, *_: (step,) + (0,) * (len(shape) - 1))


ANY = pl.BlockSpec(memory_space=pl.ANY)


def run(kernel, steps, table, ins, in_specs, outs, out_specs, scratch, flops, name):
    size = lambda shaped: shaped.size * shaped.dtype.itemsize
    moved = sum(size(a) for a in ins) + sum(size(a) for a in outs)
    return pl.pallas_call(
        kernel,
        grid_spec=pltpu.PrefetchScalarGridSpec(
            num_scalar_prefetch=1, grid=(steps,), in_specs=in_specs, out_specs=out_specs,
            scratch_shapes=scratch,
        ),
        out_shape=outs,
        compiler_params=pltpu.CompilerParams(
            dimension_semantics=("arbitrary",), vmem_limit_bytes=VMEM_LIMIT
        ),
        cost_estimate=pl.CostEstimate(flops=flops, bytes_accessed=moved, transcendentals=0),
        name=name,
    )(table, *ins)


def body(
    frames_in,
    cotangent,
    time_table,
    ada_weight,
    ada_bias,
    space_qkv,
    space_out,
    time_qkv,
    time_out,
    up_weight,
    up_bias,
    down_weight,
    down_bias,
    timesteps,
    task_mask,
    clip_weight,
    frame_table,
):
    shards = lax.axis_size("shard")
    shard_at = lax.axis_index("shard")
    frame_count, patches, width = frames_in.shape
    clips = timesteps.shape[0]
    frames = task_mask.shape[1]
    table = frame_table[0]
    group_frames = table.shape[0]
    columns = patches // shards
    rows = width // shards
    hidden = up_weight.shape[1]
    chunks = hidden // width
    tokens = group_frames * columns
    steps = tokens // ROWS
    shaped = jax.ShapeDtypeStruct

    def column_blocks(weight):
        return jnp.swapaxes(weight.reshape(rows, -1, width), 0, 1)

    def swap(values, distance):
        pairs = [(at, at ^ distance) for at in range(shards)]
        return lax.ppermute(values, "shard", pairs)

    def gather(packed):
        return lax.all_gather(packed[None], "shard", axis=0, tiled=True)

    groups = lax.axis_size("grp")
    group_at = lax.axis_index("grp")

    def swap_group(values, distance):
        pairs = [(at, at ^ distance) for at in range(groups)]
        return lax.ppermute(values, "grp", pairs)

    def every(values):
        stacked = jnp.zeros((groups,) + values.shape, values.dtype)
        for distance in range(groups):
            piece = swap_group(values, distance) if distance else values
            stacked = lax.dynamic_update_index_in_dim(stacked, piece, group_at ^ distance, 0)
        return stacked

    def shard_sum(values):
        distance = 1
        while distance < shards:
            values = values + swap(values, distance)
            distance *= 2
        return values

    def even_pieces(own):
        return [own] + [swap(own, distance) for distance in range(2, shards, 2)]

    def all_pieces(even):
        pieces = []
        for piece in even:
            pieces += [piece, swap(piece, 1)]
        return pieces

    own_space = jnp.concatenate([column_blocks(space_qkv), space_out[None]], axis=0)
    even = even_pieces(own_space)

    embed = jnp.take(time_table, timesteps, axis=0).astype(F32)
    cond = jax.nn.silu(embed).astype(BF)
    mod_local = jnp.dot(cond, ada_weight, preferred_element_type=F32)

    def spread(local):
        full = jnp.zeros((shards, local.shape[0]), F32)
        return lax.dynamic_update_slice_in_dim(
            full, local.astype(F32)[None], shard_at, 0
        ).reshape(-1)

    small = jnp.concatenate(
        [
            (mod_local + spread(ada_bias)[None]).reshape(-1),
            spread(up_bias),
            spread(down_bias),
        ]
    )
    small = lax.all_gather(small.reshape(1, -1, 128), "shard", axis=0, tiled=True)
    small, even[1] = lax.optimization_barrier((small, even[1]))
    small = jnp.sum(small, axis=0).reshape(-1)
    space_w = all_pieces(even)
    own_time = jnp.concatenate([column_blocks(time_qkv), time_out[None]], axis=0)
    own_feed = jnp.concatenate(
        [column_blocks(up_weight), down_weight.reshape(chunks, rows, width)], axis=0
    )
    own_time, own_feed, *_ = lax.optimization_barrier((own_time, own_feed, *even[1:]))
    time_w = all_pieces(even_pieces(own_time))
    feed_w = gather(own_feed)
    mod_size = clips * 9 * width
    modul = small[:mod_size].reshape(clips, 9, width)
    up_bias_full = small[mod_size:-width].reshape(1, hidden)
    down_bias_full = small[-width:].reshape(1, width)

    slot_ids = shard_at * frame_count + jnp.arange(frame_count, dtype=jnp.int32)
    frame_ids = jnp.take(table, slot_ids)
    clip_of = frame_ids // frames
    frame_of = frame_ids % frames
    where = jnp.concatenate([clip_of, shard_at[None].astype(jnp.int32)])
    slots = jnp.arange(group_frames, dtype=jnp.int32)
    inverse = jnp.sum(jnp.where(table[None, :] == slots[:, None], slots[None, :], 0), axis=1)
    inverse = jnp.concatenate([inverse, shard_at[None].astype(jnp.int32)])

    def exchange(parts):
        return lax.all_to_all(parts, "shard", split_axis=0, concat_axis=0, tiled=True)

    row_weights = task_mask[clip_of, frame_of].astype(F32) * clip_weight[clip_of]
    weighted = (cotangent * row_weights[:, None, None]).astype(BF)
    weighted = jnp.swapaxes(weighted.reshape(frame_count, shards, columns, width), 0, 1)
    arriving = exchange(weighted).reshape(group_frames, columns, width)

    own_shape = (shards, frame_count, columns, width)
    own_spec = pl.BlockSpec((shards, 1, columns, width), lambda step, *_: (0, step, 0, 0))
    mods_spec = whole((clips, 9, width))
    mods_out = shaped((clips, 3, width), F32)
    mods_out_spec = whole((clips, 3, width))
    grads_shape = (shards, 4, rows, width)
    weight_scratch = [
        pltpu.VMEM((width, 3 * width), BF),
        pltpu.VMEM((width, width), BF),
    ]
    dma = pltpu.SemaphoreType.DMA

    def kept(count):
        shapes = [
            shaped((count, ROWS, 3 * width), BF),
            shaped((count, ROWS, width), BF),
            shaped((count, 16, ROWS), F32),
            shaped((count, ROWS, width), BF),
        ]
        return shapes, [per_step(one.shape) for one in shapes]

    def back_scratch(count):
        return [
            pltpu.VMEM((count * ROWS, width), BF),
            pltpu.VMEM((count * ROWS, 3 * width), BF),
            pltpu.VMEM((count * ROWS, width), BF),
            pltpu.VMEM((count * ROWS, width), BF),
        ]

    mixer_flops = 2 * tokens * width * 4 * width + 4 * tokens * ROWS * width * 2
    space_keep, space_keep_specs = kept(frame_count)
    after_space, *space_kept = run(
        partial(space_forward_kernel, shards), frame_count, where,
        [frames_in, modul] + space_w,
        [per_step(frames_in.shape), mods_spec] + [ANY] * shards,
        [shaped(own_shape, BF)] + space_keep,
        [own_spec] + space_keep_specs,
        weight_scratch + [dma(())],
        mixer_flops, "space_forward",
    )
    received = exchange(after_space).reshape(group_frames, columns, width)
    own_ids = jnp.concatenate([embed, timesteps.astype(F32)[:, None]], axis=1)
    own_ids, _ = lax.optimization_barrier((own_ids, after_space))
    every_ids = every(own_ids).reshape(-1, own_ids.shape[1])
    received, every_ids = lax.optimization_barrier((received, every_ids))

    cols_spec = whole((group_frames, columns, width))
    cols_shape = shaped((group_frames, columns, width), BF)
    block_shape = (steps, ROWS, width)
    time_keep, time_keep_specs = kept(steps)
    time_resid, after_time, *time_kept = run(
        partial(time_forward_kernel, frames, shards), steps, inverse,
        [received, modul] + time_w,
        [cols_spec, mods_spec] + [ANY] * shards,
        [shaped(block_shape, BF), shaped(block_shape, F32)] + time_keep,
        [per_step(block_shape)] * 2 + time_keep_specs,
        weight_scratch + [pltpu.VMEM((ROWS, width), F32), dma(())],
        mixer_flops, "time_forward",
    )

    result, grad_after_time, mlp_mods, grad_up_bias, grad_down_bias, up_grads, down_grads = run(
        partial(feed_kernel, frames), steps, inverse,
        [after_time, arriving, modul, up_bias_full, down_bias_full, feed_w],
        [per_step(block_shape), cols_spec, mods_spec, whole((1, hidden)), whole((1, width)), ANY],
        [
            cols_shape,
            shaped(block_shape, F32),
            mods_out,
            shaped((1, hidden), F32),
            shaped((1, width), F32),
            shaped((shards, chunks, rows, width), BF),
            shaped((2, shards // 2, chunks, rows, width), BF),
        ],
        [
            cols_spec, per_step(block_shape), mods_out_spec, whole((1, hidden)),
            whole((1, width)), ANY, ANY,
        ],
        [
            pltpu.VMEM((width, hidden), BF),
            pltpu.VMEM((hidden, width), BF),
            pltpu.VMEM((tokens, width), BF),
            pltpu.VMEM((tokens, hidden), BF),
            pltpu.VMEM((tokens, hidden), BF),
            pltpu.VMEM((tokens, width), BF),
            pltpu.VMEM((ROWS, width), F32),
            pltpu.VMEM((2 * chunks, shards, rows, width), BF),
            dma(()),
            dma((chunks + shards,)),
        ],
        6 * 2 * tokens * width * hidden, "feed",
    )

    def to_rows(moved):
        moved = jnp.swapaxes(moved.reshape(own_shape), 0, 1)
        return moved.reshape(frame_count, patches, width).astype(F32)

    def shard_total(packed):
        return lax.psum_scatter(packed, "shard", scatter_dimension=0, tiled=True)[0]

    def parts_of(share):
        parts = share.reshape(groups, -1, width)

        def part(at):
            return lax.dynamic_index_in_dim(parts, at, 0, keepdims=False)

        return [part(group_at)] + [
            swap_group(part(group_at ^ distance), distance) for distance in range(1, groups)
        ]

    def spread_parts(parts, share):
        own = parts[0].astype(F32)
        for piece in parts[1:]:
            own = own + piece.astype(F32)
        own = own.astype(BF)
        near = [own] + [swap_group(own, distance) for distance in range(1, groups)]
        step = 1
        while step < groups:
            odd = jnp.bitwise_and(group_at, step) > 0
            near = [jnp.where(odd, near[at ^ step], near[at]) for at in range(groups)]
            step *= 2
        return jnp.concatenate(near).reshape(share.shape).astype(F32)

    def total(share):
        return spread_parts(parts_of(share), share)

    far_bits = list(range(shards.bit_length() - 2))

    def halve(values, left, bit):
        axis = len(left) - 1 - left.index(bit)
        kept, sent = (lax.index_in_dim(values, side, axis, keepdims=False) for side in (0, 1))
        return (kept.astype(F32) + swap(sent, 2 << bit).astype(F32)).astype(BF)

    def near_total(grads):
        return (grads[0].astype(F32) + swap(grads[1], 1).astype(F32)).astype(BF)

    def far_start(kept):
        half = kept.shape[1] // 2
        folded = (2,) * len(far_bits)
        return [
            halve(part.reshape(folded + part.shape[1:]), far_bits, bit)
            for part, bit in ((kept[:, :half], far_bits[0]), (kept[:, half:], far_bits[-1]))
        ]

    def far_finish(parts):
        done = []
        for values, order in zip(parts, (far_bits, far_bits[::-1])):
            left = [bit for bit in far_bits if bit != order[0]]
            for bit in order[1:]:
                values = halve(values, left, bit)
                left = [other for other in left if other != bit]
            done.append(values)
        return jnp.concatenate(done, axis=0)

    up_share = shard_total(up_grads)
    down_far = far_start(near_total(down_grads))

    going, time_mods, time_grads = run(
        partial(time_backward_kernel, frames, shards), steps, inverse,
        [grad_after_time, time_resid, modul] + time_kept + time_w,
        [per_step(block_shape)] * 2 + [mods_spec] + time_keep_specs + [ANY] * shards,
        [cols_shape, mods_out, shaped(grads_shape, BF)],
        [cols_spec, mods_out_spec, whole(grads_shape)],
        weight_scratch + back_scratch(steps) + [dma(())],
        3 * mixer_flops, "time_backward",
    )
    grad_space = exchange(going.reshape(own_shape))
    time_grads, up_share, grad_space, result, *down_far = lax.optimization_barrier(
        (time_grads, up_share, grad_space, result, *down_far)
    )
    time_share = shard_total(time_grads)
    up_parts = parts_of(up_share)
    down_share = far_finish(down_far)
    arrived = exchange(result.reshape(own_shape))
    grad_rows, space_mods, space_grads = run(
        partial(space_backward_kernel, shards), frame_count, where,
        [grad_space, frames_in, modul] + space_kept + space_w,
        [own_spec, per_step(frames_in.shape), mods_spec] + space_keep_specs + [ANY] * shards,
        [shaped(frames_in.shape, F32), mods_out, shaped(grads_shape, BF)],
        [per_step(frames_in.shape), mods_out_spec, whole(grads_shape)],
        weight_scratch + back_scratch(frame_count) + [dma(())],
        3 * mixer_flops, "space_backward",
    )
    space_grads, space_mods, arrived, down_share, time_share, *up_parts = lax.optimization_barrier(
        (space_grads, space_mods, arrived, down_share, time_share, *up_parts)
    )
    space_share = shard_total(space_grads)
    pair = jnp.stack([down_share, time_share], axis=1)
    pair_parts, up_parts, space_mods, arrived = lax.optimization_barrier(
        (parts_of(pair), up_parts, space_mods, arrived)
    )
    pair = spread_parts(pair_parts, pair)
    down_share, time_share = pair[:, 0], pair[:, 1]
    up_share = spread_parts(up_parts, up_share)
    frames_out = to_rows(arrived)

    mod_part = jnp.concatenate([space_mods, time_mods, mlp_mods], axis=1)
    small_grads = jnp.concatenate(
        [mod_part.reshape(-1), grad_up_bias.reshape(-1), grad_down_bias.reshape(-1)]
    )
    small_grads = shard_sum(small_grads.reshape(-1, 128)).reshape(-1)
    up_dev = up_bias.shape[0]
    down_dev = down_bias.shape[0]
    bias_dev = ada_bias.shape[0]
    small_grads = jnp.concatenate(
        [
            small_grads[:mod_size],
            lax.dynamic_slice_in_dim(small_grads, mod_size + shard_at * up_dev, up_dev, 0),
            lax.dynamic_slice_in_dim(
                small_grads, mod_size + shards * up_dev + shard_at * down_dev, down_dev, 0
            ),
        ]
    )
    small_size = small_grads.shape[0]
    small_grads = jnp.pad(small_grads, (0, -small_size % 1024)).reshape(1, -1, 128)
    space_share = total(space_share)
    every_small = every(small_grads).reshape(groups, -1)
    every_modul = every_small[:, :mod_size].reshape(groups * clips, 9 * width).astype(BF)
    bias_sums = jnp.sum(every_small[:, mod_size:small_size], axis=0)
    every_embed = every_ids[:, :-1]
    every_steps = every_ids[:, -1].astype(jnp.int32)
    every_cond = jax.nn.silu(every_embed).astype(BF)
    grad_ada = jnp.einsum("cd,cj->dj", every_cond, every_modul, preferred_element_type=F32)
    grad_ada_bias = lax.dynamic_slice_in_dim(
        jnp.sum(every_modul.astype(F32), axis=0), shard_at * bias_dev, bias_dev, 0
    )
    grad_cond = jnp.einsum("cj,dj->cd", every_modul, ada_weight, preferred_element_type=F32)
    _, silu_back = jax.vjp(jax.nn.silu, every_embed)
    grad_embed = silu_back(grad_cond)[0]
    vocab = time_table.shape[0]
    onehot = (jnp.arange(vocab, dtype=jnp.int32)[:, None] == every_steps[None, :]).astype(F32)
    grad_table = jnp.dot(onehot, grad_embed, precision=HIGH)

    def rows_of(blocks):
        return jnp.swapaxes(blocks, 0, 1).reshape(rows, -1)

    return (
        frames_out,
        grad_rows,
        grad_table,
        grad_ada,
        grad_ada_bias,
        rows_of(space_share[:3]),
        space_share[3],
        rows_of(time_share[:3]),
        time_share[3],
        rows_of(up_share),
        bias_sums[:up_dev],
        down_share.reshape(chunks * rows, width),
        bias_sums[up_dev:],
    )


def solution(mesh):
    placed = (
        P(("grp", "shard"), None, None),
        P(("grp", "shard"), None, None),
        P(None, "shard"),
        P("shard", None),
        P("shard"),
        P("shard", None),
        P("shard", None),
        P("shard", None),
        P("shard", None),
        P("shard", None),
        P("shard"),
        P("shard", None),
        P("shard"),
        P("grp"),
        P("grp", None),
        P("grp"),
        P("grp", None),
    )
    return jax.shard_map(
        body,
        mesh=mesh,
        in_specs=placed,
        out_specs=(
            P(("grp", "shard"), None, None),
            P(("grp", "shard"), None, None),
            P(None, "shard"),
            P("shard", None),
            P("shard"),
            P("shard", None),
            P("shard", None),
            P("shard", None),
            P("shard", None),
            P("shard", None),
            P("shard"),
            P("shard", None),
            P("shard"),
        ),
        check_vma=False,
    )
```
